32 devices in a mesh: row: 2 (over x), col: 16 (over z, y, core).
Axes of the slice: x: 2, y: 2, z: 4, core: 2. Of those that a mesh axis runs over, the one named last changes fastest.
Arguments:
- tokens: bfloat16 [16, 256, 256], P('row', 'col'), may hold values from -6 to 6
- norm_gain: float32 [256], replicated, may hold values from 0.1 to 1.9
- w_inner: bfloat16 [256, 1024], replicated, may hold values from -0.375 to 0.375
- w_select: bfloat16 [256, 512], replicated, may hold values from -0.375 to 0.375
- w_step: bfloat16 [256, 16], replicated, may hold values from -0.375 to 0.375
- step_bias: float32 [16], replicated, may hold values from -1 to 1
- rate_across: float32 [8], replicated, may hold values from 0.5 to 8
- rate_down: float32 [8], replicated, may hold values from 0.5 to 2
- conv_weight: float32 [3, 3, 512], replicated, may hold values from -4 to 4
- conv_bias: float32 [512], replicated, may hold values from -0.5 to 0.5
- skip_gain: float32 [512], replicated, may hold values from 1 to 4
- out_gain: float32 [512], replicated, may hold values from 0.1 to 1.9
- w_out: bfloat16 [512, 256], replicated, may hold values from -0.25 to 0.25
Outputs:
- mixed: bfloat16 [16, 256, 256], P('row', 'col')
The draws below stay inside these ranges and needn't reach their ends.
All inputs are finite; a program needn't handle non-finite values.
Results may differ from the reference program's by a relative error of at most 0.008.
Values may be sent and summed in bfloat16 or wider, within the bound.
A program may use at most 128 MiB of HBM per device.

```python
import math
import jax
import jax.numpy as jnp
from jax import lax

D = 256
INNER = 512
HEADS = 8
HEADP = 64
STATE = 16
ROWS_DEV = 8
COLS_DEV = 16
HEIGHT = 16
WIDTH = 256
N_ROW = 2
N_COL = 16


def shard_levels(own_key, dims, shards, least, top_value):
    def one(dim, blocks):
        heights = jax.random.uniform(jax.random.fold_in(jax.random.fold_in(own_key, 6), dim), (blocks,), jnp.float32, least / len(shards), top_value / len(shards))
        return jnp.repeat(jnp.exp(heights), dims[dim] // blocks).reshape((-1,) + (1,) * (len(dims) - dim - 1))

    level = one(*shards[0])
    for cut in shards[1:]:
        level = level * one(*cut)
    return level


def bell_draw(key, dims, spread, limit, shards=(), held_as=jnp.bfloat16):
    level = shard_levels(key, dims, shards, -0.22, 0.18) if shards else 1.0
    values = jax.random.normal(key, dims, jnp.float32) * spread * level
    return jnp.minimum(jnp.maximum(values, -limit), limit).astype(held_as)


def setup_inputs(seed: int = 0) -> dict:
    seeds = jax.random.split(jax.random.key(seed), 14)
    tokens = bell_draw(seeds[0], (HEIGHT, WIDTH, D), 1.0, 6.0, ((0, 2), (1, 16)))
    norm_gain = jnp.clip(1.0 + 0.18 * jax.random.normal(seeds[1], (D,), jnp.float32), 0.1, 1.9)
    w_inner = bell_draw(seeds[2], (D, 2 * INNER), D ** -0.5, 0.375)
    w_select = bell_draw(seeds[3], (D, 4 * HEADS * STATE), D ** -0.5, 0.375)
    w_step = bell_draw(seeds[4], (D, 2 * HEADS), D ** -0.5, 0.375)
    step_bias = jnp.clip(jax.random.uniform(seeds[5], (2 * HEADS,), jnp.float32, -1.0, 1.0), -1.0, 1.0)
    rate_across = jnp.clip(jnp.exp(jax.random.uniform(seeds[6], (HEADS,), jnp.float32, math.log(0.5), math.log(8.0))), 0.5, 8.0)
    rate_down = jnp.clip(jnp.exp(jax.random.uniform(seeds[7], (HEADS,), jnp.float32, math.log(0.5), math.log(2.0))), 0.5, 2.0)
    conv_weight = bell_draw(seeds[8], (3, 3, INNER), 0.35, 4.0, (), jnp.float32)
    conv_bias = jnp.clip(jax.random.uniform(seeds[9], (INNER,), jnp.float32, -0.5, 0.5), -0.5, 0.5)
    skip_gain = jnp.clip(jnp.exp(jax.random.uniform(seeds[10], (INNER,), jnp.float32, math.log(1.0), math.log(4.0))), 1.0, 4.0)
    out_gain = jnp.clip(1.0 + 0.18 * jax.random.normal(seeds[11], (INNER,), jnp.float32), 0.1, 1.9)
    w_out = bell_draw(seeds[12], (INNER, D), INNER ** -0.5, 0.25)
    return dict(tokens=tokens, norm_gain=norm_gain, w_inner=w_inner, w_select=w_select, w_step=w_step, step_bias=step_bias, rate_across=rate_across, rate_down=rate_down, conv_weight=conv_weight, conv_bias=conv_bias, skip_gain=skip_gain, out_gain=out_gain, w_out=w_out)


precise = lax.Precision.HIGHEST
epsilon = 1e-06

def rms_scale(values, gain_vec):
    values = values.astype(jnp.float32)
    return values * lax.rsqrt(lax.optimization_barrier(jnp.mean(values * values, axis=-1, keepdims=True)) + epsilon) * gain_vec

def project(tokens, norm_gain, w_inner, w_select, w_step):
    lead_shape = tokens.shape[:-1]
    normed = rms_scale(tokens, norm_gain).astype(jnp.bfloat16).reshape(-1, tokens.shape[-1])
    inner_both = jnp.dot(normed, w_inner, preferred_element_type=jnp.float32).astype(jnp.bfloat16)
    selects = jnp.dot(normed, w_select, preferred_element_type=jnp.float32)
    step_raw = jnp.dot(normed, w_step, preferred_element_type=jnp.float32)
    half_width = w_inner.shape[1] // 2
    return (inner_both[:, :half_width].reshape(lead_shape + (half_width,)), inner_both[:, half_width:].reshape(lead_shape + (half_width,)), selects.reshape(lead_shape + (w_select.shape[1],)), step_raw.reshape(lead_shape + (w_step.shape[1],)))

def depthwise(padded, conv_weight, conv_bias, height, full_width):
    summed = jnp.zeros((height, full_width, conv_weight.shape[2]), jnp.float32) + conv_bias
    for offset_row in range(3):
        for offset_col in range(3):
            piece_now = padded[offset_row:offset_row + height, offset_col:offset_col + full_width]
            summed = summed + piece_now.astype(jnp.float32) * conv_weight[offset_row, offset_col]
    return jax.nn.silu(summed)

def decay_logs(step_raw, step_bias, rate_across, rate_down, full_width, height):
    head_count = rate_across.shape[0]
    softened = jax.nn.softplus(step_raw + step_bias)
    return (-softened[..., :head_count] * (rate_across / full_width), -softened[..., head_count:] * (rate_down / height))

def block_terms(values, into_state, from_state, log_decay):
    cumulated = jnp.cumsum(log_decay, axis=1)
    length = log_decay.shape[1]
    lower_mask = (jnp.arange(length)[:, None] >= jnp.arange(length)[None, :])[None, :, :, None]
    log_gaps = cumulated[:, :, None, :] - cumulated[:, None, :, :]
    weights = jnp.where(lower_mask, jnp.exp(jnp.where(lower_mask, log_gaps, 0.0)), 0.0)
    scores = jnp.einsum('ntks,nuks->ntuk', from_state, into_state, precision=precise) * weights
    within = jnp.einsum('ntuk,nukp->ntkp', scores, values, precision=precise)
    total_log = cumulated[:, -1, :]
    tail_decay = jnp.exp(total_log[:, None, :] - cumulated)
    final_state = jnp.einsum('nuks,nukp->nksp', into_state * tail_decay[..., None], values, precision=precise)
    return (within, final_state, total_log, cumulated)

def carried(from_state, cumulated, incoming):
    return jnp.einsum('ntks,nksp->ntkp', from_state, incoming, precision=precise) * jnp.exp(cumulated)[..., None]

def reference(tokens, norm_gain, w_inner, w_select, w_step, step_bias, rate_across, rate_down, conv_weight, conv_bias, skip_gain, out_gain, w_out):
    row_count = ROWS_DEV
    padded_tokens = jnp.pad(tokens, ((1, 1), (0, 0), (0, 0)))

    def spanned(array):
        return array.reshape((row_count * N_COL, COLS_DEV) + array.shape[2:])

    def advance(state_now, entry_pair):
        return (jnp.exp(entry_pair[1])[..., None, None] * state_now + entry_pair[0], state_now)

    def group(state_above, group_index):
        window = lax.dynamic_slice_in_dim(padded_tokens, group_index * row_count, row_count + 2, 0)
        inner_x, gate_z, selects, step_raw = project(window, norm_gain, w_inner, w_select, w_step)
        padded = jnp.pad(inner_x, ((0, 0), (1, 1), (0, 0)))
        conved = depthwise(padded, conv_weight, conv_bias, row_count, WIDTH)
        gate_z = gate_z[1:-1]
        selections = selects[1:-1].reshape(row_count, WIDTH, 4, HEADS, STATE)
        across_log, down_log = decay_logs(step_raw[1:-1], step_bias, rate_across, rate_down, float(WIDTH), float(HEIGHT))
        values = conved.reshape(row_count, WIDTH, HEADS, HEADP)
        within, final_state, total_log, cumulated = block_terms(spanned(values), spanned(selections[:, :, 0]), spanned(selections[:, :, 1]), spanned(across_log))
        final_state = final_state.reshape(row_count, N_COL, HEADS, STATE, HEADP).transpose(1, 0, 2, 3, 4)
        total_log = total_log.reshape(row_count, N_COL, HEADS).transpose(1, 0, 2)
        initial = jnp.zeros((row_count, HEADS, STATE, HEADP), jnp.float32)
        _, incoming = lax.scan(advance, initial, (final_state, total_log))
        incoming = incoming.transpose(1, 0, 2, 3, 4).reshape(row_count * N_COL, HEADS, STATE, HEADP)
        across = (within + carried(spanned(selections[:, :, 1]), cumulated, incoming)).reshape(row_count, WIDTH, HEADS * HEADP)
        columns = values.transpose(1, 0, 2, 3)
        into_down = selections[:, :, 2].transpose(1, 0, 2, 3)
        from_down = selections[:, :, 3].transpose(1, 0, 2, 3)
        within_down, final_down, total_down, cumulated_down = block_terms(columns, into_down, from_down, down_log.transpose(1, 0, 2))
        downward = within_down + carried(from_down, cumulated_down, state_above)
        following = jnp.exp(total_down)[..., None, None] * state_above + final_down
        downward = downward.transpose(1, 0, 2, 3).reshape(row_count, WIDTH, HEADS * HEADP)
        mixed_inner = (across + downward + skip_gain * conved) * jax.nn.silu(gate_z.astype(jnp.float32))
        gated_out = rms_scale(mixed_inner, out_gain).astype(jnp.bfloat16).reshape(-1, HEADS * HEADP)
        output = jnp.dot(gated_out, w_out, preferred_element_type=jnp.float32).reshape(row_count, WIDTH, -1)
        return (following, (output + window[1:-1].astype(jnp.float32)).astype(jnp.bfloat16))
    initial_column = jnp.zeros((WIDTH, HEADS, STATE, HEADP), jnp.float32)
    _, out_blocks = lax.scan(group, initial_column, jnp.arange(N_ROW, dtype=jnp.int32))
    return out_blocks.reshape(HEIGHT, WIDTH, tokens.shape[2])
```

```python
import functools
import jax
import jax.numpy as jnp
from jax import lax
from jax.experimental import pallas as pl
from jax.experimental.pallas import tpu as pltpu
from jax.sharding import PartitionSpec as P

MESH = pl.DeviceIdType.MESH
F32 = jnp.float32
BF16 = jnp.bfloat16
HI = lax.Precision.HIGHEST
epsilon = 1e-06


def iota(shape, dim):
    return lax.broadcasted_iota(jnp.int32, shape, dim)


def exact(a, b):
    return jnp.dot(a, b, precision=HI, preferred_element_type=F32)


def mm(a, b):
    return jnp.dot(a, b, preferred_element_type=F32)


def nt(a, b):
    return lax.dot_general(a, b, (((1,), (1,)), ((), ())), preferred_element_type=F32)


def norm(x, gain):
    return x * lax.rsqrt(jnp.mean(x * x, axis=-1, keepdims=True) + epsilon) * gain


def silu(v):
    return v * (1.0 / (1.0 + jnp.exp(-v)))


def softplus(x):
    return jnp.maximum(x, 0.0) + jnp.log1p(jnp.exp(-jnp.abs(x)))


def copy_to(src, dst, send, recv, row, col):
    return pltpu.make_async_remote_copy(
        src_ref=src, dst_ref=dst, send_sem=send, recv_sem=recv,
        device_id=(row, col), device_id_type=MESH,
    )


def kernel(
    dims,
    tok_ref, ng_ref, wi_ref, wsel_ref, wst_ref, sb_ref, ra_ref, rd_ref, cw_ref, cb_ref,
    sk_ref, og_ref, wo_ref,
    out_ref,
    tok_v, ng_v, wi_v, wsel_v, wst_v, sb_v, ra_v, rd_v, cw_v, cb_v, sk_v, og_v, wo_v, w_sem,
    hb, eb, xp, vals, vbf, bd_s, logs_s, dj, fbuf, drecv, frecv, tbuf, tdec, trecv, tdrecv, ibuf, pbuf, precv,
    vrecv, brecv, lrecv, sc, gate, acc, cexp, cds, cum_s, cum_ts, btail, sel_s,
    h_send, h_recv, d_send, d_recv, f_send, f_recv, t_send, t_recv, p_send, p_recv, v_send, v_recv, know,
):
    n_row, n_col, rows, cols, heads, state, full_w, height = dims
    T = rows * cols
    loads = [
        pltpu.make_async_copy(src, dst, w_sem.at[k])
        for k, (src, dst) in enumerate((
            (tok_ref, tok_v), (ng_ref, ng_v), (wi_ref, wi_v), (wsel_ref, wsel_v), (wst_ref, wst_v),
            (sb_ref, sb_v), (ra_ref, ra_v), (rd_ref, rd_v), (cw_ref, cw_v), (cb_ref, cb_v),
            (sk_ref, sk_v), (og_ref, og_v), (wo_ref, wo_v),
        ))
    ]
    tok_ref, ng_ref, wi_ref, wsel_ref, wst_ref = tok_v, ng_v, wi_v, wsel_v, wst_v
    sb_ref, ra_ref, rd_ref, cw_ref, cb_ref = sb_v, ra_v, rd_v, cw_v, cb_v
    sk_ref, og_ref, wo_ref = sk_v, og_v, wo_v
    inner = wo_ref.shape[0]
    D = tok_ref.shape[2]
    nj = inner // 128
    G = nj
    n_grp = n_col // G
    hs = heads * state
    nh = 2 * heads
    r = lax.axis_index("row")
    c = lax.axis_index("col")
    g, q = c // G, c % G
    side = 1 - 2 * (q % 2)
    far = [(q + G // 2) % G, (q + G // 2 + side) % G, q + side, q]
    base = g * G

    barrier = pltpu.get_barrier_semaphore()

    plan = (
        (4, 1, 1, eb.at[1]),
        (5, 1, -1, eb.at[0]),
        (6, -1, 1, eb.at[1]),
        (7, -1, -1, eb.at[0]),
        (0, 1, 0, tok_ref.at[rows - 1]),
        (1, -1, 0, tok_ref.at[0]),
        (2, 0, 1, eb.at[1]),
        (3, 0, -1, eb.at[0]),
    )

    def there(dr, dc):
        return (r + dr >= 0) & (r + dr < n_row) & (c + dc >= 0) & (c + dc < n_col)

    loads[0].start()
    hb[...] = jnp.zeros_like(hb)
    eb[...] = jnp.zeros_like(eb)
    friends = [(dr, dc, there(dr, dc)) for _, dr, dc, _ in plan]
    friends += [(0, dc, (q + dc >= 0) & (q + dc < G)) for k in range(2, G) for dc in (k, -k)]
    friends += [(0, dc, there(0, dc)) for dc in (G, -G)]
    friends += [(dr, 0, there(dr, 0)) for k in range(2, n_row) for dr in (k, -k)]
    for dr, dc, ok in friends:
        @pl.when(ok)
        def _():
            pl.semaphore_signal(barrier, inc=1, device_id=(r + dr, c + dc), device_id_type=MESH)
    for load in loads[1:]:
        load.start()

    loads[0].wait()
    eb[0, 0:rows, :] = tok_ref[:, 0, :]
    eb[1, 0:rows, :] = tok_ref[:, cols - 1, :]
    pl.semaphore_wait(barrier, sum(jnp.where(ok, 1, 0) for _, _, ok in friends))

    for slot, dr, dc, src in plan:
        @pl.when(there(dr, dc))
        def _():
            copy_to(src, hb.at[slot], h_send.at[slot], h_recv.at[slot], r + dr, c + dc).start()

    def tell(level):
        if 2 < level <= n_grp:
            @pl.when(g + level - 1 < n_grp)
            def _():
                pl.semaphore_wait(know.at[level - 1], 1)
        if 2 <= level < n_grp:
            @pl.when((g >= 1) & (g + level - 1 < n_grp))
            def _():
                pl.semaphore_signal(know.at[level], inc=1, device_id=(r, c - G), device_id_type=MESH)

    tell(2)

    loads[1].wait()
    x = tok_ref[...].astype(F32).reshape(T, D)
    normed = norm(x, ng_ref[...]).astype(BF16)
    for k in (4, 5, 6, 7):
        loads[k].wait()

    def column(row):
        width = row.shape[1]
        square = jnp.broadcast_to(row, (width, width))
        return jnp.sum(
            jnp.where(iota((width, width), 0) == iota((width, width), 1), square, 0.0), axis=1, keepdims=True
        )

    t_i, u_i = iota((T, T), 0), iota((T, T), 1)
    row_same = (t_i // cols) == (u_i // cols)
    col_same = (t_i % cols) == (u_i % cols)
    step_t = nt(wst_ref[...], normed)
    rate = jnp.concatenate([column(ra_ref[...]) / full_w, column(rd_ref[...]) / height], axis=0)
    logs_t = -softplus(step_t + column(sb_ref[...])) * rate

    def thirds(v):
        hi = v.astype(BF16)
        rest = v - hi.astype(F32)
        mid = rest.astype(BF16)
        return hi, mid, (rest - mid.astype(F32)).astype(BF16)

    up = t_i <= u_i
    sums = jnp.concatenate(
        [jnp.where(m, 1.0, 0.0).astype(BF16) for m in (row_same & up, row_same, col_same & up, col_same)], axis=1
    )
    parts = mm(jnp.concatenate(thirds(logs_t), axis=0), sums)
    summed = parts[:nh] + parts[nh:2 * nh] + parts[2 * nh:]
    cum_t = jnp.concatenate([summed[:heads, 0:T], summed[heads:, 2 * T:3 * T]], axis=0)
    tot_t = jnp.concatenate([summed[:heads, T:2 * T], summed[heads:, 3 * T:]], axis=0)
    logs_s[0:heads] = tot_t[heads:] - cum_t[heads:]
    logs_s[heads:] = tot_t[heads:]
    cum_ts[...] = cum_t
    cum = jnp.concatenate([cum_t, jnp.zeros((T - nh, T), F32)], axis=0).T[:, :nh]
    cum_s[...] = cum

    row_tot = jnp.concatenate([cum[(i + 1) * cols - 1:(i + 1) * cols] for i in range(rows)], axis=0)
    spread = jnp.where(iota((nh, inner), 0) == iota((nh, inner), 1) // (inner // heads), 1.0, 0.0).astype(BF16)
    wide = sum(mm(part, spread) for part in thirds(row_tot))
    for j in range(nj):
        dj[j] = wide[:, j * 128:(j + 1) * 128]
    for p in far[:3]:
        copy_to(dj.at[p], drecv.at[q], d_send.at[p], d_recv.at[q], r, base + p).start()

    def per_state(v):
        return jnp.concatenate([jnp.broadcast_to(v[k:k + 1], (state, T)) for k in range(heads)], axis=0)

    loads[3].wait()
    sel = mm(normed, wsel_ref[...])
    sel_s[...] = sel[:, :2 * hs]
    btail[...] = sel[:, :hs].T * per_state(jnp.exp(tot_t - cum_t))
    bd_s[...] = sel[:, 2 * hs:3 * hs].astype(BF16)
    cds[...] = sel[:, 3 * hs:].astype(BF16)

    def down_early(to_row, slot, dest):
        return (
            copy_to(bd_s, brecv.at[slot], v_send.at[nj, dest], v_recv.at[nj, slot], to_row, c),
            copy_to(logs_s, lrecv.at[slot], v_send.at[nj + 1, dest], v_recv.at[nj + 1, slot], to_row, c),
        )

    def down_value(j, to_row, slot, dest):
        return copy_to(vbf.at[j], vrecv.at[slot, j], v_send.at[j, dest], v_recv.at[j, slot], to_row, c)

    for k in range(1, n_row):
        @pl.when(r < k)
        def _():
            for cp in down_early(k, r, k):
                cp.start()

    loads[2].wait()
    both = mm(normed, wi_ref[...])
    main_x = both[:, :inner].astype(BF16).astype(F32)
    gate[...] = both[:, inner:].astype(BF16).astype(F32)
    for i in range(rows):
        xp[i + 1, 8:8 + cols, :] = main_x[i * cols:(i + 1) * cols]

    for slot, dr, dc, src in plan:
        @pl.when(there(-dr, -dc))
        def _():
            copy_to(src, hb.at[slot], h_send.at[slot], h_recv.at[slot], r, c).wait_recv()
    tell(3)
    edge = norm(hb[...].astype(F32).reshape(8 * cols, D), ng_ref[...]).astype(BF16)
    edge_x = mm(edge, wi_ref[:, :inner]).astype(BF16).astype(F32)
    xp[0, 8:8 + cols, :] = edge_x[0:cols]
    xp[rows + 1, 8:8 + cols, :] = edge_x[cols:2 * cols]
    for i in range(rows):
        xp[i + 1, 7:8, :] = edge_x[2 * cols + i:2 * cols + i + 1]
        xp[i + 1, 8 + cols:9 + cols, :] = edge_x[3 * cols + i:3 * cols + i + 1]
    xp[0, 7:8, :] = edge_x[4 * cols + rows - 1:4 * cols + rows]
    xp[0, 8 + cols:9 + cols, :] = edge_x[5 * cols + rows - 1:5 * cols + rows]
    xp[rows + 1, 7:8, :] = edge_x[6 * cols:6 * cols + 1]
    xp[rows + 1, 8 + cols:9 + cols, :] = edge_x[7 * cols:7 * cols + 1]

    first = iota((1, 128), 1) < 64
    pair = 2 * state
    own = (iota((rows * pair, T), 0) // pair) == (iota((rows * pair, T), 1) // cols)
    loads[8].wait()
    loads[9].wait()
    for step, j in enumerate(far):
        ln = pl.ds(pl.multiple_of(j * 128, 128), 128)
        w9 = [cw_ref[a, b:b + 1, ln] for a in range(3) for b in range(3)]
        bias = cb_ref[:, ln]
        for i in range(rows):
            total = jnp.zeros((cols, 128), F32) + bias
            for a in range(3):
                for b in range(3):
                    total = total + xp[i + a, 7 + b:7 + b + cols, ln] * w9[a * 3 + b]
            total = silu(total)
            vals[j, i * cols:(i + 1) * cols] = total
            vbf[j, i * cols:(i + 1) * cols] = total.astype(BF16)

        rowed = pl.ds(pl.multiple_of(j * pair, pair), pair)
        piece = jnp.concatenate([btail[rowed, :]] * rows, axis=0)
        piece = jnp.where(own, piece, 0.0).astype(BF16)
        res = mm(piece, vbf[j])
        for i in range(rows):
            top = res[i * pair:i * pair + state]
            bottom = res[i * pair + state:(i + 1) * pair]
            fbuf[j, i] = jnp.where(first, top, bottom).astype(BF16)
        if step < 3:
            copy_to(fbuf.at[j], frecv.at[q], f_send.at[j], f_recv.at[q], r, base + j).start()
        for k in range(1, n_row):
            @pl.when(r < k)
            def _():
                down_value(j, k, r, k).start()

    frecv[q] = fbuf[q]
    drecv[q] = dj[q]

    low = u_i <= t_i
    mask_a, mask_d = row_same & low, col_same & low
    lane_head = iota((T, hs), 1) // state
    zero_b = jnp.zeros((T, hs), BF16)
    b_a, c_a = sel_s[:, 0:hs], sel_s[:, hs:]
    cexp[...] = (c_a * per_state(jnp.exp(cum_ts[...])).T).astype(BF16)
    b_ab, c_ab, b_db, c_db = b_a.astype(BF16), c_a.astype(BF16), bd_s[...], cds[...]
    for k in range(heads):
        only = lane_head == k
        s_a = nt(c_ab, jnp.where(only, b_ab, zero_b))
        s_d = nt(c_db, jnp.where(only, b_db, zero_b))
        g_a = jnp.where(mask_a, cum_s[:, k:k + 1] - cum_ts[k:k + 1, :], -1e30)
        g_d = jnp.where(mask_d, cum_s[:, heads + k:heads + k + 1] - cum_ts[heads + k:heads + k + 1, :], -1e30)
        sc[k // 2, :, (k % 2) * T:(k % 2 + 1) * T] = (s_a * jnp.exp(g_a) + s_d * jnp.exp(g_d)).astype(BF16)

    def times_values(scores, v_tile):
        zero = jnp.zeros((T, 128), BF16)
        stacked = jnp.concatenate(
            [jnp.where(first, v_tile, zero), jnp.where(first, zero, v_tile)], axis=0
        )
        return mm(scores, stacked)

    for level in range(4, n_grp + 1):
        tell(level)

    for e in range(G):
        @pl.when(e != q)
        def _():
            copy_to(dj.at[0], drecv.at[e], d_send.at[0], d_recv.at[e], r, c).wait_recv()
    logs = [drecv[e] for e in range(G)]
    tdec[...] = sum(logs)
    decays = [jnp.exp(v)[:, None, :] for v in logs]

    def total_decay(k):
        return copy_to(tdec, tdrecv.at[g], t_send.at[0, k], t_recv.at[0, g], r, c + G * k)

    def total_state(k):
        return copy_to(tbuf, trecv.at[g], t_send.at[1, k], t_recv.at[1, g], r, c + G * k)

    def later(k):
        return g + k < n_grp

    for k in range(1, n_grp):
        @pl.when(later(k))
        def _():
            total_decay(k).start()
    for e in range(G):
        @pl.when(e != q)
        def _():
            copy_to(fbuf.at[0], frecv.at[e], f_send.at[0], f_recv.at[e], r, c).wait_recv()
    carry = frecv[0].astype(F32)
    for e in range(1, G):
        carry = decays[e] * carry + frecv[e].astype(F32)
    tbuf[...] = carry.astype(BF16)
    for k in range(1, n_grp):
        @pl.when(later(k))
        def _():
            total_state(k).start()

    gate[...] = silu(gate[...])
    loads[10].wait()
    for j in range(nj):
        ln = slice(j * 128, (j + 1) * 128)
        acc[:, ln] = times_values(sc[j], vbf[j]) + sk_ref[:, ln] * vals[j]

    ibuf[...] = jnp.zeros_like(ibuf)
    for m in range(n_grp - 1):
        @pl.when(m < g)
        def _():
            copy_to(tdec, tdrecv.at[m], t_send.at[0, 0], t_recv.at[0, m], r, c).wait_recv()
            copy_to(tbuf, trecv.at[m], t_send.at[1, 0], t_recv.at[1, m], r, c).wait_recv()
            ibuf[...] = jnp.exp(tdrecv[m])[:, None, :] * ibuf[...] + trecv[m].astype(F32)
    carry = ibuf[...]
    for e in range(G):
        pbuf[e] = carry.astype(BF16)
        if e < G - 1:
            carry = decays[e] * carry + frecv[e].astype(F32)
    for p in far[:3]:
        copy_to(pbuf.at[p], precv.at[q], p_send.at[p], p_recv.at[q], r, base + p).start()
    precv[q] = pbuf[q]

    for back in range(1, n_row):
        @pl.when(r >= back)
        def _():
            slot = r - back
            for cp in down_early(r, slot, 0):
                cp.wait_recv()
            gap = lrecv[slot, 0:heads]
            for nearer in range(1, back):
                gap = gap + lrecv[r - nearer, heads:]
            same = (iota((T, T), 0) % cols) == (iota((T, T), 1) % cols)
            for j in range(nj):
                parts = []
                for k in (2 * j, 2 * j + 1):
                    only = (iota((T, hs), 1) // state) == k
                    s_d = nt(cds[...], jnp.where(only, brecv[slot], jnp.zeros((T, hs), BF16)))
                    g_d = jnp.where(same, cum_s[:, heads + k:heads + k + 1] + gap[k:k + 1, :], -1e30)
                    parts.append((s_d * jnp.exp(g_d)).astype(BF16))
                ln = slice(j * 128, (j + 1) * 128)
                down_value(j, r, slot, 0).wait_recv()
                acc[:, ln] += times_values(jnp.concatenate(parts, axis=1), vrecv[slot, j])

    mine = (iota((T, rows * pair), 0) // cols) == (iota((T, rows * pair), 1) // pair)
    zero_s = jnp.zeros((state, 128), BF16)
    for e in range(G):
        @pl.when(e != q)
        def _():
            copy_to(pbuf.at[0], precv.at[e], p_send.at[0], p_recv.at[e], r, c).wait_recv()
    for j in range(nj):
        ln = slice(j * 128, (j + 1) * 128)
        src = iota((hs, rows * pair), 0)
        dst = iota((hs, rows * pair), 1) % pair
        rep = (src == dst + j * pair).astype(BF16)
        maps = jnp.where(mine, mm(cexp[...], rep), 0.0).astype(BF16)
        blocks = []
        for i in range(rows):
            s = precv[j, i]
            blocks += [jnp.where(first, s, zero_s), jnp.where(first, zero_s, s)]
        acc[:, ln] += mm(maps, jnp.concatenate(blocks, axis=0))

    loads[11].wait()
    loads[12].wait()
    mixed = acc[...] * gate[...]
    gated = norm(mixed, og_ref[...]).astype(BF16)
    result = mm(gated, wo_ref[...]) + tok_ref[...].astype(F32).reshape(T, D)
    out_ref[...] = result.astype(BF16).reshape(rows, cols, D)

    for slot, dr, dc, src in plan:
        @pl.when(there(dr, dc))
        def _():
            copy_to(src, hb.at[slot], h_send.at[slot], h_recv.at[slot], r, c).wait_send()
    for p in far[:3]:
        copy_to(dj.at[p], drecv.at[q], d_send.at[p], d_recv.at[q], r, c).wait_send()
        copy_to(fbuf.at[p], frecv.at[q], f_send.at[p], f_recv.at[q], r, c).wait_send()
        copy_to(pbuf.at[p], precv.at[q], p_send.at[p], p_recv.at[q], r, c).wait_send()
    for k in range(1, n_grp):
        @pl.when(later(k))
        def _():
            total_decay(k).wait_send()
            total_state(k).wait_send()
    for k in range(1, n_row):
        @pl.when(r < k)
        def _():
            for cp in down_early(r, 0, k):
                cp.wait_send()
            for j in range(nj):
                down_value(j, r, 0, k).wait_send()


def solution(mesh):
    n_row, n_col = mesh.shape["row"], mesh.shape["col"]

    def on_device(
        tokens, norm_gain, w_inner, w_select, w_step, step_bias, rate_across, rate_down,
        conv_weight, conv_bias, skip_gain, out_gain, w_out,
    ):
        rows, cols, D = tokens.shape
        heads = rate_across.shape[0]
        inner = w_out.shape[0]
        hs = w_select.shape[1] // 4
        state = hs // heads
        T = rows * cols
        nj = inner // 128
        n_grp = n_col // nj
        dims = (n_row, n_col, rows, cols, heads, state, float(cols * n_col), float(rows * n_row))
        vm = pltpu.VMEM
        dma = pltpu.SemaphoreType.DMA
        operands = (
            tokens, norm_gain[None], w_inner, w_select, w_step.T, step_bias[None], rate_across[None],
            rate_down[None], conv_weight, conv_bias[None], skip_gain[None], out_gain[None], w_out,
        )
        operands = tuple(pltpu.with_memory_space_constraint(o, pltpu.HBM) for o in operands)
        return pl.pallas_call(
            functools.partial(kernel, dims),
            out_shape=jax.ShapeDtypeStruct(tokens.shape, tokens.dtype),
            in_specs=[pl.BlockSpec(memory_space=pltpu.HBM)] * 13,
            out_specs=pl.BlockSpec(memory_space=pltpu.VMEM),
            scratch_shapes=[vm(o.shape, o.dtype) for o in operands] + [dma((13,))] + [
                vm((8, cols, D), BF16), vm((2, cols, D), BF16),
                vm((rows + 2, cols + 16, inner), F32),
                vm((nj, T, 128), F32), vm((nj, T, 128), BF16), vm((T, hs), BF16),
                vm((2 * heads, T), F32), vm((nj, rows, 128), F32),
                vm((nj, rows, state, 128), BF16), vm((nj, rows, 128), F32), vm((nj, rows, state, 128), BF16),
                vm((rows, state, 128), BF16), vm((rows, 128), F32),
                vm((n_grp, rows, state, 128), BF16), vm((n_grp, rows, 128), F32), vm((rows, state, 128), F32),
                vm((nj, rows, state, 128), BF16), vm((nj, rows, state, 128), BF16),
                vm((n_row, nj, T, 128), BF16), vm((n_row, T, hs), BF16), vm((n_row, 2 * heads, T), F32),
                vm((heads // 2, T, 2 * T), BF16), vm((T, inner), F32), vm((T, inner), F32),
                vm((T, hs), BF16), vm((T, hs), BF16), vm((T, 2 * heads), F32), vm((2 * heads, T), F32),
                vm((hs, T), F32), vm((T, 2 * hs), F32),
                dma((8,)), dma((8,)), dma((nj,)), dma((nj,)), dma((nj,)), dma((nj,)),
                dma((2, n_grp)), dma((2, n_grp)), dma((nj,)), dma((nj,)),
                dma((nj + 2, n_row)), dma((nj + 2, n_row)), pltpu.SemaphoreType.REGULAR((n_grp,)),
            ],
            compiler_params=pltpu.CompilerParams(
                collective_id=0, has_side_effects=True, vmem_limit_bytes=48 << 20
            ),
            name="block",
        )(*operands)

    placed = (P("row", "col", None),) + (P(),) * 12
    return jax.shard_map(
        on_device, mesh=mesh, in_specs=placed, out_specs=P("row", "col", None), check_vma=False
    )
```

```python
import functools
import jax
import jax.numpy as jnp
from jax import lax
from jax.experimental import pallas as pl
from jax.experimental.pallas import tpu as pltpu
from jax.sharding import PartitionSpec as P

MESH = pl.DeviceIdType.MESH
F32 = jnp.float32
BF16 = jnp.bfloat16
HI = lax.Precision.HIGHEST
epsilon = 1e-06


def iota(shape, dim):
    return lax.broadcasted_iota(jnp.int32, shape, dim)


def exact(a, b):
    return jnp.dot(a, b, precision=HI, preferred_element_type=F32)


def mm(a, b):
    return jnp.dot(a, b, preferred_element_type=F32)


def nt(a, b):
    return lax.dot_general(a, b, (((1,), (1,)), ((), ())), preferred_element_type=F32)


def norm(x, gain):
    return x * lax.rsqrt(jnp.mean(x * x, axis=-1, keepdims=True) + epsilon) * gain


def silu(v):
    return v * (1.0 / (1.0 + jnp.exp(-v)))


def softplus(x):
    return jnp.maximum(x, 0.0) + jnp.log1p(jnp.exp(-jnp.abs(x)))


def copy_to(src, dst, send, recv, row, col):
    return pltpu.make_async_remote_copy(
        src_ref=src, dst_ref=dst, send_sem=send, recv_sem=recv,
        device_id=(row, col), device_id_type=MESH,
    )


def split(nj, rows, n_col):
    share = 2 if n_col % (2 * nj) == 0 else 1
    return share, rows // share, nj * share


def kernel(
    dims,
    tok_ref, ng_ref, wi_ref, wsel_ref, wst_ref, sb_ref, ra_ref, rd_ref, cw_ref, cb_ref,
    sk_ref, og_ref, wo_ref,
    out_ref,
    tok_v, ng_v, wi_v, wsel_v, wst_v, sb_v, ra_v, rd_v, cw_v, cb_v, sk_v, og_v, wo_v, w_sem,
    hb, eb, xp, vals, vbf, bd_s, logs_s, dj, fbuf, drecv, frecv, tbuf, tdec, trecv, tdrecv, ibuf, pbuf, precv,
    vrecv, brecv, lrecv, sc, gate, acc, cexp, cds, cum_s, cum_ts, btail, sel_s, maps,
    h_send, h_recv, d_send, d_recv, f_send, f_recv, t_send, t_recv, p_send, p_recv, v_send, v_recv, know,
):
    n_row, n_col, rows, cols, heads, state, full_w, height = dims
    T = rows * cols
    loads = [
        pltpu.make_async_copy(src, dst, w_sem.at[k])
        for k, (src, dst) in enumerate((
            (tok_ref, tok_v), (ng_ref, ng_v), (wi_ref, wi_v), (wsel_ref, wsel_v), (wst_ref, wst_v),
            (sb_ref, sb_v), (ra_ref, ra_v), (rd_ref, rd_v), (cw_ref, cw_v), (cb_ref, cb_v),
            (sk_ref, sk_v), (og_ref, og_v), (wo_ref, wo_v),
        ))
    ]
    tok_ref, ng_ref, wi_ref, wsel_ref, wst_ref = tok_v, ng_v, wi_v, wsel_v, wst_v
    sb_ref, ra_ref, rd_ref, cw_ref, cb_ref = sb_v, ra_v, rd_v, cw_v, cb_v
    sk_ref, og_ref, wo_ref = sk_v, og_v, wo_v
    inner = wo_ref.shape[0]
    D = tok_ref.shape[2]
    nj = inner // 128
    share, keep, G = split(nj, rows, n_col)
    n_grp = n_col // G
    hs = heads * state
    nh = 2 * heads
    r = lax.axis_index("row")
    c = lax.axis_index("col")
    g, q = c // G, c % G
    mine_j, mine_h = q // share, q % share
    i0 = mine_h * keep
    if nj == 4:
        far = [3 - mine_j, (mine_j + 2) % 4, mine_j + 1 - 2 * (mine_j % 2), mine_j]
    else:
        far = [(mine_j + k) % nj for k in range(1, nj)] + [mine_j]
    peers = [(j, h, j * share + h) for j in far[:-1] for h in range(share)]
    peers += [(mine_j, h, mine_j * share + h) for h in [(mine_h + k) % share for k in range(1, share)]]
    base = g * G

    barrier = pltpu.get_barrier_semaphore()

    plan = (
        (4, 1, 1, eb.at[1]),
        (5, 1, -1, eb.at[0]),
        (6, -1, 1, eb.at[1]),
        (7, -1, -1, eb.at[0]),
        (0, 1, 0, tok_ref.at[rows - 1]),
        (1, -1, 0, tok_ref.at[0]),
        (2, 0, 1, eb.at[1]),
        (3, 0, -1, eb.at[0]),
    )

    def there(dr, dc):
        return (r + dr >= 0) & (r + dr < n_row) & (c + dc >= 0) & (c + dc < n_col)

    loads[0].start()
    hb[...] = jnp.zeros_like(hb)
    eb[...] = jnp.zeros_like(eb)
    friends = [(dr, dc, there(dr, dc)) for _, dr, dc, _ in plan]
    friends += [(0, dc, (q + dc >= 0) & (q + dc < G)) for k in range(2, G) for dc in (k, -k)]
    friends += [(dr, 0, there(dr, 0)) for k in range(2, n_row) for dr in (k, -k)]
    for dr, dc, ok in friends:
        @pl.when(ok)
        def _():
            pl.semaphore_signal(barrier, inc=1, device_id=(r + dr, c + dc), device_id_type=MESH)
    for load in loads[1:]:
        load.start()

    loads[0].wait()
    eb[0, 0:rows, :] = tok_ref[:, 0, :]
    eb[1, 0:rows, :] = tok_ref[:, cols - 1, :]
    pl.semaphore_wait(barrier, sum(jnp.where(ok, 1, 0) for _, _, ok in friends))

    for slot, dr, dc, src in plan:
        @pl.when(there(dr, dc))
        def _():
            copy_to(src, hb.at[slot], h_send.at[slot], h_recv.at[slot], r + dr, c + dc).start()

    def tell(level):
        if 2 < level <= n_grp:
            @pl.when(g + level - 1 < n_grp)
            def _():
                pl.semaphore_wait(know.at[level - 1], 1)
        if 2 <= level < n_grp:
            @pl.when((g >= 1) & (g + level - 1 < n_grp))
            def _():
                pl.semaphore_signal(know.at[level], inc=1, device_id=(r, c - G), device_id_type=MESH)

    loads[1].wait()
    x = tok_ref[...].astype(F32).reshape(T, D)
    normed = norm(x, ng_ref[...]).astype(BF16)
    for k in (4, 5, 6, 7):
        loads[k].wait()

    def column(row):
        width = row.shape[1]
        square = jnp.broadcast_to(row, (width, width))
        return jnp.sum(
            jnp.where(iota((width, width), 0) == iota((width, width), 1), square, 0.0), axis=1, keepdims=True
        )

    t_i, u_i = iota((T, T), 0), iota((T, T), 1)
    row_same = (t_i // cols) == (u_i // cols)
    col_same = (t_i % cols) == (u_i % cols)
    step_t = nt(wst_ref[...], normed)
    rate = jnp.concatenate([column(ra_ref[...]) / full_w, column(rd_ref[...]) / height], axis=0)
    logs_t = -softplus(step_t + column(sb_ref[...])) * rate

    def thirds(v):
        hi = v.astype(BF16)
        rest = v - hi.astype(F32)
        mid = rest.astype(BF16)
        return hi, mid, (rest - mid.astype(F32)).astype(BF16)

    up = t_i <= u_i
    sums = jnp.concatenate(
        [jnp.where(m, 1.0, 0.0).astype(BF16) for m in (row_same & up, row_same, col_same & up, col_same)], axis=1
    )
    parts = mm(jnp.concatenate(thirds(logs_t), axis=0), sums)
    summed = parts[:nh] + parts[nh:2 * nh] + parts[2 * nh:]
    cum_t = jnp.concatenate([summed[:heads, 0:T], summed[heads:, 2 * T:3 * T]], axis=0)
    tot_t = jnp.concatenate([summed[:heads, T:2 * T], summed[heads:, 3 * T:]], axis=0)
    logs_s[0:heads] = tot_t[heads:] - cum_t[heads:]
    logs_s[heads:] = tot_t[heads:]
    cum_ts[...] = cum_t
    cum = jnp.concatenate([cum_t, jnp.zeros((T - nh, T), F32)], axis=0).T[:, :nh]
    cum_s[...] = cum

    row_tot = jnp.concatenate([cum[(i + 1) * cols - 1:(i + 1) * cols] for i in range(rows)], axis=0)
    spread = jnp.where(iota((nh, inner), 0) == iota((nh, inner), 1) // (inner // heads), 1.0, 0.0).astype(BF16)
    wide = sum(mm(part, spread) for part in thirds(row_tot))
    for j in range(nj):
        dj[j] = wide[:, j * 128:(j + 1) * 128]
    for j, h, p in peers:
        copy_to(dj.at[j], drecv.at[q], d_send.at[p], d_recv.at[q], r, base + p).start()

    def per_state(v):
        return jnp.concatenate([jnp.broadcast_to(v[k:k + 1], (state, T)) for k in range(heads)], axis=0)

    loads[3].wait()
    sel = mm(normed, wsel_ref[...])
    sel_s[...] = sel[:, :2 * hs]
    btail[...] = sel[:, :hs].T * per_state(jnp.exp(tot_t - cum_t))
    bd_s[...] = sel[:, 2 * hs:3 * hs].astype(BF16)
    cds[...] = sel[:, 3 * hs:].astype(BF16)

    def down_early(to_row, slot, dest):
        return (
            copy_to(bd_s, brecv.at[slot], v_send.at[nj, dest], v_recv.at[nj, slot], to_row, c),
            copy_to(logs_s, lrecv.at[slot], v_send.at[nj + 1, dest], v_recv.at[nj + 1, slot], to_row, c),
        )

    def down_value(j, to_row, slot, dest):
        return copy_to(vbf.at[j], vrecv.at[slot, j], v_send.at[j, dest], v_recv.at[j, slot], to_row, c)

    for k in range(1, n_row):
        @pl.when(r < k)
        def _():
            for cp in down_early(k, r, k):
                cp.start()

    loads[2].wait()
    both = mm(normed, wi_ref[...])
    main_x = both[:, :inner].astype(BF16).astype(F32)
    gate[...] = both[:, inner:].astype(BF16).astype(F32)
    for i in range(rows):
        xp[i + 1, 8:8 + cols, :] = main_x[i * cols:(i + 1) * cols]

    for slot, dr, dc, src in plan:
        @pl.when(there(-dr, -dc))
        def _():
            copy_to(src, hb.at[slot], h_send.at[slot], h_recv.at[slot], r, c).wait_recv()
    edge = norm(hb[...].astype(F32).reshape(8 * cols, D), ng_ref[...]).astype(BF16)
    edge_x = mm(edge, wi_ref[:, :inner]).astype(BF16).astype(F32)
    xp[0, 8:8 + cols, :] = edge_x[0:cols]
    xp[rows + 1, 8:8 + cols, :] = edge_x[cols:2 * cols]
    for i in range(rows):
        xp[i + 1, 7:8, :] = edge_x[2 * cols + i:2 * cols + i + 1]
        xp[i + 1, 8 + cols:9 + cols, :] = edge_x[3 * cols + i:3 * cols + i + 1]
    xp[0, 7:8, :] = edge_x[4 * cols + rows - 1:4 * cols + rows]
    xp[0, 8 + cols:9 + cols, :] = edge_x[5 * cols + rows - 1:5 * cols + rows]
    xp[rows + 1, 7:8, :] = edge_x[6 * cols:6 * cols + 1]
    xp[rows + 1, 8 + cols:9 + cols, :] = edge_x[7 * cols:7 * cols + 1]

    first = iota((1, 128), 1) < 64
    pair = 2 * state
    own = (iota((rows * pair, T), 0) // pair) == (iota((rows * pair, T), 1) // cols)
    loads[8].wait()
    loads[9].wait()
    for j in far:
        ln = pl.ds(pl.multiple_of(j * 128, 128), 128)
        w9 = [cw_ref[a, b:b + 1, ln] for a in range(3) for b in range(3)]
        bias = cb_ref[:, ln]
        for i in range(rows):
            total = jnp.zeros((cols, 128), F32) + bias
            for a in range(3):
                for b in range(3):
                    total = total + xp[i + a, 7 + b:7 + b + cols, ln] * w9[a * 3 + b]
            total = silu(total)
            vals[j, i * cols:(i + 1) * cols] = total
            vbf[j, i * cols:(i + 1) * cols] = total.astype(BF16)

        rowed = pl.ds(pl.multiple_of(j * pair, pair), pair)
        piece = jnp.concatenate([btail[rowed, :]] * rows, axis=0)
        piece = jnp.where(own, piece, 0.0).astype(BF16)
        res = mm(piece, vbf[j])
        for i in range(rows):
            top = res[i * pair:i * pair + state]
            bottom = res[i * pair + state:(i + 1) * pair]
            fbuf[j * share + i // keep, i % keep] = jnp.where(first, top, bottom).astype(BF16)
        for j2, h, p in peers:
            if j2 is j:
                copy_to(fbuf.at[p], frecv.at[q], f_send.at[p], f_recv.at[q], r, base + p).start()
        for k in range(1, n_row):
            @pl.when(r < k)
            def _():
                down_value(j, k, r, k).start()

    frecv[q] = fbuf[q]
    drecv[q] = dj[mine_j]

    low = u_i <= t_i
    mask_a, mask_d = row_same & low, col_same & low
    lane_head = iota((T, hs), 1) // state
    zero_b = jnp.zeros((T, hs), BF16)
    b_a, c_a = sel_s[:, 0:hs], sel_s[:, hs:]
    cexp[...] = (c_a * per_state(jnp.exp(cum_ts[...])).T).astype(BF16)
    b_ab, c_ab, b_db, c_db = b_a.astype(BF16), c_a.astype(BF16), bd_s[...], cds[...]
    for k in range(heads):
        only = lane_head == k
        s_a = nt(c_ab, jnp.where(only, b_ab, zero_b))
        s_d = nt(c_db, jnp.where(only, b_db, zero_b))
        g_a = jnp.where(mask_a, cum_s[:, k:k + 1] - cum_ts[k:k + 1, :], -1e30)
        g_d = jnp.where(mask_d, cum_s[:, heads + k:heads + k + 1] - cum_ts[heads + k:heads + k + 1, :], -1e30)
        sc[k // 2, :, (k % 2) * T:(k % 2 + 1) * T] = (s_a * jnp.exp(g_a) + s_d * jnp.exp(g_d)).astype(BF16)

    def times_values(scores, v_tile):
        zero = jnp.zeros((T, 128), BF16)
        stacked = jnp.concatenate(
            [jnp.where(first, v_tile, zero), jnp.where(first, zero, v_tile)], axis=0
        )
        return mm(scores, stacked)

    for e in range(G):
        @pl.when(e != q)
        def _():
            copy_to(dj.at[0], drecv.at[e], d_send.at[0], d_recv.at[e], r, c).wait_recv()
    logs = [drecv[e, pl.ds(i0, keep), :] for e in range(G)]
    tdec[...] = sum(logs)
    decays = [jnp.exp(v)[:, None, :] for v in logs]

    def total_decay(k):
        return copy_to(tdec, tdrecv.at[g], t_send.at[0, k], t_recv.at[0, g], r, c + G * k)

    def total_state(k):
        return copy_to(tbuf, trecv.at[g], t_send.at[1, k], t_recv.at[1, g], r, c + G * k)

    def later(k):
        return g + k < n_grp

    for e in range(G):
        @pl.when(e != q)
        def _():
            copy_to(fbuf.at[0], frecv.at[e], f_send.at[0], f_recv.at[e], r, c).wait_recv()
    for level in range(2, n_grp + 1):
        tell(level)
    carry = frecv[0].astype(F32)
    for e in range(1, G):
        carry = decays[e] * carry + frecv[e].astype(F32)
    tbuf[...] = carry.astype(BF16)
    for k in range(1, n_grp):
        @pl.when(later(k))
        def _():
            total_decay(k).start()
            total_state(k).start()

    gate[...] = silu(gate[...])
    loads[10].wait()
    for j in range(nj):
        ln = slice(j * 128, (j + 1) * 128)
        acc[:, ln] = times_values(sc[j], vbf[j]) + sk_ref[:, ln] * vals[j]

    mine = (iota((T, rows * pair), 0) // cols) == (iota((T, rows * pair), 1) // pair)
    for j in range(nj):
        src = iota((hs, rows * pair), 0)
        dst = iota((hs, rows * pair), 1) % pair
        rep = (src == dst + j * pair).astype(BF16)
        maps[j] = jnp.where(mine, mm(cexp[...], rep), 0.0).astype(BF16)

    ibuf[...] = jnp.zeros_like(ibuf)
    for m in range(n_grp - 1):
        @pl.when(m < g)
        def _():
            copy_to(tdec, tdrecv.at[m], t_send.at[0, 0], t_recv.at[0, m], r, c).wait_recv()
            copy_to(tbuf, trecv.at[m], t_send.at[1, 0], t_recv.at[1, m], r, c).wait_recv()
            ibuf[...] = jnp.exp(tdrecv[m])[:, None, :] * ibuf[...] + trecv[m].astype(F32)
    carry = ibuf[...]
    for e in range(G):
        pbuf[e] = carry.astype(BF16)
        if e < G - 1:
            carry = decays[e] * carry + frecv[e].astype(F32)
    for j, h, p in peers:
        copy_to(pbuf.at[p], precv.at[q], p_send.at[p], p_recv.at[q], r, base + p).start()
    precv[q] = pbuf[q]

    for back in range(1, n_row):
        @pl.when(r >= back)
        def _():
            slot = r - back
            for cp in down_early(r, slot, 0):
                cp.wait_recv()
            gap = lrecv[slot, 0:heads]
            for nearer in range(1, back):
                gap = gap + lrecv[r - nearer, heads:]
            same = (iota((T, T), 0) % cols) == (iota((T, T), 1) % cols)
            for j in range(nj):
                parts = []
                for k in (2 * j, 2 * j + 1):
                    only = (iota((T, hs), 1) // state) == k
                    s_d = nt(cds[...], jnp.where(only, brecv[slot], jnp.zeros((T, hs), BF16)))
                    g_d = jnp.where(same, cum_s[:, heads + k:heads + k + 1] + gap[k:k + 1, :], -1e30)
                    parts.append((s_d * jnp.exp(g_d)).astype(BF16))
                ln = slice(j * 128, (j + 1) * 128)
                down_value(j, r, slot, 0).wait_recv()
                acc[:, ln] += times_values(jnp.concatenate(parts, axis=1), vrecv[slot, j])

    zero_s = jnp.zeros((state, 128), BF16)
    for e in range(G):
        @pl.when(e != q)
        def _():
            copy_to(pbuf.at[0], precv.at[e], p_send.at[0], p_recv.at[e], r, c).wait_recv()
    for j in range(nj):
        ln = slice(j * 128, (j + 1) * 128)
        blocks = []
        for i in range(rows):
            s = precv[j * share + i // keep, i % keep]
            blocks += [jnp.where(first, s, zero_s), jnp.where(first, zero_s, s)]
        acc[:, ln] += mm(maps[j], jnp.concatenate(blocks, axis=0))

    loads[11].wait()
    loads[12].wait()
    mixed = acc[...] * gate[...]
    gated = norm(mixed, og_ref[...]).astype(BF16)
    result = mm(gated, wo_ref[...]) + tok_ref[...].astype(F32).reshape(T, D)
    out_ref[...] = result.astype(BF16).reshape(rows, cols, D)

    for slot, dr, dc, src in plan:
        @pl.when(there(dr, dc))
        def _():
            copy_to(src, hb.at[slot], h_send.at[slot], h_recv.at[slot], r, c).wait_send()
    for j, h, p in peers:
        copy_to(dj.at[j], drecv.at[q], d_send.at[p], d_recv.at[q], r, c).wait_send()
        copy_to(fbuf.at[p], frecv.at[q], f_send.at[p], f_recv.at[q], r, c).wait_send()
        copy_to(pbuf.at[p], precv.at[q], p_send.at[p], p_recv.at[q], r, c).wait_send()
    for k in range(1, n_grp):
        @pl.when(later(k))
        def _():
            total_decay(k).wait_send()
            total_state(k).wait_send()
    for k in range(1, n_row):
        @pl.when(r < k)
        def _():
            for cp in down_early(r, 0, k):
                cp.wait_send()
            for j in range(nj):
                down_value(j, r, 0, k).wait_send()


def solution(mesh):
    n_row, n_col = mesh.shape["row"], mesh.shape["col"]

    def on_device(
        tokens, norm_gain, w_inner, w_select, w_step, step_bias, rate_across, rate_down,
        conv_weight, conv_bias, skip_gain, out_gain, w_out,
    ):
        rows, cols, D = tokens.shape
        heads = rate_across.shape[0]
        inner = w_out.shape[0]
        hs = w_select.shape[1] // 4
        state = hs // heads
        T = rows * cols
        nj = inner // 128
        share, keep, G = split(nj, rows, n_col)
        n_grp = n_col // G
        dims = (n_row, n_col, rows, cols, heads, state, float(cols * n_col), float(rows * n_row))
        vm = pltpu.VMEM
        dma = pltpu.SemaphoreType.DMA
        operands = (
            tokens, norm_gain[None], w_inner, w_select, w_step.T, step_bias[None], rate_across[None],
            rate_down[None], conv_weight, conv_bias[None], skip_gain[None], out_gain[None], w_out,
        )
        operands = tuple(pltpu.with_memory_space_constraint(o, pltpu.HBM) for o in operands)
        return pl.pallas_call(
            functools.partial(kernel, dims),
            out_shape=jax.ShapeDtypeStruct(tokens.shape, tokens.dtype),
            in_specs=[pl.BlockSpec(memory_space=pltpu.HBM)] * 13,
            out_specs=pl.BlockSpec(memory_space=pltpu.VMEM),
            scratch_shapes=[vm(o.shape, o.dtype) for o in operands] + [dma((13,))] + [
                vm((8, cols, D), BF16), vm((2, cols, D), BF16),
                vm((rows + 2, cols + 16, inner), F32),
                vm((nj, T, 128), F32), vm((nj, T, 128), BF16), vm((T, hs), BF16),
                vm((2 * heads, T), F32), vm((nj, rows, 128), F32),
                vm((G, keep, state, 128), BF16), vm((G, rows, 128), F32), vm((G, keep, state, 128), BF16),
                vm((keep, state, 128), BF16), vm((keep, 128), F32),
                vm((n_grp, keep, state, 128), BF16), vm((n_grp, keep, 128), F32), vm((keep, state, 128), F32),
                vm((G, keep, state, 128), BF16), vm((G, keep, state, 128), BF16),
                vm((n_row, nj, T, 128), BF16), vm((n_row, T, hs), BF16), vm((n_row, 2 * heads, T), F32),
                vm((heads // 2, T, 2 * T), BF16), vm((T, inner), F32), vm((T, inner), F32),
                vm((T, hs), BF16), vm((T, hs), BF16), vm((T, 2 * heads), F32), vm((2 * heads, T), F32),
                vm((hs, T), F32), vm((T, 2 * hs), F32), vm((nj, T, rows * 2 * state), BF16),
                dma((8,)), dma((8,)), dma((G,)), dma((G,)), dma((G,)), dma((G,)),
                dma((2, n_grp)), dma((2, n_grp)), dma((G,)), dma((G,)),
                dma((nj + 2, n_row)), dma((nj + 2, n_row)), pltpu.SemaphoreType.REGULAR((n_grp,)),
            ],
            compiler_params=pltpu.CompilerParams(
                collective_id=0, has_side_effects=True, vmem_limit_bytes=48 << 20
            ),
            name="block",
        )(*operands)

    placed = (P("row", "col", None),) + (P(),) * 12
    return jax.shard_map(
        on_device, mesh=mesh, in_specs=placed, out_specs=P("row", "col", None), check_vma=False
    )
```

```python
import functools
import jax
import jax.numpy as jnp
from jax import lax
from jax.experimental import pallas as pl
from jax.experimental.pallas import tpu as pltpu
from jax.sharding import PartitionSpec as P

MESH = pl.DeviceIdType.MESH
F32 = jnp.float32
BF16 = jnp.bfloat16
HI = lax.Precision.HIGHEST
epsilon = 1e-06


def iota(shape, dim):
    return lax.broadcasted_iota(jnp.int32, shape, dim)


def exact(a, b):
    return jnp.dot(a, b, precision=HI, preferred_element_type=F32)


def mm(a, b):
    return jnp.dot(a, b, preferred_element_type=F32)


def nt(a, b):
    return lax.dot_general(a, b, (((1,), (1,)), ((), ())), preferred_element_type=F32)


def norm(x, gain):
    return x * lax.rsqrt(jnp.mean(x * x, axis=-1, keepdims=True) + epsilon) * gain


def silu(v):
    return v * (1.0 / (1.0 + jnp.exp(-v)))


def softplus(x):
    return jnp.maximum(x, 0.0) + jnp.log1p(jnp.exp(-jnp.abs(x)))


def copy_to(src, dst, send, recv, row, col):
    return pltpu.make_async_remote_copy(
        src_ref=src, dst_ref=dst, send_sem=send, recv_sem=recv,
        device_id=(row, col), device_id_type=MESH,
    )


def split(nj, rows, n_col):
    share = 2 if n_col % (2 * nj) == 0 else 1
    return share, rows // share, nj * share


def kernel(
    dims,
    tok_ref, ng_ref, wi_ref, wsel_ref, wst_ref, sb_ref, ra_ref, rd_ref, cw_ref, cb_ref,
    sk_ref, og_ref, wo_ref,
    out_ref,
    tok_v, ng_v, wi_v, wsel_v, wst_v, sb_v, ra_v, rd_v, cw_v, cb_v, sk_v, og_v, wo_v, w_sem,
    hb, eb, xp, vals, vbf, bd_s, logs_s, dj, fbuf, drecv, frecv, tbuf, tdec, trecv, tdrecv, ibuf, pbuf, precv,
    vrecv, brecv, lrecv, sc, gate, acc, cexp, cds, cum_s, cum_ts, btail, sel_s, maps, pre, lh, norm_s,
    h_send, h_recv, d_send, d_recv, f_send, f_recv, t_send, t_recv, p_send, p_recv, v_send, v_recv, s_send, s_recv, know,
):
    n_row, n_col, rows, cols, heads, state, full_w, height = dims
    T = rows * cols
    loads = [
        pltpu.make_async_copy(src, dst, w_sem.at[k])
        for k, (src, dst) in enumerate((
            (tok_ref, tok_v), (ng_ref, ng_v), (wi_ref, wi_v), (wsel_ref, wsel_v), (wst_ref, wst_v),
            (sb_ref, sb_v), (ra_ref, ra_v), (rd_ref, rd_v), (cw_ref, cw_v), (cb_ref, cb_v),
            (sk_ref, sk_v), (og_ref, og_v), (wo_ref, wo_v),
        ))
    ]
    tok_ref, ng_ref, wi_ref, wsel_ref, wst_ref = tok_v, ng_v, wi_v, wsel_v, wst_v
    sb_ref, ra_ref, rd_ref, cw_ref, cb_ref = sb_v, ra_v, rd_v, cw_v, cb_v
    sk_ref, og_ref, wo_ref = sk_v, og_v, wo_v
    inner = wo_ref.shape[0]
    D = tok_ref.shape[2]
    nj = inner // 128
    share, keep, G = split(nj, rows, n_col)
    n_grp = n_col // G
    hs = heads * state
    nh = 2 * heads
    r = lax.axis_index("row")
    c = lax.axis_index("col")
    g, q = c // G, c % G
    mine_j, mine_h = q // share, q % share
    i0 = mine_h * keep
    if nj == 4:
        far = [3 - mine_j, (mine_j + 2) % 4, mine_j + 1 - 2 * (mine_j % 2), mine_j]
    else:
        far = [(mine_j + k) % nj for k in range(1, nj)] + [mine_j]
    peers = [(j, h, j * share + h) for j in far[:-1] for h in range(share)]
    peers += [(mine_j, h, mine_j * share + h) for h in [(mine_h + k) % share for k in range(1, share)]]
    base = g * G

    barrier = pltpu.get_barrier_semaphore()

    plan = (
        (4, 1, 1, eb.at[1]),
        (5, 1, -1, eb.at[0]),
        (6, -1, 1, eb.at[1]),
        (7, -1, -1, eb.at[0]),
        (0, 1, 0, tok_ref.at[rows - 1]),
        (1, -1, 0, tok_ref.at[0]),
        (2, 0, 1, eb.at[1]),
        (3, 0, -1, eb.at[0]),
    )

    def there(dr, dc):
        return (r + dr >= 0) & (r + dr < n_row) & (c + dc >= 0) & (c + dc < n_col)

    loads[0].start()
    hb[...] = jnp.zeros_like(hb)
    eb[...] = jnp.zeros_like(eb)
    lh[...] = jnp.zeros_like(lh)
    for i in range(rows):
        xp[i + 1, 0:8, :] = jnp.zeros((8, inner), F32)
        xp[i + 1, 8 + cols:16 + cols, :] = jnp.zeros((8, inner), F32)
    friends = [(dr, dc, there(dr, dc)) for _, dr, dc, _ in plan]
    friends += [(0, dc, (q + dc >= 0) & (q + dc < G)) for k in range(2, G) for dc in (k, -k)]
    friends += [(dr, 0, there(dr, 0)) for k in range(2, n_row) for dr in (k, -k)]
    for dr, dc, ok in friends:
        @pl.when(ok)
        def _():
            pl.semaphore_signal(barrier, inc=1, device_id=(r + dr, c + dc), device_id_type=MESH)
    for load in loads[1:]:
        load.start()

    loads[0].wait()
    eb[0, 0:rows, :] = tok_ref[:, 0, :]
    eb[1, 0:rows, :] = tok_ref[:, cols - 1, :]
    loads[1].wait()
    x = tok_ref[...].astype(F32).reshape(T, D)
    normed = norm(x, ng_ref[...]).astype(BF16)
    norm_s[...] = normed
    loads[2].wait()
    main_x = mm(normed, wi_ref[:, :inner]).astype(BF16).astype(F32)
    for i in range(rows):
        xp[i + 1, 8:8 + cols, :] = main_x[i * cols:(i + 1) * cols]
    pl.semaphore_wait(barrier, sum(jnp.where(ok, 1, 0) for _, _, ok in friends))

    for slot, dr, dc, src in plan:
        @pl.when(there(dr, dc))
        def _():
            copy_to(src, hb.at[slot], h_send, h_recv, r + dr, c + dc).start()

    def tell(level):
        if 2 < level <= n_grp:
            @pl.when(g + level - 1 < n_grp)
            def _():
                pl.semaphore_wait(know.at[level - 3], 1)
        if 2 <= level < n_grp:
            @pl.when((g >= 1) & (g + level - 1 < n_grp))
            def _():
                pl.semaphore_signal(know.at[level - 2], inc=1, device_id=(r, c - G), device_id_type=MESH)

    for k in (4, 5, 6, 7):
        loads[k].wait()

    def column(row):
        width = row.shape[1]
        square = jnp.broadcast_to(row, (width, width))
        return jnp.sum(
            jnp.where(iota((width, width), 0) == iota((width, width), 1), square, 0.0), axis=1, keepdims=True
        )

    t_i, u_i = iota((T, T), 0), iota((T, T), 1)
    row_same = (t_i // cols) == (u_i // cols)
    col_same = (t_i % cols) == (u_i % cols)
    step_t = nt(wst_ref[...], normed)
    rate = jnp.concatenate([column(ra_ref[...]) / full_w, column(rd_ref[...]) / height], axis=0)
    logs_t = -softplus(step_t + column(sb_ref[...])) * rate

    def thirds(v):
        hi = v.astype(BF16)
        rest = v - hi.astype(F32)
        mid = rest.astype(BF16)
        return hi, mid, (rest - mid.astype(F32)).astype(BF16)

    up = t_i <= u_i
    sums = jnp.concatenate(
        [jnp.where(m, 1.0, 0.0).astype(BF16) for m in (row_same & up, row_same, col_same & up, col_same)], axis=1
    )
    parts = mm(jnp.concatenate(thirds(logs_t), axis=0), sums)
    summed = parts[:nh] + parts[nh:2 * nh] + parts[2 * nh:]
    cum_t = jnp.concatenate([summed[:heads, 0:T], summed[heads:, 2 * T:3 * T]], axis=0)
    tot_t = jnp.concatenate([summed[:heads, T:2 * T], summed[heads:, 3 * T:]], axis=0)
    logs_s[0:heads] = tot_t[heads:] - cum_t[heads:]
    logs_s[heads:] = tot_t[heads:]
    cum_ts[...] = cum_t
    cum = jnp.concatenate([cum_t, jnp.zeros((T - nh, T), F32)], axis=0).T[:, :nh]
    cum_s[...] = cum

    row_tot = jnp.concatenate([cum[(i + 1) * cols - 1:(i + 1) * cols] for i in range(rows)], axis=0)
    spread = jnp.where(iota((nh, inner), 0) == iota((nh, inner), 1) // (inner // heads), 1.0, 0.0).astype(BF16)
    wide = sum(mm(part, spread) for part in thirds(row_tot))
    for j in range(nj):
        dj[j] = wide[:, j * 128:(j + 1) * 128]
    for j, h, p in peers:
        copy_to(dj.at[j], drecv.at[q], d_send, d_recv, r, base + p).start()

    def per_state(v):
        return jnp.concatenate([jnp.broadcast_to(v[k:k + 1], (state, T)) for k in range(heads)], axis=0)

    loads[3].wait()
    sel = mm(normed, wsel_ref[...])
    sel_s[...] = sel[:, :2 * hs]
    btail[...] = sel[:, :hs].T * per_state(jnp.exp(tot_t - cum_t))
    bd_s[...] = sel[:, 2 * hs:3 * hs].astype(BF16)
    cds[...] = sel[:, 3 * hs:].astype(BF16)

    def down_early(to_row, slot, dest):
        return (
            copy_to(bd_s, brecv.at[slot], v_send.at[1, dest - 1], v_recv.at[1, slot], to_row, c),
            copy_to(logs_s, lrecv.at[slot], v_send.at[2, dest - 1], v_recv.at[2, slot], to_row, c),
        )

    def down_value(j, to_row, slot, dest):
        return copy_to(vbf.at[j], vrecv.at[slot, j], v_send.at[0, dest - 1], v_recv.at[0, slot], to_row, c)

    def down_values(slot, dest):
        return copy_to(vbf, vrecv.at[slot], v_send.at[0, dest - 1], v_recv.at[0, slot], r, c)

    for k in range(1, n_row):
        @pl.when(r < k)
        def _():
            for cp in down_early(k, r, k):
                cp.start()

    loads[8].wait()
    loads[9].wait()
    for j in range(nj):
        ln = slice(j * 128, (j + 1) * 128)
        w9 = [cw_ref[a, b:b + 1, ln] for a in range(3) for b in range(3)]
        bias = cb_ref[:, ln]
        for i in range(rows):
            total = jnp.zeros((cols, 128), F32) + bias
            for a in range(3):
                if 0 <= i + a - 1 < rows:
                    for b in range(3):
                        total = total + xp[i + a, 7 + b:7 + b + cols, ln] * w9[a * 3 + b]
            pre[j, i * cols:(i + 1) * cols] = total
            vals[j, i * cols:(i + 1) * cols] = silu(total)

    beside = sum(jnp.where(there(dr, dc), 1, 0) for _, dr, dc, _ in plan)

    def halos(n):
        some = hb.at[pl.ds(0, n)]
        return copy_to(some, some, h_send, h_recv, r, c)

    for n in (3, 5, 8):
        @pl.when(beside == n)
        def _():
            halos(n).wait_recv()
    edge = norm(hb[...].astype(F32).reshape(8 * cols, D), ng_ref[...]).astype(BF16)
    edge_x = mm(edge, wi_ref[:, :inner]).astype(BF16).astype(F32)
    xp[0, 8:8 + cols, :] = edge_x[0:cols]
    xp[rows + 1, 8:8 + cols, :] = edge_x[cols:2 * cols]
    lh[0, 8:8 + rows, :] = edge_x[2 * cols:2 * cols + rows]
    lh[1, 8:8 + rows, :] = edge_x[3 * cols:3 * cols + rows]
    xp[0, 7:8, :] = edge_x[4 * cols + rows - 1:4 * cols + rows]
    xp[0, 8 + cols:9 + cols, :] = edge_x[5 * cols + rows - 1:5 * cols + rows]
    xp[rows + 1, 7:8, :] = edge_x[6 * cols:6 * cols + 1]
    xp[rows + 1, 8 + cols:9 + cols, :] = edge_x[7 * cols:7 * cols + 1]

    first = iota((1, 128), 1) < 64
    pair = 2 * state
    own = (iota((rows * pair, T), 0) // pair) == (iota((rows * pair, T), 1) // cols)
    for j in far:
        ln = pl.ds(pl.multiple_of(j * 128, 128), 128)
        for i, a, edge_row in ((0, 0, 0), (rows - 1, 2, rows + 1)):
            at = slice(i * cols, (i + 1) * cols)
            total = pre[j, at]
            for b in range(3):
                total = total + xp[edge_row, 7 + b:7 + b + cols, ln] * cw_ref[a, b:b + 1, ln]
            pre[j, at] = total
            vals[j, at] = silu(total)
        for e, at, b in ((0, 0, 0), (1, cols - 1, 2)):
            some = pl.ds(at, rows, stride=cols)
            total = pre[j, some, :]
            for a in range(3):
                total = total + lh[e, 7 + a:7 + a + rows, ln] * cw_ref[a, b:b + 1, ln]
            vals[j, some, :] = silu(total)
        vbf[j] = vals[j].astype(BF16)

        rowed = pl.ds(pl.multiple_of(j * pair, pair), pair)
        piece = jnp.concatenate([btail[rowed, :]] * rows, axis=0)
        piece = jnp.where(own, piece, 0.0).astype(BF16)
        res = mm(piece, vbf[j])
        for i in range(rows):
            top = res[i * pair:i * pair + state]
            bottom = res[i * pair + state:(i + 1) * pair]
            fbuf[j * share + i // keep, i % keep] = jnp.where(first, top, bottom).astype(BF16)
        for j2, h, p in peers:
            if j2 is j:
                copy_to(fbuf.at[p], frecv.at[q], f_send, f_recv, r, base + p).start()
        for k in range(1, n_row):
            @pl.when(r < k)
            def _():
                down_value(j, k, r, k).start()

    @pl.when(c == 0)
    def _():
        copy_to(fbuf, precv, s_send, s_recv, r, c + 1).start()
        precv[...] = jnp.zeros_like(precv)

    frecv[q] = fbuf[q]
    drecv[q] = dj[mine_j]

    low = u_i <= t_i
    mask_a, mask_d = row_same & low, col_same & low
    lane_head = iota((T, hs), 1) // state
    zero_b = jnp.zeros((T, hs), BF16)
    b_a, c_a = sel_s[:, 0:hs], sel_s[:, hs:]
    cexp[...] = (c_a * per_state(jnp.exp(cum_ts[...])).T).astype(BF16)
    b_ab, c_ab, b_db, c_db = b_a.astype(BF16), c_a.astype(BF16), bd_s[...], cds[...]
    for k in range(heads):
        only = lane_head == k
        s_a = nt(c_ab, jnp.where(only, b_ab, zero_b))
        s_d = nt(c_db, jnp.where(only, b_db, zero_b))
        g_a = jnp.where(mask_a, cum_s[:, k:k + 1] - cum_ts[k:k + 1, :], -1e30)
        g_d = jnp.where(mask_d, cum_s[:, heads + k:heads + k + 1] - cum_ts[heads + k:heads + k + 1, :], -1e30)
        sc[k // 2, :, (k % 2) * T:(k % 2 + 1) * T] = (s_a * jnp.exp(g_a) + s_d * jnp.exp(g_d)).astype(BF16)

    def times_values(scores, v_tile):
        zero = jnp.zeros((T, 128), BF16)
        stacked = jnp.concatenate(
            [jnp.where(first, v_tile, zero), jnp.where(first, zero, v_tile)], axis=0
        )
        return mm(scores, stacked)

    others = pl.ds(0, G - 1)

    def whole(ref, send, recv):
        return copy_to(ref.at[others], ref.at[others], send, recv, r, c)

    whole(drecv, d_send, d_recv).wait_recv()
    logs = [drecv[e, pl.ds(i0, keep), :] for e in range(G)]
    tdec[...] = sum(logs)
    decays = [jnp.exp(v)[:, None, :] for v in logs]

    def total_decay(k):
        return copy_to(tdec, tdrecv.at[g], t_send.at[0, k - 1], t_recv.at[0, g], r, c + G * k)

    def total_state(k):
        return copy_to(tbuf, trecv.at[g], t_send.at[1, k - 1], t_recv.at[1, g], r, c + G * k)

    def later(k):
        return g + k < n_grp

    whole(frecv, f_send, f_recv).wait_recv()
    for level in range(2, n_grp + 1):
        tell(level)
    carry = frecv[0].astype(F32)
    for e in range(1, G):
        carry = decays[e] * carry + frecv[e].astype(F32)
    tbuf[...] = carry.astype(BF16)
    for k in range(1, n_grp):
        @pl.when(later(k))
        def _():
            total_decay(k).start()
            total_state(k).start()

    gate[...] = silu(mm(norm_s[...], wi_ref[:, inner:]).astype(BF16).astype(F32))
    loads[10].wait()
    for j in range(nj):
        ln = slice(j * 128, (j + 1) * 128)
        acc[:, ln] = times_values(sc[j], vbf[j]) + sk_ref[:, ln] * vals[j]

    mine = (iota((T, rows * pair), 0) // cols) == (iota((T, rows * pair), 1) // pair)
    for j in range(nj):
        src = iota((hs, rows * pair), 0)
        dst = iota((hs, rows * pair), 1) % pair
        rep = (src == dst + j * pair).astype(BF16)
        maps[j] = jnp.where(mine, mm(cexp[...], rep), 0.0).astype(BF16)

    ibuf[...] = jnp.zeros_like(ibuf)
    for m in range(n_grp - 1):
        @pl.when(m < g)
        def _():
            copy_to(tdec, tdrecv.at[m], t_send.at[0, 0], t_recv.at[0, m], r, c).wait_recv()
            copy_to(tbuf, trecv.at[m], t_send.at[1, 0], t_recv.at[1, m], r, c).wait_recv()
            ibuf[...] = jnp.exp(tdrecv[m])[:, None, :] * ibuf[...] + trecv[m].astype(F32)
    carry = ibuf[...]
    for e in range(G):
        pbuf[e] = carry.astype(BF16)
        if e < G - 1:
            carry = decays[e] * carry + frecv[e].astype(F32)
    for j, h, p in peers:
        @pl.when(base + p > 1)
        def _():
            copy_to(pbuf.at[p], precv.at[q], p_send, p_recv, r, base + p).start()

    @pl.when(c > 1)
    def _():
        precv[q] = pbuf[q]

    for back in range(1, n_row):
        @pl.when(r >= back)
        def _():
            slot = r - back
            for cp in down_early(r, slot, 1):
                cp.wait_recv()
            down_values(slot, 1).wait_recv()
            gap = lrecv[slot, 0:heads]
            for nearer in range(1, back):
                gap = gap + lrecv[r - nearer, heads:]
            same = (iota((T, T), 0) % cols) == (iota((T, T), 1) % cols)
            for j in range(nj):
                parts = []
                for k in (2 * j, 2 * j + 1):
                    only = (iota((T, hs), 1) // state) == k
                    s_d = nt(cds[...], jnp.where(only, brecv[slot], jnp.zeros((T, hs), BF16)))
                    g_d = jnp.where(same, cum_s[:, heads + k:heads + k + 1] + gap[k:k + 1, :], -1e30)
                    parts.append((s_d * jnp.exp(g_d)).astype(BF16))
                ln = slice(j * 128, (j + 1) * 128)
                acc[:, ln] += times_values(jnp.concatenate(parts, axis=1), vrecv[slot, j])

    @pl.when(c == 1)
    def _():
        copy_to(fbuf, precv, s_send, s_recv, r, c).wait_recv()

    zero_s = jnp.zeros((state, 128), BF16)
    @pl.when(c > 1)
    def _():
        whole(precv, p_send, p_recv).wait_recv()

    for j in range(nj):
        ln = slice(j * 128, (j + 1) * 128)
        blocks = []
        for i in range(rows):
            s = precv[j * share + i // keep, i % keep]
            blocks += [jnp.where(first, s, zero_s), jnp.where(first, zero_s, s)]
        acc[:, ln] += mm(maps[j], jnp.concatenate(blocks, axis=0))

    loads[11].wait()
    loads[12].wait()
    mixed = acc[...] * gate[...]
    gated = norm(mixed, og_ref[...]).astype(BF16)
    result = mm(gated, wo_ref[...]) + tok_ref[...].astype(F32).reshape(T, D)
    out_ref[...] = result.astype(BF16).reshape(rows, cols, D)

    for n in (3, 5, 8):
        @pl.when(beside == n)
        def _():
            halos(n).wait_send()
    whole(drecv, d_send, d_recv).wait_send()
    whole(frecv, f_send, f_recv).wait_send()
    skipped = jnp.where(g > 0, 0, jnp.where(c > 1, 2, 1))
    for n in range(3):
        @pl.when(skipped == n)
        def _():
            some = pbuf.at[pl.ds(0, G - 1 - n)]
            copy_to(some, some, p_send, p_recv, r, c).wait_send()

    @pl.when(c == 0)
    def _():
        copy_to(fbuf, precv, s_send, s_recv, r, c).wait_send()
    for k in range(1, n_grp):
        @pl.when(later(k))
        def _():
            total_decay(k).wait_send()
            total_state(k).wait_send()
    for k in range(1, n_row):
        @pl.when(r < k)
        def _():
            for cp in down_early(r, 0, k):
                cp.wait_send()
            down_values(0, k).wait_send()


def solution(mesh):
    n_row, n_col = mesh.shape["row"], mesh.shape["col"]

    def on_device(
        tokens, norm_gain, w_inner, w_select, w_step, step_bias, rate_across, rate_down,
        conv_weight, conv_bias, skip_gain, out_gain, w_out,
    ):
        rows, cols, D = tokens.shape
        heads = rate_across.shape[0]
        inner = w_out.shape[0]
        hs = w_select.shape[1] // 4
        state = hs // heads
        T = rows * cols
        nj = inner // 128
        share, keep, G = split(nj, rows, n_col)
        n_grp = n_col // G
        dims = (n_row, n_col, rows, cols, heads, state, float(cols * n_col), float(rows * n_row))
        vm = pltpu.VMEM
        dma = pltpu.SemaphoreType.DMA
        operands = (
            tokens, norm_gain[None], w_inner, w_select, w_step.T, step_bias[None], rate_across[None],
            rate_down[None], conv_weight, conv_bias[None], skip_gain[None], out_gain[None], w_out,
        )
        operands = tuple(pltpu.with_memory_space_constraint(o, pltpu.HBM) for o in operands)
        return pl.pallas_call(
            functools.partial(kernel, dims),
            out_shape=jax.ShapeDtypeStruct(tokens.shape, tokens.dtype),
            in_specs=[pl.BlockSpec(memory_space=pltpu.HBM)] * 13,
            out_specs=pl.BlockSpec(memory_space=pltpu.VMEM),
            scratch_shapes=[vm(o.shape, o.dtype) for o in operands] + [dma((13,))] + [
                vm((8, cols, D), BF16), vm((2, cols, D), BF16),
                vm((rows + 2, cols + 16, inner), F32),
                vm((nj, T, 128), F32), vm((nj, T, 128), BF16), vm((T, hs), BF16),
                vm((2 * heads, T), F32), vm((nj, rows, 128), F32),
                vm((G, keep, state, 128), BF16), vm((G, rows, 128), F32), vm((G, keep, state, 128), BF16),
                vm((keep, state, 128), BF16), vm((keep, 128), F32),
                vm((n_grp, keep, state, 128), BF16), vm((n_grp, keep, 128), F32), vm((keep, state, 128), F32),
                vm((G, keep, state, 128), BF16), vm((G, keep, state, 128), BF16),
                vm((n_row, nj, T, 128), BF16), vm((n_row, T, hs), BF16), vm((n_row, 2 * heads, T), F32),
                vm((heads // 2, T, 2 * T), BF16), vm((T, inner), F32), vm((T, inner), F32),
                vm((T, hs), BF16), vm((T, hs), BF16), vm((T, 2 * heads), F32), vm((2 * heads, T), F32),
                vm((hs, T), F32), vm((T, 2 * hs), F32), vm((nj, T, rows * 2 * state), BF16),
                vm((nj, T, 128), F32), vm((2, rows + 16, inner), F32), vm((T, D), BF16),
                dma, dma, dma, dma, dma, dma,
                dma((2, max(n_grp - 1, 1))), dma((2, max(n_grp - 1, 1))), dma, dma,
                dma((3, n_row - 1)), dma((3, n_row - 1)), dma, dma, pltpu.SemaphoreType.REGULAR((max(n_grp - 2, 1),)),
            ],
            compiler_params=pltpu.CompilerParams(
                collective_id=0, has_side_effects=True, vmem_limit_bytes=48 << 20
            ),
            name="block",
        )(*operands)

    placed = (P("row", "col", None),) + (P(),) * 12
    return jax.shard_map(
        on_device, mesh=mesh, in_specs=placed, out_specs=P("row", "col", None), check_vma=False
    )
```

```python
import functools
import jax
import jax.numpy as jnp
from jax import lax
from jax.experimental import pallas as pl
from jax.experimental.pallas import tpu as pltpu
from jax.sharding import PartitionSpec as P

MESH = pl.DeviceIdType.MESH
F32 = jnp.float32
BF16 = jnp.bfloat16
HI = lax.Precision.HIGHEST
epsilon = 1e-06


def iota(shape, dim):
    return lax.broadcasted_iota(jnp.int32, shape, dim)


def exact(a, b):
    return jnp.dot(a, b, precision=HI, preferred_element_type=F32)


def mm(a, b):
    return jnp.dot(a, b, preferred_element_type=F32)


def nt(a, b):
    return lax.dot_general(a, b, (((1,), (1,)), ((), ())), preferred_element_type=F32)


def norm(x, gain):
    return x * lax.rsqrt(jnp.mean(x * x, axis=-1, keepdims=True) + epsilon) * gain


def silu(v):
    return v * (1.0 / (1.0 + jnp.exp(-v)))


def softplus(x):
    return jnp.maximum(x, 0.0) + jnp.log1p(jnp.exp(-jnp.abs(x)))


def copy_to(src, dst, send, recv, row, col):
    return pltpu.make_async_remote_copy(
        src_ref=src, dst_ref=dst, send_sem=send, recv_sem=recv,
        device_id=(row, col), device_id_type=MESH,
    )


def split(nj, rows, n_col):
    share = 2 if n_col % (2 * nj) == 0 else 1
    return share, rows // share, nj * share


def kernel(
    dims,
    tok_ref, ng_ref, wi_ref, wsel_ref, wst_ref, sb_ref, ra_ref, rd_ref, cw_ref, cb_ref,
    sk_ref, og_ref, wo_ref,
    out_ref,
    tok_v, ng_v, wi_v, wsel_v, wst_v, sb_v, ra_v, rd_v, cw_v, cb_v, sk_v, og_v, wo_v, w_sem,
    hb, eb, xp, vals, vbf, bd_s, logs_s, dj, fbuf, drecv, frecv, tbuf, tdec, trecv, tdrecv, ibuf, pbuf, precv,
    vrecv, brecv, lrecv, sc, gate, acc, cexp, cds, cum_s, cum_ts, btail, sel_s, maps, pre, lh, norm_s,
    h_send, h_recv, d_send, d_recv, f_send, f_recv, t_send, t_recv, p_send, p_recv, v_send, v_recv, s_send, s_recv, near,
):
    n_row, n_col, rows, cols, heads, state, full_w, height = dims
    T = rows * cols
    loads = [
        pltpu.make_async_copy(src, dst, w_sem.at[k])
        for k, (src, dst) in enumerate((
            (tok_ref, tok_v), (ng_ref, ng_v), (wi_ref, wi_v), (wsel_ref, wsel_v), (wst_ref, wst_v),
            (sb_ref, sb_v), (ra_ref, ra_v), (rd_ref, rd_v), (cw_ref, cw_v), (cb_ref, cb_v),
            (sk_ref, sk_v), (og_ref, og_v), (wo_ref, wo_v),
        ))
    ]
    tok_ref, ng_ref, wi_ref, wsel_ref, wst_ref = tok_v, ng_v, wi_v, wsel_v, wst_v
    sb_ref, ra_ref, rd_ref, cw_ref, cb_ref = sb_v, ra_v, rd_v, cw_v, cb_v
    sk_ref, og_ref, wo_ref = sk_v, og_v, wo_v
    inner = wo_ref.shape[0]
    D = tok_ref.shape[2]
    nj = inner // 128
    share, keep, G = split(nj, rows, n_col)
    n_grp = n_col // G
    hs = heads * state
    nh = 2 * heads
    r = lax.axis_index("row")
    c = lax.axis_index("col")
    g, q = c // G, c % G
    mine_j, mine_h = q // share, q % share
    i0 = mine_h * keep
    if nj == 4:
        far = [3 - mine_j, (mine_j + 2) % 4, mine_j + 1 - 2 * (mine_j % 2), mine_j]
    else:
        far = [(mine_j + k) % nj for k in range(1, nj)] + [mine_j]
    peers = [(j, h, j * share + h) for j in far[:-1] for h in range(share)]
    peers += [(mine_j, h, mine_j * share + h) for h in [(mine_h + k) % share for k in range(1, share)]]
    base = g * G

    barrier = pltpu.get_barrier_semaphore()

    plan = (
        (4, 1, 1, eb.at[1]),
        (5, 1, -1, eb.at[0]),
        (6, -1, 1, eb.at[1]),
        (7, -1, -1, eb.at[0]),
        (0, 1, 0, tok_ref.at[rows - 1]),
        (1, -1, 0, tok_ref.at[0]),
        (2, 0, 1, eb.at[1]),
        (3, 0, -1, eb.at[0]),
    )

    def there(dr, dc):
        return (r + dr >= 0) & (r + dr < n_row) & (c + dc >= 0) & (c + dc < n_col)

    loads[0].start()
    hb[...] = jnp.zeros_like(hb)
    eb[...] = jnp.zeros_like(eb)
    lh[...] = jnp.zeros_like(lh)
    for i in range(rows):
        xp[i + 1, 0:8, :] = jnp.zeros((8, inner), F32)
        xp[i + 1, 8 + cols:16 + cols, :] = jnp.zeros((8, inner), F32)
    friends = [(dr, dc, there(dr, dc)) for _, dr, dc, _ in plan]
    friends += [(dr, 0, there(dr, 0)) for k in range(2, n_row) for dr in (k, -k)]
    ahead = [(0, dc, q + dc < G) for dc in range(2, G)] + [(0, G * k, g + k < n_grp) for k in range(1, n_grp)]
    for dr, dc, ok in friends + ahead:
        @pl.when(ok)
        def _():
            pl.semaphore_signal(barrier, inc=1, device_id=(r + dr, c + dc), device_id_type=MESH)
    for load in loads[1:]:
        load.start()

    loads[0].wait()
    eb[0, 0:rows, :] = tok_ref[:, 0, :]
    eb[1, 0:rows, :] = tok_ref[:, cols - 1, :]
    pl.semaphore_wait(barrier, sum(jnp.where(ok, 1, 0) for _, _, ok in friends) + jnp.maximum(q - 1, 0) + g)

    for slot, dr, dc, src in plan:
        @pl.when(there(dr, dc))
        def _():
            copy_to(src, hb.at[slot], h_send, h_recv, r + dr, c + dc).start()

    for dc in range(2, G):
        @pl.when(q >= dc)
        def _():
            pl.semaphore_signal(near.at[0], inc=1, device_id=(r, c - dc), device_id_type=MESH)
    for k in range(1, n_grp):
        @pl.when(g >= k)
        def _():
            pl.semaphore_signal(near.at[1], inc=1, device_id=(r, c - G * k), device_id_type=MESH)

    loads[1].wait()
    x = tok_ref[...].astype(F32).reshape(T, D)
    normed = norm(x, ng_ref[...]).astype(BF16)
    norm_s[...] = normed
    loads[2].wait()
    main_x = mm(normed, wi_ref[:, :inner]).astype(BF16).astype(F32)
    for i in range(rows):
        xp[i + 1, 8:8 + cols, :] = main_x[i * cols:(i + 1) * cols]
    for k in (4, 5, 6, 7):
        loads[k].wait()

    def column(row):
        width = row.shape[1]
        square = jnp.broadcast_to(row, (width, width))
        return jnp.sum(
            jnp.where(iota((width, width), 0) == iota((width, width), 1), square, 0.0), axis=1, keepdims=True
        )

    t_i, u_i = iota((T, T), 0), iota((T, T), 1)
    row_same = (t_i // cols) == (u_i // cols)
    col_same = (t_i % cols) == (u_i % cols)
    step_t = nt(wst_ref[...], normed)
    rate = jnp.concatenate([column(ra_ref[...]) / full_w, column(rd_ref[...]) / height], axis=0)
    logs_t = -softplus(step_t + column(sb_ref[...])) * rate

    def thirds(v):
        hi = v.astype(BF16)
        rest = v - hi.astype(F32)
        mid = rest.astype(BF16)
        return hi, mid, (rest - mid.astype(F32)).astype(BF16)

    up = t_i <= u_i
    sums = jnp.concatenate(
        [jnp.where(m, 1.0, 0.0).astype(BF16) for m in (row_same & up, row_same, col_same & up, col_same)], axis=1
    )
    parts = mm(jnp.concatenate(thirds(logs_t), axis=0), sums)
    summed = parts[:nh] + parts[nh:2 * nh] + parts[2 * nh:]
    cum_t = jnp.concatenate([summed[:heads, 0:T], summed[heads:, 2 * T:3 * T]], axis=0)
    tot_t = jnp.concatenate([summed[:heads, T:2 * T], summed[heads:, 3 * T:]], axis=0)
    logs_s[0:heads] = tot_t[heads:] - cum_t[heads:]
    logs_s[heads:] = tot_t[heads:]
    cum_ts[...] = cum_t
    cum = jnp.concatenate([cum_t, jnp.zeros((T - nh, T), F32)], axis=0).T[:, :nh]
    cum_s[...] = cum

    row_tot = jnp.concatenate([cum[(i + 1) * cols - 1:(i + 1) * cols] for i in range(rows)], axis=0)
    spread = jnp.where(iota((nh, inner), 0) == iota((nh, inner), 1) // (inner // heads), 1.0, 0.0).astype(BF16)
    wide = sum(mm(part, spread) for part in thirds(row_tot))
    for j in range(nj):
        dj[j] = wide[:, j * 128:(j + 1) * 128]

    def per_state(v):
        return jnp.concatenate([jnp.broadcast_to(v[k:k + 1], (state, T)) for k in range(heads)], axis=0)

    loads[3].wait()
    sel = mm(normed, wsel_ref[...])
    sel_s[...] = sel[:, :2 * hs]
    btail[...] = sel[:, :hs].T * per_state(jnp.exp(tot_t - cum_t))
    bd_s[...] = sel[:, 2 * hs:3 * hs].astype(BF16)
    cds[...] = sel[:, 3 * hs:].astype(BF16)

    def down_early(to_row, slot, dest):
        return (
            copy_to(bd_s, brecv.at[slot], v_send.at[1, dest - 1], v_recv.at[1, slot], to_row, c),
            copy_to(logs_s, lrecv.at[slot], v_send.at[2, dest - 1], v_recv.at[2, slot], to_row, c),
        )

    def down_value(j, to_row, slot, dest):
        return copy_to(vbf.at[j], vrecv.at[slot, j], v_send.at[0, dest - 1], v_recv.at[0, slot], to_row, c)

    def down_values(slot, dest):
        return copy_to(vbf, vrecv.at[slot], v_send.at[0, dest - 1], v_recv.at[0, slot], r, c)

    for k in range(1, n_row):
        @pl.when(r < k)
        def _():
            for cp in down_early(k, r, k):
                cp.start()

    loads[8].wait()
    loads[9].wait()
    for j in range(nj):
        ln = slice(j * 128, (j + 1) * 128)
        w9 = [cw_ref[a, b:b + 1, ln] for a in range(3) for b in range(3)]
        bias = cb_ref[:, ln]
        for i in range(rows):
            total = jnp.zeros((cols, 128), F32) + bias
            for a in range(3):
                if 0 <= i + a - 1 < rows:
                    for b in range(3):
                        total = total + xp[i + a, 7 + b:7 + b + cols, ln] * w9[a * 3 + b]
            pre[j, i * cols:(i + 1) * cols] = total
            vals[j, i * cols:(i + 1) * cols] = silu(total)

    @pl.when(q < G - 2)
    def _():
        pl.semaphore_wait(near.at[0], G - 2 - q)

    for j, h, p in peers:
        copy_to(dj.at[j], drecv.at[q], d_send, d_recv, r, base + p).start()

    beside = sum(jnp.where(there(dr, dc), 1, 0) for _, dr, dc, _ in plan)

    def halos(n):
        some = hb.at[pl.ds(0, n)]
        return copy_to(some, some, h_send, h_recv, r, c)

    for n in (3, 5, 8):
        @pl.when(beside == n)
        def _():
            halos(n).wait_recv()
    edge = norm(hb[...].astype(F32).reshape(8 * cols, D), ng_ref[...]).astype(BF16)
    edge_x = mm(edge, wi_ref[:, :inner]).astype(BF16).astype(F32)
    xp[0, 8:8 + cols, :] = edge_x[0:cols]
    xp[rows + 1, 8:8 + cols, :] = edge_x[cols:2 * cols]
    lh[0, 8:8 + rows, :] = edge_x[2 * cols:2 * cols + rows]
    lh[1, 8:8 + rows, :] = edge_x[3 * cols:3 * cols + rows]
    xp[0, 7:8, :] = edge_x[4 * cols + rows - 1:4 * cols + rows]
    xp[0, 8 + cols:9 + cols, :] = edge_x[5 * cols + rows - 1:5 * cols + rows]
    xp[rows + 1, 7:8, :] = edge_x[6 * cols:6 * cols + 1]
    xp[rows + 1, 8 + cols:9 + cols, :] = edge_x[7 * cols:7 * cols + 1]

    first = iota((1, 128), 1) < 64
    pair = 2 * state
    own = (iota((rows * pair, T), 0) // pair) == (iota((rows * pair, T), 1) // cols)
    for j in far:
        ln = pl.ds(pl.multiple_of(j * 128, 128), 128)
        for i, a, edge_row in ((0, 0, 0), (rows - 1, 2, rows + 1)):
            at = slice(i * cols, (i + 1) * cols)
            total = pre[j, at]
            for b in range(3):
                total = total + xp[edge_row, 7 + b:7 + b + cols, ln] * cw_ref[a, b:b + 1, ln]
            pre[j, at] = total
            vals[j, at] = silu(total)
        for e, at, b in ((0, 0, 0), (1, cols - 1, 2)):
            some = pl.ds(at, rows, stride=cols)
            total = pre[j, some, :]
            for a in range(3):
                total = total + lh[e, 7 + a:7 + a + rows, ln] * cw_ref[a, b:b + 1, ln]
            vals[j, some, :] = silu(total)
        vbf[j] = vals[j].astype(BF16)

        rowed = pl.ds(pl.multiple_of(j * pair, pair), pair)
        piece = jnp.concatenate([btail[rowed, :]] * rows, axis=0)
        piece = jnp.where(own, piece, 0.0).astype(BF16)
        res = mm(piece, vbf[j])
        for i in range(rows):
            top = res[i * pair:i * pair + state]
            bottom = res[i * pair + state:(i + 1) * pair]
            fbuf[j * share + i // keep, i % keep] = jnp.where(first, top, bottom).astype(BF16)
        for j2, h, p in peers:
            if j2 is j:
                copy_to(fbuf.at[p], frecv.at[q], f_send, f_recv, r, base + p).start()
        for k in range(1, n_row):
            @pl.when(r < k)
            def _():
                down_value(j, k, r, k).start()

    @pl.when(c == 0)
    def _():
        copy_to(fbuf, precv, s_send, s_recv, r, c + 1).start()
        precv[...] = jnp.zeros_like(precv)

    frecv[q] = fbuf[q]
    drecv[q] = dj[mine_j]

    low = u_i <= t_i
    mask_a, mask_d = row_same & low, col_same & low
    lane_head = iota((T, hs), 1) // state
    zero_b = jnp.zeros((T, hs), BF16)
    b_a, c_a = sel_s[:, 0:hs], sel_s[:, hs:]
    cexp[...] = (c_a * per_state(jnp.exp(cum_ts[...])).T).astype(BF16)
    b_ab, c_ab, b_db, c_db = b_a.astype(BF16), c_a.astype(BF16), bd_s[...], cds[...]
    for k in range(heads):
        only = lane_head == k
        s_a = nt(c_ab, jnp.where(only, b_ab, zero_b))
        s_d = nt(c_db, jnp.where(only, b_db, zero_b))
        g_a = jnp.where(mask_a, cum_s[:, k:k + 1] - cum_ts[k:k + 1, :], -1e30)
        g_d = jnp.where(mask_d, cum_s[:, heads + k:heads + k + 1] - cum_ts[heads + k:heads + k + 1, :], -1e30)
        sc[k // 2, :, (k % 2) * T:(k % 2 + 1) * T] = (s_a * jnp.exp(g_a) + s_d * jnp.exp(g_d)).astype(BF16)

    def times_values(scores, v_tile):
        zero = jnp.zeros((T, 128), BF16)
        stacked = jnp.concatenate(
            [jnp.where(first, v_tile, zero), jnp.where(first, zero, v_tile)], axis=0
        )
        return mm(scores, stacked)

    others = pl.ds(0, G - 1)

    def whole(ref, send, recv):
        return copy_to(ref.at[others], ref.at[others], send, recv, r, c)

    whole(drecv, d_send, d_recv).wait_recv()
    logs = [drecv[e, pl.ds(i0, keep), :] for e in range(G)]
    tdec[...] = sum(logs)
    decays = [jnp.exp(v)[:, None, :] for v in logs]

    def total_decay(k):
        return copy_to(tdec, tdrecv.at[g], t_send.at[0, k - 1], t_recv.at[0, g], r, c + G * k)

    def total_state(k):
        return copy_to(tbuf, trecv.at[g], t_send.at[1, k - 1], t_recv.at[1, g], r, c + G * k)

    def later(k):
        return g + k < n_grp

    whole(frecv, f_send, f_recv).wait_recv()
    @pl.when(g < n_grp - 1)
    def _():
        pl.semaphore_wait(near.at[1], n_grp - 1 - g)

    carry = frecv[0].astype(F32)
    for e in range(1, G):
        carry = decays[e] * carry + frecv[e].astype(F32)
    tbuf[...] = carry.astype(BF16)
    for k in range(1, n_grp):
        @pl.when(later(k))
        def _():
            total_decay(k).start()
            total_state(k).start()

    gate[...] = silu(mm(norm_s[...], wi_ref[:, inner:]).astype(BF16).astype(F32))
    loads[10].wait()
    for j in range(nj):
        ln = slice(j * 128, (j + 1) * 128)
        acc[:, ln] = times_values(sc[j], vbf[j]) + sk_ref[:, ln] * vals[j]

    mine = (iota((T, rows * pair), 0) // cols) == (iota((T, rows * pair), 1) // pair)
    for j in range(nj):
        src = iota((hs, rows * pair), 0)
        dst = iota((hs, rows * pair), 1) % pair
        rep = (src == dst + j * pair).astype(BF16)
        maps[j] = jnp.where(mine, mm(cexp[...], rep), 0.0).astype(BF16)

    ibuf[...] = jnp.zeros_like(ibuf)
    for m in range(n_grp - 1):
        @pl.when(m < g)
        def _():
            copy_to(tdec, tdrecv.at[m], t_send.at[0, 0], t_recv.at[0, m], r, c).wait_recv()
            copy_to(tbuf, trecv.at[m], t_send.at[1, 0], t_recv.at[1, m], r, c).wait_recv()
            ibuf[...] = jnp.exp(tdrecv[m])[:, None, :] * ibuf[...] + trecv[m].astype(F32)
    carry = ibuf[...]
    for e in range(G):
        pbuf[e] = carry.astype(BF16)
        if e < G - 1:
            carry = decays[e] * carry + frecv[e].astype(F32)
    for j, h, p in peers:
        @pl.when(base + p > 1)
        def _():
            copy_to(pbuf.at[p], precv.at[q], p_send, p_recv, r, base + p).start()

    @pl.when(c > 1)
    def _():
        precv[q] = pbuf[q]

    for back in range(1, n_row):
        @pl.when(r >= back)
        def _():
            slot = r - back
            for cp in down_early(r, slot, 1):
                cp.wait_recv()
            down_values(slot, 1).wait_recv()
            gap = lrecv[slot, 0:heads]
            for nearer in range(1, back):
                gap = gap + lrecv[r - nearer, heads:]
            same = (iota((T, T), 0) % cols) == (iota((T, T), 1) % cols)
            for j in range(nj):
                parts = []
                for k in (2 * j, 2 * j + 1):
                    only = (iota((T, hs), 1) // state) == k
                    s_d = nt(cds[...], jnp.where(only, brecv[slot], jnp.zeros((T, hs), BF16)))
                    g_d = jnp.where(same, cum_s[:, heads + k:heads + k + 1] + gap[k:k + 1, :], -1e30)
                    parts.append((s_d * jnp.exp(g_d)).astype(BF16))
                ln = slice(j * 128, (j + 1) * 128)
                acc[:, ln] += times_values(jnp.concatenate(parts, axis=1), vrecv[slot, j])

    @pl.when(c == 1)
    def _():
        copy_to(fbuf, precv, s_send, s_recv, r, c).wait_recv()

    zero_s = jnp.zeros((state, 128), BF16)
    @pl.when(c > 1)
    def _():
        whole(precv, p_send, p_recv).wait_recv()

    for j in range(nj):
        ln = slice(j * 128, (j + 1) * 128)
        blocks = []
        for i in range(rows):
            s = precv[j * share + i // keep, i % keep]
            blocks += [jnp.where(first, s, zero_s), jnp.where(first, zero_s, s)]
        acc[:, ln] += mm(maps[j], jnp.concatenate(blocks, axis=0))

    loads[11].wait()
    loads[12].wait()
    mixed = acc[...] * gate[...]
    gated = norm(mixed, og_ref[...]).astype(BF16)
    result = mm(gated, wo_ref[...]) + tok_ref[...].astype(F32).reshape(T, D)
    out_ref[...] = result.astype(BF16).reshape(rows, cols, D)

    for n in (3, 5, 8):
        @pl.when(beside == n)
        def _():
            halos(n).wait_send()
    whole(drecv, d_send, d_recv).wait_send()
    whole(frecv, f_send, f_recv).wait_send()
    skipped = jnp.where(g > 0, 0, jnp.where(c > 1, 2, 1))
    for n in range(3):
        @pl.when(skipped == n)
        def _():
            some = pbuf.at[pl.ds(0, G - 1 - n)]
            copy_to(some, some, p_send, p_recv, r, c).wait_send()

    @pl.when(c == 0)
    def _():
        copy_to(fbuf, precv, s_send, s_recv, r, c).wait_send()
    for k in range(1, n_grp):
        @pl.when(later(k))
        def _():
            total_decay(k).wait_send()
            total_state(k).wait_send()
    for k in range(1, n_row):
        @pl.when(r < k)
        def _():
            for cp in down_early(r, 0, k):
                cp.wait_send()
            down_values(0, k).wait_send()


def solution(mesh):
    n_row, n_col = mesh.shape["row"], mesh.shape["col"]

    def on_device(
        tokens, norm_gain, w_inner, w_select, w_step, step_bias, rate_across, rate_down,
        conv_weight, conv_bias, skip_gain, out_gain, w_out,
    ):
        rows, cols, D = tokens.shape
        heads = rate_across.shape[0]
        inner = w_out.shape[0]
        hs = w_select.shape[1] // 4
        state = hs // heads
        T = rows * cols
        nj = inner // 128
        share, keep, G = split(nj, rows, n_col)
        n_grp = n_col // G
        dims = (n_row, n_col, rows, cols, heads, state, float(cols * n_col), float(rows * n_row))
        vm = pltpu.VMEM
        dma = pltpu.SemaphoreType.DMA
        operands = (
            tokens, norm_gain[None], w_inner, w_select, w_step.T, step_bias[None], rate_across[None],
            rate_down[None], conv_weight, conv_bias[None], skip_gain[None], out_gain[None], w_out,
        )
        operands = tuple(pltpu.with_memory_space_constraint(o, pltpu.HBM) for o in operands)
        return pl.pallas_call(
            functools.partial(kernel, dims),
            out_shape=jax.ShapeDtypeStruct(tokens.shape, tokens.dtype),
            in_specs=[pl.BlockSpec(memory_space=pltpu.HBM)] * 13,
            out_specs=pl.BlockSpec(memory_space=pltpu.VMEM),
            scratch_shapes=[vm(o.shape, o.dtype) for o in operands] + [dma((13,))] + [
                vm((8, cols, D), BF16), vm((2, cols, D), BF16),
                vm((rows + 2, cols + 16, inner), F32),
                vm((nj, T, 128), F32), vm((nj, T, 128), BF16), vm((T, hs), BF16),
                vm((2 * heads, T), F32), vm((nj, rows, 128), F32),
                vm((G, keep, state, 128), BF16), vm((G, rows, 128), F32), vm((G, keep, state, 128), BF16),
                vm((keep, state, 128), BF16), vm((keep, 128), F32),
                vm((n_grp, keep, state, 128), BF16), vm((n_grp, keep, 128), F32), vm((keep, state, 128), F32),
                vm((G, keep, state, 128), BF16), vm((G, keep, state, 128), BF16),
                vm((n_row, nj, T, 128), BF16), vm((n_row, T, hs), BF16), vm((n_row, 2 * heads, T), F32),
                vm((heads // 2, T, 2 * T), BF16), vm((T, inner), F32), vm((T, inner), F32),
                vm((T, hs), BF16), vm((T, hs), BF16), vm((T, 2 * heads), F32), vm((2 * heads, T), F32),
                vm((hs, T), F32), vm((T, 2 * hs), F32), vm((nj, T, rows * 2 * state), BF16),
                vm((nj, T, 128), F32), vm((2, rows + 16, inner), F32), vm((T, D), BF16),
                dma, dma, dma, dma, dma, dma,
                dma((2, max(n_grp - 1, 1))), dma((2, max(n_grp - 1, 1))), dma, dma,
                dma((3, n_row - 1)), dma((3, n_row - 1)), dma, dma, pltpu.SemaphoreType.REGULAR((2,)),
            ],
            compiler_params=pltpu.CompilerParams(
                collective_id=0, has_side_effects=True, vmem_limit_bytes=48 << 20
            ),
            name="block",
        )(*operands)

    placed = (P("row", "col", None),) + (P(),) * 12
    return jax.shard_map(
        on_device, mesh=mesh, in_specs=placed, out_specs=P("row", "col", None), check_vma=False
    )
```

```python
import functools
import jax
import jax.numpy as jnp
from jax import lax
from jax.experimental import pallas as pl
from jax.experimental.pallas import tpu as pltpu
from jax.sharding import PartitionSpec as P

MESH = pl.DeviceIdType.MESH
F32 = jnp.float32
BF16 = jnp.bfloat16
HI = lax.Precision.HIGHEST
epsilon = 1e-06


def iota(shape, dim):
    return lax.broadcasted_iota(jnp.int32, shape, dim)


def exact(a, b):
    return jnp.dot(a, b, precision=HI, preferred_element_type=F32)


def mm(a, b):
    return jnp.dot(a, b, preferred_element_type=F32)


def nt(a, b):
    return lax.dot_general(a, b, (((1,), (1,)), ((), ())), preferred_element_type=F32)


def norm(x, gain):
    return x * lax.rsqrt(jnp.mean(x * x, axis=-1, keepdims=True) + epsilon) * gain


def silu(v):
    return v * (1.0 / (1.0 + jnp.exp(-v)))


def softplus(x):
    return jnp.maximum(x, 0.0) + jnp.log1p(jnp.exp(-jnp.abs(x)))


def copy_to(src, dst, send, recv, row, col):
    return pltpu.make_async_remote_copy(
        src_ref=src, dst_ref=dst, send_sem=send, recv_sem=recv,
        device_id=(row, col), device_id_type=MESH,
    )


def split(nj, rows, n_col):
    share = 2 if n_col % (2 * nj) == 0 else 1
    return share, rows // share, nj * share


def kernel(
    dims,
    tok_ref, ng_ref, wi_ref, wsel_ref, wst_ref, sb_ref, ra_ref, rd_ref, cw_ref, cb_ref,
    sk_ref, og_ref, wo_ref,
    out_ref,
    tok_v, ng_v, wi_v, wsel_v, wst_v, sb_v, ra_v, rd_v, cw_v, cb_v, sk_v, og_v, wo_v, w_sem,
    hb, eb, xp, vals, vbf, bd_s, logs_s, dj, fbuf, drecv, frecv, tbuf, tdec, trecv, tdrecv, ibuf, pbuf, precv,
    vrecv, brecv, lrecv, sc, gate, acc, cexp, cds, cum_s, cum_ts, btail, sel_s, maps, pre, lh, norm_s,
    sent, h_recv, d_recv, f_recv, t_recv, p_recv, v_recv, s_recv, near,
):
    n_row, n_col, rows, cols, heads, state, full_w, height = dims
    T = rows * cols
    loads = [
        pltpu.make_async_copy(src, dst, w_sem.at[(0, 1, 2, 3, 1, 1, 1, 1, 4, 4, 4, 4, 5)[k]])
        for k, (src, dst) in enumerate((
            (tok_ref, tok_v), (ng_ref, ng_v), (wi_ref, wi_v), (wsel_ref, wsel_v), (wst_ref, wst_v),
            (sb_ref, sb_v), (ra_ref, ra_v), (rd_ref, rd_v), (cw_ref, cw_v), (cb_ref, cb_v),
            (sk_ref, sk_v), (og_ref, og_v), (wo_ref, wo_v),
        ))
    ]
    tok_ref, ng_ref, wi_ref, wsel_ref, wst_ref = tok_v, ng_v, wi_v, wsel_v, wst_v
    sb_ref, ra_ref, rd_ref, cw_ref, cb_ref = sb_v, ra_v, rd_v, cw_v, cb_v
    sk_ref, og_ref, wo_ref = sk_v, og_v, wo_v
    inner = wo_ref.shape[0]
    D = tok_ref.shape[2]
    nj = inner // 128
    share, keep, G = split(nj, rows, n_col)
    n_grp = n_col // G
    hs = heads * state
    nh = 2 * heads
    r = lax.axis_index("row")
    c = lax.axis_index("col")
    g, q = c // G, c % G
    mine_j, mine_h = q // share, q % share
    i0 = mine_h * keep
    if nj == 4:
        far = [3 - mine_j, (mine_j + 2) % 4, mine_j + 1 - 2 * (mine_j % 2), mine_j]
    else:
        far = [(mine_j + k) % nj for k in range(1, nj)] + [mine_j]
    peers = [(j, h, j * share + h) for j in far[:-1] for h in range(share)]
    peers += [(mine_j, h, mine_j * share + h) for h in [(mine_h + k) % share for k in range(1, share)]]
    base = g * G

    barrier = pltpu.get_barrier_semaphore()

    plan = (
        (4, 1, 1, eb.at[1]),
        (5, 1, -1, eb.at[0]),
        (6, -1, 1, eb.at[1]),
        (7, -1, -1, eb.at[0]),
        (0, 1, 0, tok_ref.at[rows - 1]),
        (1, -1, 0, tok_ref.at[0]),
        (2, 0, 1, eb.at[1]),
        (3, 0, -1, eb.at[0]),
    )

    def there(dr, dc):
        return (r + dr >= 0) & (r + dr < n_row) & (c + dc >= 0) & (c + dc < n_col)

    loads[0].start()
    hb[...] = jnp.zeros_like(hb)
    friends = [(dr, dc, there(dr, dc)) for _, dr, dc, _ in plan]
    friends += [(dr, 0, there(dr, 0)) for k in range(2, n_row) for dr in (k, -k)]
    ahead = [(0, dc, q + dc < G) for dc in range(2, G)] + [(0, G * k, g + k < n_grp) for k in range(1, n_grp)]
    for dr, dc, ok in friends + ahead:
        @pl.when(ok)
        def _():
            pl.semaphore_signal(barrier, inc=1, device_id=(r + dr, c + dc), device_id_type=MESH)
    for load in loads[1:]:
        load.start()
    eb[...] = jnp.zeros_like(eb)
    lh[...] = jnp.zeros_like(lh)
    for i in range(rows):
        xp[i + 1, 0:8, :] = jnp.zeros((8, inner), F32)
        xp[i + 1, 8 + cols:16 + cols, :] = jnp.zeros((8, inner), F32)

    loads[0].wait()
    eb[0, 0:rows, :] = tok_ref[:, 0, :]
    eb[1, 0:rows, :] = tok_ref[:, cols - 1, :]
    pl.semaphore_wait(barrier, sum(jnp.where(ok, 1, 0) for _, _, ok in friends) + jnp.maximum(q - 1, 0) + g)

    for slot, dr, dc, src in plan:
        @pl.when(there(dr, dc))
        def _():
            copy_to(src, hb.at[slot], sent, h_recv, r + dr, c + dc).start()

    for dc in range(2, G):
        @pl.when(q >= dc)
        def _():
            pl.semaphore_signal(near.at[0], inc=1, device_id=(r, c - dc), device_id_type=MESH)
    for k in range(1, n_grp):
        @pl.when(g >= k)
        def _():
            pl.semaphore_signal(near.at[1], inc=1, device_id=(r, c - G * k), device_id_type=MESH)

    for k in (1, 4, 5, 6, 7):
        loads[k].wait()
    x = tok_ref[...].astype(F32).reshape(T, D)
    normed = norm(x, ng_ref[...]).astype(BF16)
    norm_s[...] = normed
    loads[2].wait()
    main_x = mm(normed, wi_ref[:, :inner]).astype(BF16).astype(F32)
    for i in range(rows):
        xp[i + 1, 8:8 + cols, :] = main_x[i * cols:(i + 1) * cols]

    def column(row):
        width = row.shape[1]
        square = jnp.broadcast_to(row, (width, width))
        return jnp.sum(
            jnp.where(iota((width, width), 0) == iota((width, width), 1), square, 0.0), axis=1, keepdims=True
        )

    t_i, u_i = iota((T, T), 0), iota((T, T), 1)
    row_same = (t_i // cols) == (u_i // cols)
    col_same = (t_i % cols) == (u_i % cols)
    step_t = nt(wst_ref[...], normed)
    rate = jnp.concatenate([column(ra_ref[...]) / full_w, column(rd_ref[...]) / height], axis=0)
    logs_t = -softplus(step_t + column(sb_ref[...])) * rate

    def thirds(v):
        hi = v.astype(BF16)
        rest = v - hi.astype(F32)
        mid = rest.astype(BF16)
        return hi, mid, (rest - mid.astype(F32)).astype(BF16)

    up = t_i <= u_i
    sums = jnp.concatenate(
        [jnp.where(m, 1.0, 0.0).astype(BF16) for m in (row_same & up, row_same, col_same & up, col_same)], axis=1
    )
    parts = mm(jnp.concatenate(thirds(logs_t), axis=0), sums)
    summed = parts[:nh] + parts[nh:2 * nh] + parts[2 * nh:]
    cum_t = jnp.concatenate([summed[:heads, 0:T], summed[heads:, 2 * T:3 * T]], axis=0)
    tot_t = jnp.concatenate([summed[:heads, T:2 * T], summed[heads:, 3 * T:]], axis=0)
    logs_s[0:heads] = tot_t[heads:] - cum_t[heads:]
    logs_s[heads:] = tot_t[heads:]
    cum_ts[...] = cum_t
    cum = jnp.concatenate([cum_t, jnp.zeros((T - nh, T), F32)], axis=0).T[:, :nh]
    cum_s[...] = cum

    row_tot = jnp.concatenate([cum[(i + 1) * cols - 1:(i + 1) * cols] for i in range(rows)], axis=0)
    spread = jnp.where(iota((nh, inner), 0) == iota((nh, inner), 1) // (inner // heads), 1.0, 0.0).astype(BF16)
    wide = sum(mm(part, spread) for part in thirds(row_tot))
    for j in range(nj):
        dj[j] = wide[:, j * 128:(j + 1) * 128]

    def per_state(v):
        return jnp.concatenate([jnp.broadcast_to(v[k:k + 1], (state, T)) for k in range(heads)], axis=0)

    loads[3].wait()
    sel = mm(normed, wsel_ref[...])
    sel_s[...] = sel[:, :2 * hs]
    btail[...] = sel[:, :hs].T * per_state(jnp.exp(tot_t - cum_t))
    bd_s[...] = sel[:, 2 * hs:3 * hs].astype(BF16)
    cds[...] = sel[:, 3 * hs:].astype(BF16)

    def down_early(to_row, slot, dest):
        return (
            copy_to(bd_s, brecv.at[slot], sent, v_recv.at[1, slot], to_row, c),
            copy_to(logs_s, lrecv.at[slot], sent, v_recv.at[2, slot], to_row, c),
        )

    def down_values(to_row, slot, dest):
        return copy_to(vbf, vrecv.at[slot], sent, v_recv.at[0, slot], to_row, c)

    for k in range(1, n_row):
        @pl.when(r < k)
        def _():
            for cp in down_early(k, r, k):
                cp.start()

    for k in (8, 9, 10, 11):
        loads[k].wait()
    for j in range(nj):
        ln = slice(j * 128, (j + 1) * 128)
        w9 = [cw_ref[a, b:b + 1, ln] for a in range(3) for b in range(3)]
        bias = cb_ref[:, ln]
        for i in range(rows):
            total = jnp.zeros((cols, 128), F32) + bias
            for a in range(3):
                if 0 <= i + a - 1 < rows:
                    for b in range(3):
                        total = total + xp[i + a, 7 + b:7 + b + cols, ln] * w9[a * 3 + b]
            pre[j, i * cols:(i + 1) * cols] = total
            vals[j, i * cols:(i + 1) * cols] = silu(total)

    @pl.when(q < G - 2)
    def _():
        pl.semaphore_wait(near.at[0], G - 2 - q)

    for j, h, p in peers:
        copy_to(dj.at[j], drecv.at[q], sent, d_recv, r, base + p).start()

    beside = sum(jnp.where(there(dr, dc), 1, 0) for _, dr, dc, _ in plan)

    def halos(n):
        some = hb.at[pl.ds(0, n)]
        return copy_to(some, some, sent, h_recv, r, c)

    for n in (3, 5, 8):
        @pl.when(beside == n)
        def _():
            halos(n).wait_recv()
    edge = norm(hb[...].astype(F32).reshape(8 * cols, D), ng_ref[...]).astype(BF16)
    edge_x = mm(edge, wi_ref[:, :inner]).astype(BF16).astype(F32)
    xp[0, 8:8 + cols, :] = edge_x[0:cols]
    xp[rows + 1, 8:8 + cols, :] = edge_x[cols:2 * cols]
    lh[0, 8:8 + rows, :] = edge_x[2 * cols:2 * cols + rows]
    lh[1, 8:8 + rows, :] = edge_x[3 * cols:3 * cols + rows]
    xp[0, 7:8, :] = edge_x[4 * cols + rows - 1:4 * cols + rows]
    xp[0, 8 + cols:9 + cols, :] = edge_x[5 * cols + rows - 1:5 * cols + rows]
    xp[rows + 1, 7:8, :] = edge_x[6 * cols:6 * cols + 1]
    xp[rows + 1, 8 + cols:9 + cols, :] = edge_x[7 * cols:7 * cols + 1]

    first = iota((1, 128), 1) < 64
    pair = 2 * state
    own = (iota((rows * pair, T), 0) // pair) == (iota((rows * pair, T), 1) // cols)
    for j in range(nj):
        ln = slice(j * 128, (j + 1) * 128)
        for i, a, edge_row in ((0, 0, 0), (rows - 1, 2, rows + 1)):
            at = slice(i * cols, (i + 1) * cols)
            total = pre[j, at]
            for b in range(3):
                total = total + xp[edge_row, 7 + b:7 + b + cols, ln] * cw_ref[a, b:b + 1, ln]
            pre[j, at] = total
            vals[j, at] = silu(total)
        for e, at, b in ((0, 0, 0), (1, cols - 1, 2)):
            some = pl.ds(at, rows, stride=cols)
            total = pre[j, some, :]
            for a in range(3):
                total = total + lh[e, 7 + a:7 + a + rows, ln] * cw_ref[a, b:b + 1, ln]
            vals[j, some, :] = silu(total)
        vbf[j] = vals[j].astype(BF16)

        piece = jnp.concatenate([btail[j * pair:(j + 1) * pair, :]] * rows, axis=0)
        piece = jnp.where(own, piece, 0.0).astype(BF16)
        res = mm(piece, vbf[j])
        for i in range(rows):
            top = res[i * pair:i * pair + state]
            bottom = res[i * pair + state:(i + 1) * pair]
            fbuf[j * share + i // keep, i % keep] = jnp.where(first, top, bottom).astype(BF16)
    for _, _, p in peers:
        copy_to(fbuf.at[p], frecv.at[q], sent, f_recv, r, base + p).start()

    for k in range(1, n_row):
        @pl.when(r < k)
        def _():
            down_values(k, r, k).start()

    @pl.when(c == 0)
    def _():
        copy_to(fbuf, precv, sent, s_recv, r, c + 1).start()
        precv[...] = jnp.zeros_like(precv)

    frecv[q] = fbuf[q]
    drecv[q] = dj[mine_j]

    low = u_i <= t_i
    mask_a, mask_d = row_same & low, col_same & low
    lane_head = iota((T, hs), 1) // state
    zero_b = jnp.zeros((T, hs), BF16)
    b_a, c_a = sel_s[:, 0:hs], sel_s[:, hs:]
    cexp[...] = (c_a * per_state(jnp.exp(cum_ts[...])).T).astype(BF16)
    b_ab, c_ab, b_db, c_db = b_a.astype(BF16), c_a.astype(BF16), bd_s[...], cds[...]
    for k in range(heads):
        only = lane_head == k
        s_a = nt(c_ab, jnp.where(only, b_ab, zero_b))
        s_d = nt(c_db, jnp.where(only, b_db, zero_b))
        g_a = jnp.where(mask_a, cum_s[:, k:k + 1] - cum_ts[k:k + 1, :], -1e30)
        g_d = jnp.where(mask_d, cum_s[:, heads + k:heads + k + 1] - cum_ts[heads + k:heads + k + 1, :], -1e30)
        sc[k // 2, :, (k % 2) * T:(k % 2 + 1) * T] = (s_a * jnp.exp(g_a) + s_d * jnp.exp(g_d)).astype(BF16)

    def times_values(scores, v_tile):
        zero = jnp.zeros((T, 128), BF16)
        stacked = jnp.concatenate(
            [jnp.where(first, v_tile, zero), jnp.where(first, zero, v_tile)], axis=0
        )
        return mm(scores, stacked)

    others = pl.ds(0, G - 1)

    def whole(ref, send, recv):
        return copy_to(ref.at[others], ref.at[others], send, recv, r, c)

    whole(drecv, sent, d_recv).wait_recv()
    logs = [drecv[e, pl.ds(i0, keep), :] for e in range(G)]
    tdec[...] = sum(logs)
    decays = [jnp.exp(v)[:, None, :] for v in logs]

    def total_decay(k):
        return copy_to(tdec, tdrecv.at[g], sent, t_recv.at[0, g], r, c + G * k)

    def total_state(k):
        return copy_to(tbuf, trecv.at[g], sent, t_recv.at[1, g], r, c + G * k)

    def later(k):
        return g + k < n_grp

    whole(frecv, sent, f_recv).wait_recv()
    @pl.when(g < n_grp - 1)
    def _():
        pl.semaphore_wait(near.at[1], n_grp - 1 - g)

    carry = frecv[0].astype(F32)
    for e in range(1, G):
        carry = decays[e] * carry + frecv[e].astype(F32)
    tbuf[...] = carry.astype(BF16)
    for k in range(1, n_grp):
        @pl.when(later(k))
        def _():
            total_state(k).start()

        @pl.when(later(k) & (g > 0))
        def _():
            total_decay(k).start()

    gate[...] = silu(mm(norm_s[...], wi_ref[:, inner:]).astype(BF16).astype(F32))
    for j in range(nj):
        ln = slice(j * 128, (j + 1) * 128)
        acc[:, ln] = times_values(sc[j], vbf[j]) + sk_ref[:, ln] * vals[j]

    mine = (iota((T, rows * pair), 0) // cols) == (iota((T, rows * pair), 1) // pair)
    for j in range(nj):
        src = iota((hs, rows * pair), 0)
        dst = iota((hs, rows * pair), 1) % pair
        rep = (src == dst + j * pair).astype(BF16)
        maps[j] = jnp.where(mine, mm(cexp[...], rep), 0.0).astype(BF16)

    ibuf[...] = jnp.zeros_like(ibuf)
    for m in range(n_grp - 1):
        @pl.when(m < g)
        def _():
            if m:
                copy_to(tdec, tdrecv.at[m], sent, t_recv.at[0, m], r, c).wait_recv()
            copy_to(tbuf, trecv.at[m], sent, t_recv.at[1, m], r, c).wait_recv()
            if m:
                ibuf[...] = jnp.exp(tdrecv[m])[:, None, :] * ibuf[...] + trecv[m].astype(F32)
            else:
                ibuf[...] = trecv[m].astype(F32)
    carry = ibuf[...]
    for e in range(G):
        pbuf[e] = carry.astype(BF16)
        if e < G - 1:
            carry = decays[e] * carry + frecv[e].astype(F32)
    for j, h, p in peers:
        @pl.when(base + p > 1)
        def _():
            copy_to(pbuf.at[p], precv.at[q], sent, p_recv, r, base + p).start()

    @pl.when(c > 1)
    def _():
        precv[q] = pbuf[q]

    for back in range(1, n_row):
        @pl.when(r >= back)
        def _():
            slot = r - back
            for cp in down_early(r, slot, 1):
                cp.wait_recv()
            down_values(r, slot, 1).wait_recv()
            gap = lrecv[slot, 0:heads]
            for nearer in range(1, back):
                gap = gap + lrecv[r - nearer, heads:]
            same = (iota((T, T), 0) % cols) == (iota((T, T), 1) % cols)
            for j in range(nj):
                parts = []
                for k in (2 * j, 2 * j + 1):
                    only = (iota((T, hs), 1) // state) == k
                    s_d = nt(cds[...], jnp.where(only, brecv[slot], jnp.zeros((T, hs), BF16)))
                    g_d = jnp.where(same, cum_s[:, heads + k:heads + k + 1] + gap[k:k + 1, :], -1e30)
                    parts.append((s_d * jnp.exp(g_d)).astype(BF16))
                ln = slice(j * 128, (j + 1) * 128)
                acc[:, ln] += times_values(jnp.concatenate(parts, axis=1), vrecv[slot, j])

    @pl.when(c == 1)
    def _():
        copy_to(fbuf, precv, sent, s_recv, r, c).wait_recv()

    zero_s = jnp.zeros((state, 128), BF16)
    @pl.when(c > 1)
    def _():
        whole(precv, sent, p_recv).wait_recv()

    for j in range(nj):
        ln = slice(j * 128, (j + 1) * 128)
        blocks = []
        for i in range(rows):
            s = precv[j * share + i // keep, i % keep]
            blocks += [jnp.where(first, s, zero_s), jnp.where(first, zero_s, s)]
        acc[:, ln] += mm(maps[j], jnp.concatenate(blocks, axis=0))

    loads[12].wait()
    mixed = acc[...] * gate[...]
    gated = norm(mixed, og_ref[...]).astype(BF16)
    result = mm(gated, wo_ref[...]) + tok_ref[...].astype(F32).reshape(T, D)
    out_ref[...] = result.astype(BF16).reshape(rows, cols, D)

    for n in (3, 5, 8):
        @pl.when(beside == n)
        def _():
            halos(n).wait_send()
    whole(drecv, sent, d_recv).wait_send()
    whole(frecv, sent, f_recv).wait_send()
    skipped = jnp.where(g > 0, 0, jnp.where(c > 1, 2, 1))
    for n in range(3):
        @pl.when(skipped == n)
        def _():
            some = pbuf.at[pl.ds(0, G - 1 - n)]
            copy_to(some, some, sent, p_recv, r, c).wait_send()

    @pl.when(c == 0)
    def _():
        copy_to(fbuf, precv, sent, s_recv, r, c).wait_send()
    for k in range(1, n_grp):
        @pl.when(later(k))
        def _():
            total_state(k).wait_send()

        @pl.when(later(k) & (g > 0))
        def _():
            total_decay(k).wait_send()
    for k in range(1, n_row):
        @pl.when(r < k)
        def _():
            for cp in down_early(r, 0, k):
                cp.wait_send()
            down_values(r, 0, k).wait_send()


def solution(mesh):
    n_row, n_col = mesh.shape["row"], mesh.shape["col"]

    def on_device(
        tokens, norm_gain, w_inner, w_select, w_step, step_bias, rate_across, rate_down,
        conv_weight, conv_bias, skip_gain, out_gain, w_out,
    ):
        rows, cols, D = tokens.shape
        heads = rate_across.shape[0]
        inner = w_out.shape[0]
        hs = w_select.shape[1] // 4
        state = hs // heads
        T = rows * cols
        nj = inner // 128
        share, keep, G = split(nj, rows, n_col)
        n_grp = n_col // G
        dims = (n_row, n_col, rows, cols, heads, state, float(cols * n_col), float(rows * n_row))
        vm = pltpu.VMEM
        dma = pltpu.SemaphoreType.DMA
        operands = (
            tokens, norm_gain[None], w_inner, w_select, w_step.T, step_bias[None], rate_across[None],
            rate_down[None], conv_weight, conv_bias[None], skip_gain[None], out_gain[None], w_out,
        )
        operands = tuple(pltpu.with_memory_space_constraint(o, pltpu.HBM) for o in operands)
        return pl.pallas_call(
            functools.partial(kernel, dims),
            out_shape=jax.ShapeDtypeStruct(tokens.shape, tokens.dtype),
            in_specs=[pl.BlockSpec(memory_space=pltpu.HBM)] * 13,
            out_specs=pl.BlockSpec(memory_space=pltpu.VMEM),
            scratch_shapes=[vm(o.shape, o.dtype) for o in operands] + [dma((6,))] + [
                vm((8, cols, D), BF16), vm((2, cols, D), BF16),
                vm((rows + 2, cols + 16, inner), F32),
                vm((nj, T, 128), F32), vm((nj, T, 128), BF16), vm((T, hs), BF16),
                vm((2 * heads, T), F32), vm((nj, rows, 128), F32),
                vm((G, keep, state, 128), BF16), vm((G, rows, 128), F32), vm((G, keep, state, 128), BF16),
                vm((keep, state, 128), BF16), vm((keep, 128), F32),
                vm((n_grp, keep, state, 128), BF16), vm((n_grp, keep, 128), F32), vm((keep, state, 128), F32),
                vm((G, keep, state, 128), BF16), vm((G, keep, state, 128), BF16),
                vm((n_row, nj, T, 128), BF16), vm((n_row, T, hs), BF16), vm((n_row, 2 * heads, T), F32),
                vm((heads // 2, T, 2 * T), BF16), vm((T, inner), F32), vm((T, inner), F32),
                vm((T, hs), BF16), vm((T, hs), BF16), vm((T, 2 * heads), F32), vm((2 * heads, T), F32),
                vm((hs, T), F32), vm((T, 2 * hs), F32), vm((nj, T, rows * 2 * state), BF16),
                vm((nj, T, 128), F32), vm((2, rows + 16, inner), F32), vm((T, D), BF16),
                dma, dma, dma, dma, dma((2, max(n_grp - 1, 1))), dma, dma((3, n_row - 1)), dma, pltpu.SemaphoreType.REGULAR((2,)),
            ],
            compiler_params=pltpu.CompilerParams(
                collective_id=0, has_side_effects=True, vmem_limit_bytes=48 << 20
            ),
            name="block",
        )(*operands)

    placed = (P("row", "col", None),) + (P(),) * 12
    return jax.shard_map(
        on_device, mesh=mesh, in_specs=placed, out_specs=P("row", "col", None), check_vma=False
    )
```

```python
import functools
import jax
import jax.numpy as jnp
from jax import lax
from jax.experimental import pallas as pl
from jax.experimental.pallas import tpu as pltpu
from jax.sharding import PartitionSpec as P

MESH = pl.DeviceIdType.MESH
F32 = jnp.float32
BF16 = jnp.bfloat16
HI = lax.Precision.HIGHEST
epsilon = 1e-06


def iota(shape, dim):
    return lax.broadcasted_iota(jnp.int32, shape, dim)


def exact(a, b):
    return jnp.dot(a, b, precision=HI, preferred_element_type=F32)


def mm(a, b):
    return jnp.dot(a, b, preferred_element_type=F32)


def nt(a, b):
    return lax.dot_general(a, b, (((1,), (1,)), ((), ())), preferred_element_type=F32)


def norm(x, gain):
    return x * lax.rsqrt(jnp.mean(x * x, axis=-1, keepdims=True) + epsilon) * gain


def silu(v):
    return v * (1.0 / (1.0 + jnp.exp(-v)))


def softplus(x):
    return jnp.maximum(x, 0.0) + jnp.log1p(jnp.exp(-jnp.abs(x)))


def copy_to(src, dst, send, recv, row, col):
    return pltpu.make_async_remote_copy(
        src_ref=src, dst_ref=dst, send_sem=send, recv_sem=recv,
        device_id=(row, col), device_id_type=MESH,
    )


def split(nj, rows, n_col):
    share = 2 if n_col % (2 * nj) == 0 else 1
    return share, rows // share, nj * share


def kernel(
    dims,
    tok_ref, ng_ref, wi_ref, wsel_ref, wst_ref, sb_ref, ra_ref, rd_ref, cw_ref, cb_ref,
    sk_ref, og_ref, wo_ref,
    out_ref,
    tok_v, ng_v, wi_v, wsel_v, wst_v, sb_v, ra_v, rd_v, cw_v, cb_v, sk_v, og_v, wo_v, w_sem,
    hb, eb, xp, vals, vbf, bd_s, logs_s, dj, fbuf, drecv, frecv, tbuf, tdec, trecv, tdrecv, ibuf, pbuf, precv,
    vrecv, brecv, lrecv, sc, gate, acc, cexp, cds, cum_s, cum_ts, btail, sel_s, maps, pre, lh, norm_s,
    sent, h_recv, d_recv, f_recv, t_recv, p_recv, v_recv, s_recv, near,
):
    n_row, n_col, rows, cols, heads, state, full_w, height = dims
    T = rows * cols
    loads = [
        pltpu.make_async_copy(src, dst, w_sem.at[(0, 1, 2, 3, 1, 1, 1, 1, 4, 4, 4, 4, 5)[k]])
        for k, (src, dst) in enumerate((
            (tok_ref, tok_v), (ng_ref, ng_v), (wi_ref, wi_v), (wsel_ref, wsel_v), (wst_ref, wst_v),
            (sb_ref, sb_v), (ra_ref, ra_v), (rd_ref, rd_v), (cw_ref, cw_v), (cb_ref, cb_v),
            (sk_ref, sk_v), (og_ref, og_v), (wo_ref, wo_v),
        ))
    ]
    tok_ref, ng_ref, wi_ref, wsel_ref, wst_ref = tok_v, ng_v, wi_v, wsel_v, wst_v
    sb_ref, ra_ref, rd_ref, cw_ref, cb_ref = sb_v, ra_v, rd_v, cw_v, cb_v
    sk_ref, og_ref, wo_ref = sk_v, og_v, wo_v
    inner = wo_ref.shape[0]
    D = tok_ref.shape[2]
    nj = inner // 128
    share, keep, G = split(nj, rows, n_col)
    n_grp = n_col // G
    hs = heads * state
    nh = 2 * heads
    r = lax.axis_index("row")
    c = lax.axis_index("col")
    g, q = c // G, c % G
    mine_j, mine_h = q // share, q % share
    i0 = mine_h * keep
    if nj == 4:
        far = [3 - mine_j, (mine_j + 2) % 4, mine_j + 1 - 2 * (mine_j % 2), mine_j]
    else:
        far = [(mine_j + k) % nj for k in range(1, nj)] + [mine_j]
    peers = [(j, h, j * share + h) for j in far[:-1] for h in range(share)]
    peers += [(mine_j, h, mine_j * share + h) for h in [(mine_h + k) % share for k in range(1, share)]]
    if len(peers) == 7:
        peers = [peers[k] for k in (0, 2, 1, 3, 4, 5, 6)]
    base = g * G

    barrier = pltpu.get_barrier_semaphore()

    plan = (
        (4, 1, 1, eb.at[1]),
        (5, 1, -1, eb.at[0]),
        (6, -1, 1, eb.at[1]),
        (7, -1, -1, eb.at[0]),
        (0, 1, 0, tok_ref.at[rows - 1]),
        (1, -1, 0, tok_ref.at[0]),
        (2, 0, 1, eb.at[1]),
        (3, 0, -1, eb.at[0]),
    )

    def there(dr, dc):
        return (r + dr >= 0) & (r + dr < n_row) & (c + dc >= 0) & (c + dc < n_col)

    loads[0].start()
    hb[...] = jnp.zeros_like(hb)
    friends = [(dr, dc, there(dr, dc)) for _, dr, dc, _ in plan]
    friends += [(dr, 0, there(dr, 0)) for k in range(2, n_row) for dr in (k, -k)]
    ahead = [(0, dc, q + dc < G) for dc in range(2, G)] + [(0, G * k, g + k < n_grp) for k in range(1, n_grp)]
    for dr, dc, ok in friends + ahead:
        @pl.when(ok)
        def _():
            pl.semaphore_signal(barrier, inc=1, device_id=(r + dr, c + dc), device_id_type=MESH)
    for load in loads[1:]:
        load.start()
    eb[...] = jnp.zeros_like(eb)
    lh[...] = jnp.zeros_like(lh)
    for i in range(rows):
        xp[i + 1, 0:8, :] = jnp.zeros((8, inner), F32)
        xp[i + 1, 8 + cols:16 + cols, :] = jnp.zeros((8, inner), F32)

    loads[0].wait()
    eb[0, 0:rows, :] = tok_ref[:, 0, :]
    eb[1, 0:rows, :] = tok_ref[:, cols - 1, :]
    pl.semaphore_wait(barrier, sum(jnp.where(ok, 1, 0) for _, _, ok in friends) + jnp.maximum(q - 1, 0) + g)

    for slot, dr, dc, src in plan:
        @pl.when(there(dr, dc))
        def _():
            copy_to(src, hb.at[slot], sent, h_recv, r + dr, c + dc).start()

    for dc in range(2, G):
        @pl.when(q >= dc)
        def _():
            pl.semaphore_signal(near.at[0], inc=1, device_id=(r, c - dc), device_id_type=MESH)
    for k in range(1, n_grp):
        @pl.when(g >= k)
        def _():
            pl.semaphore_signal(near.at[1], inc=1, device_id=(r, c - G * k), device_id_type=MESH)

    for k in (1, 4, 5, 6, 7):
        loads[k].wait()
    x = tok_ref[...].astype(F32).reshape(T, D)
    normed = norm(x, ng_ref[...]).astype(BF16)
    norm_s[...] = normed
    loads[2].wait()
    main_x = mm(normed, wi_ref[:, :inner]).astype(BF16).astype(F32)
    for i in range(rows):
        xp[i + 1, 8:8 + cols, :] = main_x[i * cols:(i + 1) * cols]

    def column(row):
        width = row.shape[1]
        square = jnp.broadcast_to(row, (width, width))
        return jnp.sum(
            jnp.where(iota((width, width), 0) == iota((width, width), 1), square, 0.0), axis=1, keepdims=True
        )

    t_i, u_i = iota((T, T), 0), iota((T, T), 1)
    row_same = (t_i // cols) == (u_i // cols)
    col_same = (t_i % cols) == (u_i % cols)
    step_t = nt(wst_ref[...], normed)
    rate = jnp.concatenate([column(ra_ref[...]) / full_w, column(rd_ref[...]) / height], axis=0)
    logs_t = -softplus(step_t + column(sb_ref[...])) * rate

    def thirds(v):
        hi = v.astype(BF16)
        rest = v - hi.astype(F32)
        mid = rest.astype(BF16)
        return hi, mid, (rest - mid.astype(F32)).astype(BF16)

    up = t_i <= u_i
    sums = jnp.concatenate(
        [jnp.where(m, 1.0, 0.0).astype(BF16) for m in (row_same & up, row_same, col_same & up, col_same)], axis=1
    )
    parts = mm(jnp.concatenate(thirds(logs_t), axis=0), sums)
    summed = parts[:nh] + parts[nh:2 * nh] + parts[2 * nh:]
    cum_t = jnp.concatenate([summed[:heads, 0:T], summed[heads:, 2 * T:3 * T]], axis=0)
    tot_t = jnp.concatenate([summed[:heads, T:2 * T], summed[heads:, 3 * T:]], axis=0)
    logs_s[0:heads] = tot_t[heads:] - cum_t[heads:]
    logs_s[heads:] = tot_t[heads:]
    cum_ts[...] = cum_t
    cum = jnp.concatenate([cum_t, jnp.zeros((T - nh, T), F32)], axis=0).T[:, :nh]
    cum_s[...] = cum

    row_tot = jnp.concatenate([cum[(i + 1) * cols - 1:(i + 1) * cols] for i in range(rows)], axis=0)
    spread = jnp.where(iota((nh, inner), 0) == iota((nh, inner), 1) // (inner // heads), 1.0, 0.0).astype(BF16)
    wide = sum(mm(part, spread) for part in thirds(row_tot))
    for j in range(nj):
        dj[j] = wide[:, j * 128:(j + 1) * 128]

    def per_state(v):
        return jnp.concatenate([jnp.broadcast_to(v[k:k + 1], (state, T)) for k in range(heads)], axis=0)

    loads[3].wait()
    sel = mm(normed, wsel_ref[...])
    sel_s[...] = sel[:, :2 * hs]
    btail[...] = sel[:, :hs].T * per_state(jnp.exp(tot_t - cum_t))
    bd_s[...] = sel[:, 2 * hs:3 * hs].astype(BF16)
    cds[...] = sel[:, 3 * hs:].astype(BF16)

    def down_early(to_row, slot, dest):
        return (
            copy_to(bd_s, brecv.at[slot], sent, v_recv.at[1, slot], to_row, c),
            copy_to(logs_s, lrecv.at[slot], sent, v_recv.at[2, slot], to_row, c),
        )

    def down_values(to_row, slot, dest):
        return copy_to(vbf, vrecv.at[slot], sent, v_recv.at[0, slot], to_row, c)

    for k in range(1, n_row):
        @pl.when(r < k)
        def _():
            for cp in down_early(k, r, k):
                cp.start()

    for k in (8, 9, 10, 11):
        loads[k].wait()
    for j in range(nj):
        ln = slice(j * 128, (j + 1) * 128)
        w9 = [cw_ref[a, b:b + 1, ln] for a in range(3) for b in range(3)]
        bias = cb_ref[:, ln]
        for i in range(rows):
            total = jnp.zeros((cols, 128), F32) + bias
            for a in range(3):
                if 0 <= i + a - 1 < rows:
                    for b in range(3):
                        total = total + xp[i + a, 7 + b:7 + b + cols, ln] * w9[a * 3 + b]
            pre[j, i * cols:(i + 1) * cols] = total
            vals[j, i * cols:(i + 1) * cols] = silu(total)

    @pl.when(q < G - 2)
    def _():
        pl.semaphore_wait(near.at[0], G - 2 - q)

    for j, h, p in peers:
        copy_to(dj.at[j], drecv.at[q], sent, d_recv, r, base + p).start()

    beside = sum(jnp.where(there(dr, dc), 1, 0) for _, dr, dc, _ in plan)

    def halos(n):
        some = hb.at[pl.ds(0, n)]
        return copy_to(some, some, sent, h_recv, r, c)

    for n in (3, 5, 8):
        @pl.when(beside == n)
        def _():
            halos(n).wait_recv()
    edge = norm(hb[...].astype(F32).reshape(8 * cols, D), ng_ref[...]).astype(BF16)
    edge_x = mm(edge, wi_ref[:, :inner]).astype(BF16).astype(F32)
    xp[0, 8:8 + cols, :] = edge_x[0:cols]
    xp[rows + 1, 8:8 + cols, :] = edge_x[cols:2 * cols]
    lh[0, 8:8 + rows, :] = edge_x[2 * cols:2 * cols + rows]
    lh[1, 8:8 + rows, :] = edge_x[3 * cols:3 * cols + rows]
    xp[0, 7:8, :] = edge_x[4 * cols + rows - 1:4 * cols + rows]
    xp[0, 8 + cols:9 + cols, :] = edge_x[5 * cols + rows - 1:5 * cols + rows]
    xp[rows + 1, 7:8, :] = edge_x[6 * cols:6 * cols + 1]
    xp[rows + 1, 8 + cols:9 + cols, :] = edge_x[7 * cols:7 * cols + 1]

    first = iota((1, 128), 1) < 64
    pair = 2 * state
    own = (iota((rows * pair, T), 0) // pair) == (iota((rows * pair, T), 1) // cols)
    for j in range(nj):
        ln = slice(j * 128, (j + 1) * 128)
        for i, a, edge_row in ((0, 0, 0), (rows - 1, 2, rows + 1)):
            at = slice(i * cols, (i + 1) * cols)
            total = pre[j, at]
            for b in range(3):
                total = total + xp[edge_row, 7 + b:7 + b + cols, ln] * cw_ref[a, b:b + 1, ln]
            pre[j, at] = total
            vals[j, at] = silu(total)
        for e, at, b in ((0, 0, 0), (1, cols - 1, 2)):
            some = pl.ds(at, rows, stride=cols)
            total = pre[j, some, :]
            for a in range(3):
                total = total + lh[e, 7 + a:7 + a + rows, ln] * cw_ref[a, b:b + 1, ln]
            vals[j, some, :] = silu(total)
        vbf[j] = vals[j].astype(BF16)

        piece = jnp.concatenate([btail[j * pair:(j + 1) * pair, :]] * rows, axis=0)
        piece = jnp.where(own, piece, 0.0).astype(BF16)
        res = mm(piece, vbf[j])
        for i in range(rows):
            top = res[i * pair:i * pair + state]
            bottom = res[i * pair + state:(i + 1) * pair]
            fbuf[j * share + i // keep, i % keep] = jnp.where(first, top, bottom).astype(BF16)
    for _, _, p in peers:
        copy_to(fbuf.at[p], frecv.at[q], sent, f_recv, r, base + p).start()

    for k in range(1, n_row):
        @pl.when(r < k)
        def _():
            down_values(k, r, k).start()

    @pl.when(c == 0)
    def _():
        copy_to(fbuf, precv, sent, s_recv, r, c + 1).start()
        precv[...] = jnp.zeros_like(precv)

    frecv[q] = fbuf[q]
    drecv[q] = dj[mine_j]

    low = u_i <= t_i
    mask_a, mask_d = row_same & low, col_same & low
    lane_head = iota((T, hs), 1) // state
    zero_b = jnp.zeros((T, hs), BF16)
    b_a, c_a = sel_s[:, 0:hs], sel_s[:, hs:]
    cexp[...] = (c_a * per_state(jnp.exp(cum_ts[...])).T).astype(BF16)
    b_ab, c_ab, b_db, c_db = b_a.astype(BF16), c_a.astype(BF16), bd_s[...], cds[...]
    for k in range(heads):
        only = lane_head == k
        s_a = nt(c_ab, jnp.where(only, b_ab, zero_b))
        s_d = nt(c_db, jnp.where(only, b_db, zero_b))
        g_a = jnp.where(mask_a, cum_s[:, k:k + 1] - cum_ts[k:k + 1, :], -1e30)
        g_d = jnp.where(mask_d, cum_s[:, heads + k:heads + k + 1] - cum_ts[heads + k:heads + k + 1, :], -1e30)
        sc[k // 2, :, (k % 2) * T:(k % 2 + 1) * T] = (s_a * jnp.exp(g_a) + s_d * jnp.exp(g_d)).astype(BF16)

    def times_values(scores, v_tile):
        zero = jnp.zeros((T, 128), BF16)
        stacked = jnp.concatenate(
            [jnp.where(first, v_tile, zero), jnp.where(first, zero, v_tile)], axis=0
        )
        return mm(scores, stacked)

    others = pl.ds(0, G - 1)

    def whole(ref, send, recv):
        return copy_to(ref.at[others], ref.at[others], send, recv, r, c)

    whole(drecv, sent, d_recv).wait_recv()
    logs = [drecv[e, pl.ds(i0, keep), :] for e in range(G)]
    tdec[...] = sum(logs)
    decays = [jnp.exp(v)[:, None, :] for v in logs]

    def total_decay(k):
        return copy_to(tdec, tdrecv.at[g], sent, t_recv.at[0, g], r, c + G * k)

    def total_state(k):
        return copy_to(tbuf, trecv.at[g], sent, t_recv.at[1, g], r, c + G * k)

    def later(k):
        return g + k < n_grp

    whole(frecv, sent, f_recv).wait_recv()
    @pl.when(g < n_grp - 1)
    def _():
        pl.semaphore_wait(near.at[1], n_grp - 1 - g)

    carry = frecv[0].astype(F32)
    for e in range(1, G):
        carry = decays[e] * carry + frecv[e].astype(F32)
    tbuf[...] = carry.astype(BF16)
    for k in range(1, n_grp):
        @pl.when(later(k))
        def _():
            total_state(k).start()

        @pl.when(later(k) & (g > 0))
        def _():
            total_decay(k).start()

    gate[...] = silu(mm(norm_s[...], wi_ref[:, inner:]).astype(BF16).astype(F32))
    for j in range(nj):
        ln = slice(j * 128, (j + 1) * 128)
        acc[:, ln] = times_values(sc[j], vbf[j]) + sk_ref[:, ln] * vals[j]

    mine = (iota((T, rows * pair), 0) // cols) == (iota((T, rows * pair), 1) // pair)
    for j in range(nj):
        src = iota((hs, rows * pair), 0)
        dst = iota((hs, rows * pair), 1) % pair
        rep = (src == dst + j * pair).astype(BF16)
        maps[j] = jnp.where(mine, mm(cexp[...], rep), 0.0).astype(BF16)

    ibuf[...] = jnp.zeros_like(ibuf)
    for m in range(n_grp - 1):
        @pl.when(m < g)
        def _():
            if m:
                copy_to(tdec, tdrecv.at[m], sent, t_recv.at[0, m], r, c).wait_recv()
            copy_to(tbuf, trecv.at[m], sent, t_recv.at[1, m], r, c).wait_recv()
            if m:
                ibuf[...] = jnp.exp(tdrecv[m])[:, None, :] * ibuf[...] + trecv[m].astype(F32)
            else:
                ibuf[...] = trecv[m].astype(F32)
    carry = ibuf[...]
    for e in range(G):
        pbuf[e] = carry.astype(BF16)
        if e < G - 1:
            carry = decays[e] * carry + frecv[e].astype(F32)
    for j, h, p in peers:
        @pl.when(base + p > 1)
        def _():
            copy_to(pbuf.at[p], precv.at[q], sent, p_recv, r, base + p).start()

    @pl.when(c > 1)
    def _():
        precv[q] = pbuf[q]

    for back in range(1, n_row):
        @pl.when(r >= back)
        def _():
            slot = r - back
            for cp in down_early(r, slot, 1):
                cp.wait_recv()
            down_values(r, slot, 1).wait_recv()
            gap = lrecv[slot, 0:heads]
            for nearer in range(1, back):
                gap = gap + lrecv[r - nearer, heads:]
            same = (iota((T, T), 0) % cols) == (iota((T, T), 1) % cols)
            for j in range(nj):
                parts = []
                for k in (2 * j, 2 * j + 1):
                    only = (iota((T, hs), 1) // state) == k
                    s_d = nt(cds[...], jnp.where(only, brecv[slot], jnp.zeros((T, hs), BF16)))
                    g_d = jnp.where(same, cum_s[:, heads + k:heads + k + 1] + gap[k:k + 1, :], -1e30)
                    parts.append((s_d * jnp.exp(g_d)).astype(BF16))
                ln = slice(j * 128, (j + 1) * 128)
                acc[:, ln] += times_values(jnp.concatenate(parts, axis=1), vrecv[slot, j])

    for n in (3, 5, 8):
        @pl.when(beside == n)
        def _():
            halos(n).wait_send()
    whole(drecv, sent, d_recv).wait_send()
    whole(frecv, sent, f_recv).wait_send()
    @pl.when(c == 0)
    def _():
        copy_to(fbuf, precv, sent, s_recv, r, c).wait_send()
    for k in range(1, n_grp):
        @pl.when(later(k))
        def _():
            total_state(k).wait_send()

        @pl.when(later(k) & (g > 0))
        def _():
            total_decay(k).wait_send()
    for k in range(1, n_row):
        @pl.when(r < k)
        def _():
            for cp in down_early(r, 0, k):
                cp.wait_send()
            down_values(r, 0, k).wait_send()

    @pl.when(c == 1)
    def _():
        copy_to(fbuf, precv, sent, s_recv, r, c).wait_recv()

    tiles = []
    zero_s = jnp.zeros((state, 128), BF16)
    @pl.when(c > 1)
    def _():
        whole(precv, sent, p_recv).wait_recv()

    for j in range(nj):
        ln = slice(j * 128, (j + 1) * 128)
        blocks = []
        for i in range(rows):
            s = precv[j * share + i // keep, i % keep]
            blocks += [jnp.where(first, s, zero_s), jnp.where(first, zero_s, s)]
        tiles.append((acc[:, ln] + mm(maps[j], jnp.concatenate(blocks, axis=0))) * gate[:, ln])

    loads[12].wait()
    mixed = jnp.concatenate(tiles, axis=1)
    gated = norm(mixed, og_ref[...]).astype(BF16)
    result = mm(gated, wo_ref[...]) + tok_ref[...].astype(F32).reshape(T, D)
    out_ref[...] = result.astype(BF16).reshape(rows, cols, D)

    skipped = jnp.where(g > 0, 0, jnp.where(c > 1, 2, 1))
    for n in range(3):
        @pl.when(skipped == n)
        def _():
            some = pbuf.at[pl.ds(0, G - 1 - n)]
            copy_to(some, some, sent, p_recv, r, c).wait_send()


def solution(mesh):
    n_row, n_col = mesh.shape["row"], mesh.shape["col"]

    def on_device(
        tokens, norm_gain, w_inner, w_select, w_step, step_bias, rate_across, rate_down,
        conv_weight, conv_bias, skip_gain, out_gain, w_out,
    ):
        rows, cols, D = tokens.shape
        heads = rate_across.shape[0]
        inner = w_out.shape[0]
        hs = w_select.shape[1] // 4
        state = hs // heads
        T = rows * cols
        nj = inner // 128
        share, keep, G = split(nj, rows, n_col)
        n_grp = n_col // G
        dims = (n_row, n_col, rows, cols, heads, state, float(cols * n_col), float(rows * n_row))
        vm = pltpu.VMEM
        dma = pltpu.SemaphoreType.DMA
        operands = (
            tokens, norm_gain[None], w_inner, w_select, w_step.T, step_bias[None], rate_across[None],
            rate_down[None], conv_weight, conv_bias[None], skip_gain[None], out_gain[None], w_out,
        )
        operands = tuple(pltpu.with_memory_space_constraint(o, pltpu.HBM) for o in operands)
        return pl.pallas_call(
            functools.partial(kernel, dims),
            out_shape=jax.ShapeDtypeStruct(tokens.shape, tokens.dtype),
            in_specs=[pl.BlockSpec(memory_space=pltpu.HBM)] * 13,
            out_specs=pl.BlockSpec(memory_space=pltpu.VMEM),
            scratch_shapes=[vm(o.shape, o.dtype) for o in operands] + [dma((6,))] + [
                vm((8, cols, D), BF16), vm((2, cols, D), BF16),
                vm((rows + 2, cols + 16, inner), F32),
                vm((nj, T, 128), F32), vm((nj, T, 128), BF16), vm((T, hs), BF16),
                vm((2 * heads, T), F32), vm((nj, rows, 128), F32),
                vm((G, keep, state, 128), BF16), vm((G, rows, 128), F32), vm((G, keep, state, 128), BF16),
                vm((keep, state, 128), BF16), vm((keep, 128), F32),
                vm((n_grp, keep, state, 128), BF16), vm((n_grp, keep, 128), F32), vm((keep, state, 128), F32),
                vm((G, keep, state, 128), BF16), vm((G, keep, state, 128), BF16),
                vm((n_row, nj, T, 128), BF16), vm((n_row, T, hs), BF16), vm((n_row, 2 * heads, T), F32),
                vm((heads // 2, T, 2 * T), BF16), vm((T, inner), F32), vm((T, inner), F32),
                vm((T, hs), BF16), vm((T, hs), BF16), vm((T, 2 * heads), F32), vm((2 * heads, T), F32),
                vm((hs, T), F32), vm((T, 2 * hs), F32), vm((nj, T, rows * 2 * state), BF16),
                vm((nj, T, 128), F32), vm((2, rows + 16, inner), F32), vm((T, D), BF16),
                dma, dma, dma, dma, dma((2, max(n_grp - 1, 1))), dma, dma((3, n_row - 1)), dma, pltpu.SemaphoreType.REGULAR((2,)),
            ],
            compiler_params=pltpu.CompilerParams(
                collective_id=0, has_side_effects=True, vmem_limit_bytes=48 << 20
            ),
            name="block",
        )(*operands)

    placed = (P("row", "col", None),) + (P(),) * 12
    return jax.shard_map(
        on_device, mesh=mesh, in_specs=placed, out_specs=P("row", "col", None), check_vma=False
    )
```

```python
import functools
import jax
import jax.numpy as jnp
from jax import lax
from jax.experimental import pallas as pl
from jax.experimental.pallas import tpu as pltpu
from jax.sharding import PartitionSpec as P

MESH = pl.DeviceIdType.MESH
F32 = jnp.float32
BF16 = jnp.bfloat16
HI = lax.Precision.HIGHEST
epsilon = 1e-06


def iota(shape, dim):
    return lax.broadcasted_iota(jnp.int32, shape, dim)


def exact(a, b):
    return jnp.dot(a, b, precision=HI, preferred_element_type=F32)


def mm(a, b):
    return jnp.dot(a, b, preferred_element_type=F32)


def nt(a, b):
    return lax.dot_general(a, b, (((1,), (1,)), ((), ())), preferred_element_type=F32)


def norm(x, gain):
    return x * lax.rsqrt(jnp.mean(x * x, axis=-1, keepdims=True) + epsilon) * gain


def silu(v):
    return v * (1.0 / (1.0 + jnp.exp(-v)))


def softplus(x):
    return jnp.maximum(x, 0.0) + jnp.log1p(jnp.exp(-jnp.abs(x)))


def copy_to(src, dst, send, recv, row, col):
    return pltpu.make_async_remote_copy(
        src_ref=src, dst_ref=dst, send_sem=send, recv_sem=recv,
        device_id=(row, col), device_id_type=MESH,
    )


def split(nj, rows, n_col):
    share = 2 if n_col % (2 * nj) == 0 else 1
    return share, rows // share, nj * share


def kernel(
    dims,
    tok_ref, ng_ref, wi_ref, wsel_ref, wst_ref, sb_ref, ra_ref, rd_ref, cw_ref, cb_ref,
    sk_ref, og_ref, wo_ref,
    out_ref,
    tok_v, ng_v, wi_v, wsel_v, wst_v, sb_v, ra_v, rd_v, cw_v, cb_v, sk_v, og_v, wo_v, w_sem,
    hb, eb, xp, vals, vbf, bd_s, logs_s, dj, fbuf, drecv, frecv, tbuf, tdec, trecv, tdrecv, ibuf, pbuf, precv,
    vrecv, brecv, lrecv, sc, gate, acc, cexp, cds, cum_s, cum_ts, btail, sel_s, maps, pre, lh, norm_s,
    sent, h_recv, d_recv, f_recv, t_recv, p_recv, v_recv, s_recv, near,
):
    n_row, n_col, rows, cols, heads, state, full_w, height = dims
    T = rows * cols
    loads = [
        pltpu.make_async_copy(src, dst, w_sem.at[(0, 1, 2, 3, 1, 1, 1, 1, 4, 4, 4, 4, 5)[k]])
        for k, (src, dst) in enumerate((
            (tok_ref, tok_v), (ng_ref, ng_v), (wi_ref, wi_v), (wsel_ref, wsel_v), (wst_ref, wst_v),
            (sb_ref, sb_v), (ra_ref, ra_v), (rd_ref, rd_v), (cw_ref, cw_v), (cb_ref, cb_v),
            (sk_ref, sk_v), (og_ref, og_v), (wo_ref, wo_v),
        ))
    ]
    tok_ref, ng_ref, wi_ref, wsel_ref, wst_ref = tok_v, ng_v, wi_v, wsel_v, wst_v
    sb_ref, ra_ref, rd_ref, cw_ref, cb_ref = sb_v, ra_v, rd_v, cw_v, cb_v
    sk_ref, og_ref, wo_ref = sk_v, og_v, wo_v
    inner = wo_ref.shape[0]
    D = tok_ref.shape[2]
    nj = inner // 128
    share, keep, G = split(nj, rows, n_col)
    n_grp = n_col // G
    hs = heads * state
    nh = 2 * heads
    r = lax.axis_index("row")
    c = lax.axis_index("col")
    g, q = c // G, c % G
    mine_j, mine_h = q // share, q % share
    i0 = mine_h * keep
    if nj == 4:
        far = [3 - mine_j, (mine_j + 2) % 4, mine_j + 1 - 2 * (mine_j % 2), mine_j]
    else:
        far = [(mine_j + k) % nj for k in range(1, nj)] + [mine_j]
    peers = [(j, h, j * share + h) for j in far[:-1] for h in range(share)]
    peers += [(mine_j, h, mine_j * share + h) for h in [(mine_h + k) % share for k in range(1, share)]]
    if len(peers) == 7:
        peers = [peers[k] for k in (0, 2, 1, 3, 4, 5, 6)]
    base = g * G

    barrier = pltpu.get_barrier_semaphore()

    plan = (
        (0, 1, 0, tok_ref.at[rows - 1]),
        (1, -1, 0, tok_ref.at[0]),
        (2, 0, 1, eb.at[1]),
        (3, 0, -1, eb.at[0]),
        (4, 1, 1, eb.at[1]),
        (5, 1, -1, eb.at[0]),
        (6, -1, 1, eb.at[1]),
        (7, -1, -1, eb.at[0]),
    )

    def there(dr, dc):
        return (r + dr >= 0) & (r + dr < n_row) & (c + dc >= 0) & (c + dc < n_col)

    loads[0].start()
    hb[...] = jnp.zeros_like(hb)
    friends = [(dr, dc, there(dr, dc)) for _, dr, dc, _ in plan]
    friends += [(dr, 0, there(dr, 0)) for k in range(2, n_row) for dr in (k, -k)]
    ahead = [(0, dc, q + dc < G) for dc in range(2, G)] + [(0, G * k, g + k < n_grp) for k in range(1, n_grp)]
    for dr, dc, ok in friends + ahead:
        @pl.when(ok)
        def _():
            pl.semaphore_signal(barrier, inc=1, device_id=(r + dr, c + dc), device_id_type=MESH)
    for load in loads[1:]:
        load.start()
    eb[...] = jnp.zeros_like(eb)
    lh[...] = jnp.zeros_like(lh)
    for i in range(rows):
        xp[i + 1, 0:8, :] = jnp.zeros((8, inner), F32)
        xp[i + 1, 8 + cols:16 + cols, :] = jnp.zeros((8, inner), F32)

    loads[0].wait()
    eb[0, 0:rows, :] = tok_ref[:, 0, :]
    eb[1, 0:rows, :] = tok_ref[:, cols - 1, :]
    pl.semaphore_wait(barrier, sum(jnp.where(ok, 1, 0) for _, _, ok in friends) + jnp.maximum(q - 1, 0) + g)

    for slot, dr, dc, src in plan:
        @pl.when(there(dr, dc))
        def _():
            copy_to(src, hb.at[slot], sent, h_recv, r + dr, c + dc).start()

    for dc in range(2, G):
        @pl.when(q >= dc)
        def _():
            pl.semaphore_signal(near.at[0], inc=1, device_id=(r, c - dc), device_id_type=MESH)
    for k in range(1, n_grp):
        @pl.when(g >= k)
        def _():
            pl.semaphore_signal(near.at[1], inc=1, device_id=(r, c - G * k), device_id_type=MESH)

    for k in (1, 4, 5, 6, 7):
        loads[k].wait()
    x = tok_ref[...].astype(F32).reshape(T, D)
    normed = norm(x, ng_ref[...]).astype(BF16)
    norm_s[...] = normed
    loads[2].wait()
    main_x = mm(normed, wi_ref[:, :inner]).astype(BF16).astype(F32)
    for i in range(rows):
        xp[i + 1, 8:8 + cols, :] = main_x[i * cols:(i + 1) * cols]

    def column(row):
        width = row.shape[1]
        square = jnp.broadcast_to(row, (width, width))
        return jnp.sum(
            jnp.where(iota((width, width), 0) == iota((width, width), 1), square, 0.0), axis=1, keepdims=True
        )

    t_i, u_i = iota((T, T), 0), iota((T, T), 1)
    row_same = (t_i // cols) == (u_i // cols)
    col_same = (t_i % cols) == (u_i % cols)
    step_t = nt(wst_ref[...], normed)
    rate = jnp.concatenate([column(ra_ref[...]) / full_w, column(rd_ref[...]) / height], axis=0)
    logs_t = -softplus(step_t + column(sb_ref[...])) * rate

    def thirds(v):
        hi = v.astype(BF16)
        rest = v - hi.astype(F32)
        mid = rest.astype(BF16)
        return hi, mid, (rest - mid.astype(F32)).astype(BF16)

    up = t_i <= u_i
    sums = jnp.concatenate(
        [jnp.where(m, 1.0, 0.0).astype(BF16) for m in (row_same & up, row_same, col_same & up, col_same)], axis=1
    )
    parts = mm(jnp.concatenate(thirds(logs_t), axis=0), sums)
    summed = parts[:nh] + parts[nh:2 * nh] + parts[2 * nh:]
    cum_t = jnp.concatenate([summed[:heads, 0:T], summed[heads:, 2 * T:3 * T]], axis=0)
    tot_t = jnp.concatenate([summed[:heads, T:2 * T], summed[heads:, 3 * T:]], axis=0)
    logs_s[0:heads] = tot_t[heads:] - cum_t[heads:]
    logs_s[heads:] = tot_t[heads:]
    cum_ts[...] = cum_t
    cum = jnp.concatenate([cum_t, jnp.zeros((T - nh, T), F32)], axis=0).T[:, :nh]
    cum_s[...] = cum

    row_tot = jnp.concatenate([cum[(i + 1) * cols - 1:(i + 1) * cols] for i in range(rows)], axis=0)
    spread = jnp.where(iota((nh, inner), 0) == iota((nh, inner), 1) // (inner // heads), 1.0, 0.0).astype(BF16)
    wide = sum(mm(part, spread) for part in thirds(row_tot))
    for j in range(nj):
        dj[j] = wide[:, j * 128:(j + 1) * 128]

    def per_state(v):
        return jnp.concatenate([jnp.broadcast_to(v[k:k + 1], (state, T)) for k in range(heads)], axis=0)

    loads[3].wait()
    sel = mm(normed, wsel_ref[...])
    sel_s[...] = sel[:, :2 * hs]
    btail[...] = sel[:, :hs].T * per_state(jnp.exp(tot_t - cum_t))
    bd_s[...] = sel[:, 2 * hs:3 * hs].astype(BF16)
    cds[...] = sel[:, 3 * hs:].astype(BF16)

    def down_early(to_row, slot, dest):
        return (
            copy_to(bd_s, brecv.at[slot], sent, v_recv.at[1, slot], to_row, c),
            copy_to(logs_s, lrecv.at[slot], sent, v_recv.at[2, slot], to_row, c),
        )

    def down_values(to_row, slot, dest):
        return copy_to(vbf, vrecv.at[slot], sent, v_recv.at[0, slot], to_row, c)

    for k in range(1, n_row):
        @pl.when(r < k)
        def _():
            for cp in down_early(k, r, k):
                cp.start()

    for k in (8, 9, 10, 11):
        loads[k].wait()
    for j in range(nj):
        ln = slice(j * 128, (j + 1) * 128)
        w9 = [cw_ref[a, b:b + 1, ln] for a in range(3) for b in range(3)]
        bias = cb_ref[:, ln]
        for i in range(rows):
            total = jnp.zeros((cols, 128), F32) + bias
            for a in range(3):
                if 0 <= i + a - 1 < rows:
                    for b in range(3):
                        total = total + xp[i + a, 7 + b:7 + b + cols, ln] * w9[a * 3 + b]
            pre[j, i * cols:(i + 1) * cols] = total
            vals[j, i * cols:(i + 1) * cols] = silu(total)

    @pl.when(q < G - 2)
    def _():
        pl.semaphore_wait(near.at[0], G - 2 - q)

    for j, h, p in peers:
        copy_to(dj.at[j], drecv.at[q], sent, d_recv, r, base + p).start()

    beside = sum(jnp.where(there(dr, dc), 1, 0) for _, dr, dc, _ in plan)

    def halos(n):
        some = hb.at[pl.ds(0, n)]
        return copy_to(some, some, sent, h_recv, r, c)

    for n in (3, 5, 8):
        @pl.when(beside == n)
        def _():
            halos(n).wait_recv()
    edge = norm(hb[...].astype(F32).reshape(8 * cols, D), ng_ref[...]).astype(BF16)
    edge_x = mm(edge, wi_ref[:, :inner]).astype(BF16).astype(F32)
    xp[0, 8:8 + cols, :] = edge_x[0:cols]
    xp[rows + 1, 8:8 + cols, :] = edge_x[cols:2 * cols]
    lh[0, 8:8 + rows, :] = edge_x[2 * cols:2 * cols + rows]
    lh[1, 8:8 + rows, :] = edge_x[3 * cols:3 * cols + rows]
    xp[0, 7:8, :] = edge_x[4 * cols + rows - 1:4 * cols + rows]
    xp[0, 8 + cols:9 + cols, :] = edge_x[5 * cols + rows - 1:5 * cols + rows]
    xp[rows + 1, 7:8, :] = edge_x[6 * cols:6 * cols + 1]
    xp[rows + 1, 8 + cols:9 + cols, :] = edge_x[7 * cols:7 * cols + 1]

    first = iota((1, 128), 1) < 64
    pair = 2 * state
    own = (iota((rows * pair, T), 0) // pair) == (iota((rows * pair, T), 1) // cols)
    for j in range(nj):
        ln = slice(j * 128, (j + 1) * 128)
        for i, a, edge_row in ((0, 0, 0), (rows - 1, 2, rows + 1)):
            at = slice(i * cols, (i + 1) * cols)
            total = pre[j, at]
            for b in range(3):
                total = total + xp[edge_row, 7 + b:7 + b + cols, ln] * cw_ref[a, b:b + 1, ln]
            pre[j, at] = total
            vals[j, at] = silu(total)
        for e, at, b in ((0, 0, 0), (1, cols - 1, 2)):
            some = pl.ds(at, rows, stride=cols)
            total = pre[j, some, :]
            for a in range(3):
                total = total + lh[e, 7 + a:7 + a + rows, ln] * cw_ref[a, b:b + 1, ln]
            vals[j, some, :] = silu(total)
        vbf[j] = vals[j].astype(BF16)

        piece = jnp.concatenate([btail[j * pair:(j + 1) * pair, :]] * rows, axis=0)
        piece = jnp.where(own, piece, 0.0).astype(BF16)
        res = mm(piece, vbf[j])
        for i in range(rows):
            top = res[i * pair:i * pair + state]
            bottom = res[i * pair + state:(i + 1) * pair]
            fbuf[j * share + i // keep, i % keep] = jnp.where(first, top, bottom).astype(BF16)
    for _, _, p in peers:
        copy_to(fbuf.at[p], frecv.at[q], sent, f_recv, r, base + p).start()

    for k in range(1, n_row):
        @pl.when(r < k)
        def _():
            down_values(k, r, k).start()

    @pl.when(c == 0)
    def _():
        copy_to(fbuf, precv, sent, s_recv, r, c + 1).start()
        precv[...] = jnp.zeros_like(precv)

    frecv[q] = fbuf[q]
    drecv[q] = dj[mine_j]

    low = u_i <= t_i
    mask_a, mask_d = row_same & low, col_same & low
    lane_head = iota((T, hs), 1) // state
    zero_b = jnp.zeros((T, hs), BF16)
    b_a, c_a = sel_s[:, 0:hs], sel_s[:, hs:]
    cexp[...] = (c_a * per_state(jnp.exp(cum_ts[...])).T).astype(BF16)
    b_ab, c_ab, b_db, c_db = b_a.astype(BF16), c_a.astype(BF16), bd_s[...], cds[...]
    for k in range(heads):
        only = lane_head == k
        s_a = nt(c_ab, jnp.where(only, b_ab, zero_b))
        s_d = nt(c_db, jnp.where(only, b_db, zero_b))
        g_a = jnp.where(mask_a, cum_s[:, k:k + 1] - cum_ts[k:k + 1, :], -1e30)
        g_d = jnp.where(mask_d, cum_s[:, heads + k:heads + k + 1] - cum_ts[heads + k:heads + k + 1, :], -1e30)
        sc[k // 2, :, (k % 2) * T:(k % 2 + 1) * T] = (s_a * jnp.exp(g_a) + s_d * jnp.exp(g_d)).astype(BF16)

    def times_values(scores, v_tile):
        zero = jnp.zeros((T, 128), BF16)
        stacked = jnp.concatenate(
            [jnp.where(first, v_tile, zero), jnp.where(first, zero, v_tile)], axis=0
        )
        return mm(scores, stacked)

    others = pl.ds(0, G - 1)

    def whole(ref, send, recv):
        return copy_to(ref.at[others], ref.at[others], send, recv, r, c)

    whole(drecv, sent, d_recv).wait_recv()
    logs = [drecv[e, pl.ds(i0, keep), :] for e in range(G)]
    tdec[...] = sum(logs)
    decays = [jnp.exp(v)[:, None, :] for v in logs]

    def total_decay(k):
        return copy_to(tdec, tdrecv.at[g], sent, t_recv.at[0, g], r, c + G * k)

    def total_state(k):
        return copy_to(tbuf, trecv.at[g], sent, t_recv.at[1, g], r, c + G * k)

    def later(k):
        return g + k < n_grp

    whole(frecv, sent, f_recv).wait_recv()
    @pl.when(g < n_grp - 1)
    def _():
        pl.semaphore_wait(near.at[1], n_grp - 1 - g)

    carry = frecv[0].astype(F32)
    for e in range(1, G):
        carry = decays[e] * carry + frecv[e].astype(F32)
    tbuf[...] = carry.astype(BF16)
    for k in range(1, n_grp):
        @pl.when(later(k))
        def _():
            total_state(k).start()

        @pl.when(later(k) & (g > 0))
        def _():
            total_decay(k).start()

    gate[...] = silu(mm(norm_s[...], wi_ref[:, inner:]).astype(BF16).astype(F32))
    for j in range(nj):
        ln = slice(j * 128, (j + 1) * 128)
        acc[:, ln] = times_values(sc[j], vbf[j]) + sk_ref[:, ln] * vals[j]

    mine = (iota((T, rows * pair), 0) // cols) == (iota((T, rows * pair), 1) // pair)
    for j in range(nj):
        src = iota((hs, rows * pair), 0)
        dst = iota((hs, rows * pair), 1) % pair
        rep = (src == dst + j * pair).astype(BF16)
        maps[j] = jnp.where(mine, mm(cexp[...], rep), 0.0).astype(BF16)

    ibuf[...] = jnp.zeros_like(ibuf)
    for m in range(n_grp - 1):
        @pl.when(m < g)
        def _():
            if m:
                copy_to(tdec, tdrecv.at[m], sent, t_recv.at[0, m], r, c).wait_recv()
            copy_to(tbuf, trecv.at[m], sent, t_recv.at[1, m], r, c).wait_recv()
            if m:
                ibuf[...] = jnp.exp(tdrecv[m])[:, None, :] * ibuf[...] + trecv[m].astype(F32)
            else:
                ibuf[...] = trecv[m].astype(F32)
    carry = ibuf[...]
    for e in range(G):
        pbuf[e] = carry.astype(BF16)
        if e < G - 1:
            carry = decays[e] * carry + frecv[e].astype(F32)
    for j, h, p in peers:
        @pl.when(base + p > 1)
        def _():
            copy_to(pbuf.at[p], precv.at[q], sent, p_recv, r, base + p).start()

    @pl.when(c > 1)
    def _():
        precv[q] = pbuf[q]

    for back in range(1, n_row):
        @pl.when(r >= back)
        def _():
            slot = r - back
            for cp in down_early(r, slot, 1):
                cp.wait_recv()
            down_values(r, slot, 1).wait_recv()
            gap = lrecv[slot, 0:heads]
            for nearer in range(1, back):
                gap = gap + lrecv[r - nearer, heads:]
            same = (iota((T, T), 0) % cols) == (iota((T, T), 1) % cols)
            for j in range(nj):
                parts = []
                for k in (2 * j, 2 * j + 1):
                    only = (iota((T, hs), 1) // state) == k
                    s_d = nt(cds[...], jnp.where(only, brecv[slot], jnp.zeros((T, hs), BF16)))
                    g_d = jnp.where(same, cum_s[:, heads + k:heads + k + 1] + gap[k:k + 1, :], -1e30)
                    parts.append((s_d * jnp.exp(g_d)).astype(BF16))
                ln = slice(j * 128, (j + 1) * 128)
                acc[:, ln] += times_values(jnp.concatenate(parts, axis=1), vrecv[slot, j])

    for n in (3, 5, 8):
        @pl.when(beside == n)
        def _():
            halos(n).wait_send()
    whole(drecv, sent, d_recv).wait_send()
    whole(frecv, sent, f_recv).wait_send()
    @pl.when(c == 0)
    def _():
        copy_to(fbuf, precv, sent, s_recv, r, c).wait_send()
    for k in range(1, n_grp):
        @pl.when(later(k))
        def _():
            total_state(k).wait_send()

        @pl.when(later(k) & (g > 0))
        def _():
            total_decay(k).wait_send()
    for k in range(1, n_row):
        @pl.when(r < k)
        def _():
            for cp in down_early(r, 0, k):
                cp.wait_send()
            down_values(r, 0, k).wait_send()

    @pl.when(c == 1)
    def _():
        copy_to(fbuf, precv, sent, s_recv, r, c).wait_recv()

    tiles = []
    zero_s = jnp.zeros((state, 128), BF16)
    @pl.when(c > 1)
    def _():
        whole(precv, sent, p_recv).wait_recv()

    for j in range(nj):
        ln = slice(j * 128, (j + 1) * 128)
        blocks = []
        for i in range(rows):
            s = precv[j * share + i // keep, i % keep]
            blocks += [jnp.where(first, s, zero_s), jnp.where(first, zero_s, s)]
        tiles.append((acc[:, ln] + mm(maps[j], jnp.concatenate(blocks, axis=0))) * gate[:, ln])

    loads[12].wait()
    mixed = jnp.concatenate(tiles, axis=1)
    gated = norm(mixed, og_ref[...]).astype(BF16)
    result = mm(gated, wo_ref[...]) + tok_ref[...].astype(F32).reshape(T, D)
    out_ref[...] = result.astype(BF16).reshape(rows, cols, D)

    skipped = jnp.where(g > 0, 0, jnp.where(c > 1, 2, 1))
    for n in range(3):
        @pl.when(skipped == n)
        def _():
            some = pbuf.at[pl.ds(0, G - 1 - n)]
            copy_to(some, some, sent, p_recv, r, c).wait_send()


def solution(mesh):
    n_row, n_col = mesh.shape["row"], mesh.shape["col"]

    def on_device(
        tokens, norm_gain, w_inner, w_select, w_step, step_bias, rate_across, rate_down,
        conv_weight, conv_bias, skip_gain, out_gain, w_out,
    ):
        rows, cols, D = tokens.shape
        heads = rate_across.shape[0]
        inner = w_out.shape[0]
        hs = w_select.shape[1] // 4
        state = hs // heads
        T = rows * cols
        nj = inner // 128
        share, keep, G = split(nj, rows, n_col)
        n_grp = n_col // G
        dims = (n_row, n_col, rows, cols, heads, state, float(cols * n_col), float(rows * n_row))
        vm = pltpu.VMEM
        dma = pltpu.SemaphoreType.DMA
        operands = (
            tokens, norm_gain[None], w_inner, w_select, w_step.T, step_bias[None], rate_across[None],
            rate_down[None], conv_weight, conv_bias[None], skip_gain[None], out_gain[None], w_out,
        )
        operands = tuple(pltpu.with_memory_space_constraint(o, pltpu.HBM) for o in operands)
        return pl.pallas_call(
            functools.partial(kernel, dims),
            out_shape=jax.ShapeDtypeStruct(tokens.shape, tokens.dtype),
            in_specs=[pl.BlockSpec(memory_space=pltpu.HBM)] * 13,
            out_specs=pl.BlockSpec(memory_space=pltpu.VMEM),
            scratch_shapes=[vm(o.shape, o.dtype) for o in operands] + [dma((6,))] + [
                vm((8, cols, D), BF16), vm((2, cols, D), BF16),
                vm((rows + 2, cols + 16, inner), F32),
                vm((nj + 1, T, 128), F32), vm((nj, T, 128), BF16), vm((T, hs), BF16),
                vm((2 * heads, T), F32), vm((nj, rows, 128), F32),
                vm((G, keep, state, 128), BF16), vm((G + 1, rows, 128), F32), vm((G, keep, state, 128), BF16),
                vm((keep, state, 128), BF16), vm((keep, 128), F32),
                vm((n_grp, keep, state, 128), BF16), vm((n_grp, keep, 128), F32), vm((keep, state, 128), F32),
                vm((G, keep, state, 128), BF16), vm((G, keep, state, 128), BF16),
                vm((n_row, nj, T, 128), BF16), vm((n_row, T, hs), BF16), vm((n_row, 2 * heads, T), F32),
                vm((heads // 2, T, 2 * T), BF16), vm((T, inner), F32), vm((T, inner), F32),
                vm((T, hs), BF16), vm((T, hs), BF16), vm((T, 2 * heads), F32), vm((2 * heads, T), F32),
                vm((hs, T), F32), vm((T, 2 * hs), F32), vm((nj, T, rows * 2 * state), BF16),
                vm((nj + 1, T, 128), F32), vm((2, rows + 16, inner), F32), vm((T, D), BF16),
                dma, dma, dma, dma, dma((2, max(n_grp - 1, 1))), dma, dma((3, n_row - 1)), dma, pltpu.SemaphoreType.REGULAR((2,)),
            ],
            compiler_params=pltpu.CompilerParams(
                collective_id=0, has_side_effects=True, vmem_limit_bytes=48 << 20
            ),
            name="block",
        )(*operands)

    placed = (P("row", "col", None),) + (P(),) * 12
    return jax.shard_map(
        on_device, mesh=mesh, in_specs=placed, out_specs=P("row", "col", None), check_vma=False
    )
```

```python
import functools
import jax
import jax.numpy as jnp
from jax import lax
from jax.experimental import pallas as pl
from jax.experimental.pallas import tpu as pltpu
from jax.sharding import PartitionSpec as P

MESH = pl.DeviceIdType.MESH
F32 = jnp.float32
BF16 = jnp.bfloat16
HI = lax.Precision.HIGHEST
epsilon = 1e-06


def iota(shape, dim):
    return lax.broadcasted_iota(jnp.int32, shape, dim)


def exact(a, b):
    return jnp.dot(a, b, precision=HI, preferred_element_type=F32)


def mm(a, b):
    return jnp.dot(a, b, preferred_element_type=F32)


def nt(a, b):
    return lax.dot_general(a, b, (((1,), (1,)), ((), ())), preferred_element_type=F32)


def norm(x, gain):
    return x * lax.rsqrt(jnp.mean(x * x, axis=-1, keepdims=True) + epsilon) * gain


def silu(v):
    return v * (1.0 / (1.0 + jnp.exp(-v)))


def softplus(x):
    return jnp.maximum(x, 0.0) + jnp.log1p(jnp.exp(-jnp.abs(x)))


def copy_to(src, dst, send, recv, row, col):
    return pltpu.make_async_remote_copy(
        src_ref=src, dst_ref=dst, send_sem=send, recv_sem=recv,
        device_id=(row, col), device_id_type=MESH,
    )


def split(nj, rows, n_col):
    return 2, rows // 2, 2 * nj


def kernel(
    dims,
    tok_ref, ng_ref, wi_ref, wsel_ref, wst_ref, sb_ref, ra_ref, rd_ref, cw_ref, cb_ref,
    sk_ref, og_ref, wo_ref,
    out_ref,
    tok_v, ng_v, wi_v, wsel_v, wst_v, sb_v, ra_v, rd_v, cw_v, cb_v, sk_v, og_v, wo_v, w_sem,
    hb, eb, xp, vals, vbf, bd_s, logs_s, dj, fbuf, drecv, frecv, tbuf, tdec, trecv, tdrecv, ibuf, pbuf, precv,
    vrecv, brecv, lrecv, sc, gate, acc, cexp, cds, cum_s, cum_ts, btail, sel_s, maps, pre, lh, norm_s,
    sent, h_recv, d_recv, f_recv, t_recv, p_recv, v_recv, s_recv, near,
):
    n_row, n_col, rows, cols, heads, state, full_w, height = dims
    T = rows * cols
    loads = [
        pltpu.make_async_copy(src, dst, w_sem.at[(0, 1, 2, 3, 1, 1, 1, 1, 4, 4, 4, 4, 5)[k]])
        for k, (src, dst) in enumerate((
            (tok_ref, tok_v), (ng_ref, ng_v), (wi_ref, wi_v), (wsel_ref, wsel_v), (wst_ref, wst_v),
            (sb_ref, sb_v), (ra_ref, ra_v), (rd_ref, rd_v), (cw_ref, cw_v), (cb_ref, cb_v),
            (sk_ref, sk_v), (og_ref, og_v), (wo_ref, wo_v),
        ))
    ]
    tok_ref, ng_ref, wi_ref, wsel_ref, wst_ref = tok_v, ng_v, wi_v, wsel_v, wst_v
    sb_ref, ra_ref, rd_ref, cw_ref, cb_ref = sb_v, ra_v, rd_v, cw_v, cb_v
    sk_ref, og_ref, wo_ref = sk_v, og_v, wo_v
    inner = wo_ref.shape[0]
    D = tok_ref.shape[2]
    nj = inner // 128
    share, keep, G = split(nj, rows, n_col)
    n_grp = n_col // G
    hs = heads * state
    nh = 2 * heads
    r = lax.axis_index("row")
    c = lax.axis_index("col")
    g, q = c // G, c % G
    mine_j, mine_h = q // share, q % share
    i0 = mine_h * keep
    if nj == 4:
        far = [3 - mine_j, (mine_j + 2) % 4, mine_j + 1 - 2 * (mine_j % 2), mine_j]
    else:
        far = [(mine_j + k) % nj for k in range(1, nj)] + [mine_j]
    peers = [(j, h, j * share + h) for j in far[:-1] for h in range(share)]
    peers += [(mine_j, h, mine_j * share + h) for h in [(mine_h + k) % share for k in range(1, share)]]
    if len(peers) == 7:
        peers = [peers[k] for k in (0, 2, 1, 3, 4, 5, 6)]
    base = g * G

    barrier = pltpu.get_barrier_semaphore()

    plan = (
        (0, 0, 1, eb.at[1]),
        (1, 0, -1, eb.at[0]),
        (4, 1, 1, eb.at[1]),
        (5, 1, -1, eb.at[0]),
        (6, -1, 1, eb.at[1]),
        (7, -1, -1, eb.at[0]),
        (2, 1, 0, tok_ref.at[rows - 1]),
        (3, -1, 0, tok_ref.at[0]),
    )

    def there(dr, dc):
        return (r + dr >= 0) & (r + dr < n_row) & (c + dc >= 0) & (c + dc < n_col)

    loads[0].start()
    hb[...] = jnp.zeros_like(hb)
    friends = [(dr, dc, there(dr, dc)) for _, dr, dc, _ in plan]
    friends += [(dr, 0, there(dr, 0)) for k in range(2, n_row) for dr in (k, -k)]
    ahead = [(0, dc, q + dc < G) for dc in range(2, G)] + [(0, G * k, g + k < n_grp) for k in range(1, n_grp)]
    for dr, dc, ok in friends + ahead:
        @pl.when(ok)
        def _():
            pl.semaphore_signal(barrier, inc=1, device_id=(r + dr, c + dc), device_id_type=MESH)
    for load in loads[1:]:
        load.start()
    eb[...] = jnp.zeros_like(eb)
    lh[...] = jnp.zeros_like(lh)
    for i in (0, rows + 1):
        xp[i] = jnp.zeros(xp.shape[1:], F32)
    for i in range(rows):
        xp[i + 1, 0:8, :] = jnp.zeros((8, inner), F32)
        xp[i + 1, 8 + cols:16 + cols, :] = jnp.zeros((8, inner), F32)

    loads[0].wait()
    eb[0, 0:rows, :] = tok_ref[:, 0, :]
    eb[1, 0:rows, :] = tok_ref[:, cols - 1, :]
    pl.semaphore_wait(barrier, sum(jnp.where(ok, 1, 0) for _, _, ok in friends) + jnp.maximum(q - 1, 0) + g)

    for slot, dr, dc, src in plan:
        @pl.when(there(dr, dc))
        def _():
            copy_to(src, hb.at[slot], sent, h_recv.at[min(slot, 2) // 2], r + dr, c + dc).start()

    for dc in range(2, G):
        @pl.when(q >= dc)
        def _():
            pl.semaphore_signal(near.at[0], inc=1, device_id=(r, c - dc), device_id_type=MESH)
    for k in range(1, n_grp):
        @pl.when(g >= k)
        def _():
            pl.semaphore_signal(near.at[1], inc=1, device_id=(r, c - G * k), device_id_type=MESH)

    for k in (1, 4, 5, 6, 7):
        loads[k].wait()
    x = tok_ref[...].astype(F32).reshape(T, D)
    normed = norm(x, ng_ref[...]).astype(BF16)
    norm_s[...] = normed
    loads[2].wait()
    main_x = mm(normed, wi_ref[:, :inner]).astype(BF16).astype(F32)
    for i in range(rows):
        xp[i + 1, 8:8 + cols, :] = main_x[i * cols:(i + 1) * cols]

    def column(row):
        width = row.shape[1]
        square = jnp.broadcast_to(row, (width, width))
        return jnp.sum(
            jnp.where(iota((width, width), 0) == iota((width, width), 1), square, 0.0), axis=1, keepdims=True
        )

    t_i, u_i = iota((T, T), 0), iota((T, T), 1)
    row_same = (t_i // cols) == (u_i // cols)
    col_same = (t_i % cols) == (u_i % cols)
    step_t = nt(wst_ref[...], normed)
    rate = jnp.concatenate([column(ra_ref[...]) / full_w, column(rd_ref[...]) / height], axis=0)
    logs_t = -softplus(step_t + column(sb_ref[...])) * rate

    def thirds(v):
        hi = v.astype(BF16)
        rest = v - hi.astype(F32)
        mid = rest.astype(BF16)
        return hi, mid, (rest - mid.astype(F32)).astype(BF16)

    up = t_i <= u_i
    sums = jnp.concatenate(
        [jnp.where(m, 1.0, 0.0).astype(BF16) for m in (row_same & up, row_same, col_same & up, col_same)], axis=1
    )
    parts = mm(jnp.concatenate(thirds(logs_t), axis=0), sums)
    summed = parts[:nh] + parts[nh:2 * nh] + parts[2 * nh:]
    cum_t = jnp.concatenate([summed[:heads, 0:T], summed[heads:, 2 * T:3 * T]], axis=0)
    tot_t = jnp.concatenate([summed[:heads, T:2 * T], summed[heads:, 3 * T:]], axis=0)
    logs_s[0:heads] = tot_t[heads:] - cum_t[heads:]
    logs_s[heads:] = tot_t[heads:]
    cum_ts[...] = cum_t
    cum = jnp.concatenate([cum_t, jnp.zeros((T - nh, T), F32)], axis=0).T[:, :nh]
    cum_s[...] = cum

    row_tot = jnp.concatenate([cum[(i + 1) * cols - 1:(i + 1) * cols] for i in range(rows)], axis=0)
    spread = jnp.where(iota((nh, inner), 0) == iota((nh, inner), 1) // (inner // heads), 1.0, 0.0).astype(BF16)
    wide = sum(mm(part, spread) for part in thirds(row_tot))
    for j in range(nj):
        dj[j] = wide[:, j * 128:(j + 1) * 128]

    def per_state(v):
        return jnp.concatenate([jnp.broadcast_to(v[k:k + 1], (state, T)) for k in range(heads)], axis=0)

    loads[3].wait()
    sel = mm(normed, wsel_ref[...])
    sel_s[...] = sel[:, :2 * hs]
    btail[...] = sel[:, :hs].T * per_state(jnp.exp(tot_t - cum_t))
    bd_s[...] = sel[:, 2 * hs:3 * hs].astype(BF16)
    cds[...] = sel[:, 3 * hs:].astype(BF16)

    def down_early(to_row, slot, dest):
        return (
            copy_to(bd_s, brecv.at[slot], sent, v_recv.at[1, slot], to_row, c),
            copy_to(logs_s, lrecv.at[slot], sent, v_recv.at[2, slot], to_row, c),
        )

    def down_values(to_row, slot, dest):
        return copy_to(vbf, vrecv.at[slot], sent, v_recv.at[0, slot], to_row, c)

    for k in range(1, n_row):
        @pl.when(r < k)
        def _():
            for cp in down_early(k, r, k):
                cp.start()

    for k in (8, 9, 10, 11):
        loads[k].wait()
    for j in range(nj):
        ln = slice(j * 128, (j + 1) * 128)
        w9 = [cw_ref[a, b:b + 1, ln] for a in range(3) for b in range(3)]
        bias = cb_ref[:, ln]
        for i in range(rows):
            total = jnp.zeros((cols, 128), F32) + bias
            for a in range(3):
                if 0 <= i + a - 1 < rows:
                    for b in range(3):
                        total = total + xp[i + a, 7 + b:7 + b + cols, ln] * w9[a * 3 + b]
            pre[j, i * cols:(i + 1) * cols] = total
            vals[j, i * cols:(i + 1) * cols] = silu(total)

    @pl.when(q < G - 2)
    def _():
        pl.semaphore_wait(near.at[0], G - 2 - q)

    for j, h, p in peers:
        copy_to(dj.at[j], drecv.at[q], sent, d_recv, r, base + p).start()

    sides, rest = (
        sum(jnp.where(there(dr, dc), 1, 0) for slot, dr, dc, _ in plan if (slot >= 2) == other)
        for other in (False, True)
    )

    def halos(n, kind):
        some = hb.at[pl.ds(0, n)]
        return copy_to(some, some, sent, h_recv.at[kind], r, c)

    def halo_x(lo, hi):
        edge = norm(hb[lo:hi].astype(F32).reshape((hi - lo) * cols, D), ng_ref[...]).astype(BF16)
        return mm(edge, wi_ref[:, :inner]).astype(BF16).astype(F32)

    for n in (1, 2):
        @pl.when(sides == n)
        def _():
            halos(n, 0).wait_recv()
    side_x = halo_x(0, 2)
    lh[0, 8:8 + rows, :] = side_x[0:rows]
    lh[1, 8:8 + rows, :] = side_x[cols:cols + rows]

    def take_rest():
        for n in (2, 3, 4, 6):
            @pl.when(rest == n)
            def _():
                halos(n, 1).wait_recv()
        edge_x = halo_x(2, 8)
        xp[0, 8:8 + cols, :] = edge_x[0:cols]
        xp[rows + 1, 8:8 + cols, :] = edge_x[cols:2 * cols]
        xp[0, 7:8, :] = edge_x[2 * cols + rows - 1:2 * cols + rows]
        xp[0, 8 + cols:9 + cols, :] = edge_x[3 * cols + rows - 1:3 * cols + rows]
        xp[rows + 1, 7:8, :] = edge_x[4 * cols:4 * cols + 1]
        xp[rows + 1, 8 + cols:9 + cols, :] = edge_x[5 * cols:5 * cols + 1]

    first = iota((1, 128), 1) < 64
    pair = 2 * state
    for j in range(nj):
        ln = slice(j * 128, (j + 1) * 128)
        for e, at, b in ((0, 0, 0), (1, cols - 1, 2)):
            some = pl.ds(at, rows, stride=cols)
            total = pre[j, some, :]
            for a in range(3):
                total = total + lh[e, 7 + a:7 + a + rows, ln] * cw_ref[a, b:b + 1, ln]
            pre[j, some, :] = total
            vals[j, some, :] = silu(total)

    def states(half):
        row, a, edge_row = ((0, 0, 0), (rows - 1, 2, rows + 1))[half]
        lo = half * keep * cols
        at = slice(row * cols, (row + 1) * cols)
        part = slice(lo, lo + keep * cols)
        own = (iota((keep * pair, keep * cols), 0) // pair) == (iota((keep * pair, keep * cols), 1) // cols)
        for j in range(nj):
            ln = slice(j * 128, (j + 1) * 128)
            total = pre[j, at]
            for b in range(3):
                total = total + xp[edge_row, 7 + b:7 + b + cols, ln] * cw_ref[a, b:b + 1, ln]
            vals[j, at] = silu(total)
            vbf[j, part] = vals[j, part].astype(BF16)
            piece = jnp.concatenate([btail[j * pair:(j + 1) * pair, part]] * keep, axis=0)
            piece = jnp.where(own, piece, 0.0).astype(BF16)
            res = mm(piece, vbf[j, part])
            for i in range(keep):
                top = res[i * pair:i * pair + state]
                bottom = res[i * pair + state:(i + 1) * pair]
                fbuf[j * share + half, i] = jnp.where(first, top, bottom).astype(BF16)

        def send(p):
            copy_to(fbuf.at[p], frecv.at[q], sent, f_recv, r, base + p).start()

        for j in far[:-1]:
            send(j * share + half)

        @pl.when(mine_h != half)
        def _():
            send(mine_j * share + half)

    @pl.when(r == 0)
    def _():
        states(0)
        take_rest()
        states(1)

    @pl.when((r > 0) & (r == n_row - 1))
    def _():
        states(1)
        take_rest()
        states(0)

    if n_row > 2:
        @pl.when((r > 0) & (r < n_row - 1))
        def _():
            take_rest()
            states(0)
            states(1)

    for k in range(1, n_row):
        @pl.when(r < k)
        def _():
            down_values(k, r, k).start()

    @pl.when(c == 0)
    def _():
        copy_to(fbuf, precv, sent, s_recv, r, c + 1).start()
        precv[...] = jnp.zeros_like(precv)

    frecv[q] = fbuf[q]
    drecv[q] = dj[mine_j]

    low = u_i <= t_i
    mask_a, mask_d = row_same & low, col_same & low
    lane_head = iota((T, hs), 1) // state
    zero_b = jnp.zeros((T, hs), BF16)
    b_a, c_a = sel_s[:, 0:hs], sel_s[:, hs:]
    cexp[...] = (c_a * per_state(jnp.exp(cum_ts[...])).T).astype(BF16)
    b_ab, c_ab, b_db, c_db = b_a.astype(BF16), c_a.astype(BF16), bd_s[...], cds[...]
    for k in range(heads):
        only = lane_head == k
        s_a = nt(c_ab, jnp.where(only, b_ab, zero_b))
        s_d = nt(c_db, jnp.where(only, b_db, zero_b))
        g_a = jnp.where(mask_a, cum_s[:, k:k + 1] - cum_ts[k:k + 1, :], -1e30)
        g_d = jnp.where(mask_d, cum_s[:, heads + k:heads + k + 1] - cum_ts[heads + k:heads + k + 1, :], -1e30)
        sc[k // 2, :, (k % 2) * T:(k % 2 + 1) * T] = (s_a * jnp.exp(g_a) + s_d * jnp.exp(g_d)).astype(BF16)

    def times_values(scores, v_tile):
        zero = jnp.zeros((T, 128), BF16)
        stacked = jnp.concatenate(
            [jnp.where(first, v_tile, zero), jnp.where(first, zero, v_tile)], axis=0
        )
        return mm(scores, stacked)

    others = pl.ds(0, G - 1)

    def whole(ref, send, recv):
        return copy_to(ref.at[others], ref.at[others], send, recv, r, c)

    whole(drecv, sent, d_recv).wait_recv()
    logs = [drecv[e, pl.ds(i0, keep), :] for e in range(G)]
    tdec[...] = sum(logs)
    decays = [jnp.exp(v)[:, None, :] for v in logs]

    def total_decay(k):
        return copy_to(tdec, tdrecv.at[g], sent, t_recv.at[0, g], r, c + G * k)

    def total_state(k):
        return copy_to(tbuf, trecv.at[g], sent, t_recv.at[1, g], r, c + G * k)

    def later(k):
        return g + k < n_grp

    whole(frecv, sent, f_recv).wait_recv()
    @pl.when(g < n_grp - 1)
    def _():
        pl.semaphore_wait(near.at[1], n_grp - 1 - g)

    carry = frecv[0].astype(F32)
    for e in range(1, G):
        carry = decays[e] * carry + frecv[e].astype(F32)
    tbuf[...] = carry.astype(BF16)
    for k in range(1, n_grp):
        @pl.when(later(k))
        def _():
            total_state(k).start()

        @pl.when(later(k) & (g > 0))
        def _():
            total_decay(k).start()

    gate[...] = silu(mm(norm_s[...], wi_ref[:, inner:]).astype(BF16).astype(F32))
    for j in range(nj):
        ln = slice(j * 128, (j + 1) * 128)
        acc[:, ln] = times_values(sc[j], vbf[j]) + sk_ref[:, ln] * vals[j]

    mine = (iota((T, rows * pair), 0) // cols) == (iota((T, rows * pair), 1) // pair)
    for j in range(nj):
        src = iota((hs, rows * pair), 0)
        dst = iota((hs, rows * pair), 1) % pair
        rep = (src == dst + j * pair).astype(BF16)
        maps[j] = jnp.where(mine, mm(cexp[...], rep), 0.0).astype(BF16)

    ibuf[...] = jnp.zeros_like(ibuf)
    for m in range(n_grp - 1):
        @pl.when(m < g)
        def _():
            if m:
                copy_to(tdec, tdrecv.at[m], sent, t_recv.at[0, m], r, c).wait_recv()
            copy_to(tbuf, trecv.at[m], sent, t_recv.at[1, m], r, c).wait_recv()
            if m:
                ibuf[...] = jnp.exp(tdrecv[m])[:, None, :] * ibuf[...] + trecv[m].astype(F32)
            else:
                ibuf[...] = trecv[m].astype(F32)
    carry = ibuf[...]
    for e in range(G):
        pbuf[e] = carry.astype(BF16)
        if e < G - 1:
            carry = decays[e] * carry + frecv[e].astype(F32)
    for j, h, p in peers:
        @pl.when(base + p > 1)
        def _():
            copy_to(pbuf.at[p], precv.at[q], sent, p_recv, r, base + p).start()

    @pl.when(c > 1)
    def _():
        precv[q] = pbuf[q]

    for back in range(1, n_row):
        @pl.when(r >= back)
        def _():
            slot = r - back
            for cp in down_early(r, slot, 1):
                cp.wait_recv()
            down_values(r, slot, 1).wait_recv()
            gap = lrecv[slot, 0:heads]
            for nearer in range(1, back):
                gap = gap + lrecv[r - nearer, heads:]
            same = (iota((T, T), 0) % cols) == (iota((T, T), 1) % cols)
            for j in range(nj):
                parts = []
                for k in (2 * j, 2 * j + 1):
                    only = (iota((T, hs), 1) // state) == k
                    s_d = nt(cds[...], jnp.where(only, brecv[slot], jnp.zeros((T, hs), BF16)))
                    g_d = jnp.where(same, cum_s[:, heads + k:heads + k + 1] + gap[k:k + 1, :], -1e30)
                    parts.append((s_d * jnp.exp(g_d)).astype(BF16))
                ln = slice(j * 128, (j + 1) * 128)
                acc[:, ln] += times_values(jnp.concatenate(parts, axis=1), vrecv[slot, j])

    for n in (3, 5, 8):
        @pl.when(sides + rest == n)
        def _():
            halos(n, 0).wait_send()
    whole(drecv, sent, d_recv).wait_send()
    whole(frecv, sent, f_recv).wait_send()
    @pl.when(c == 0)
    def _():
        copy_to(fbuf, precv, sent, s_recv, r, c).wait_send()
    for k in range(1, n_grp):
        @pl.when(later(k))
        def _():
            total_state(k).wait_send()

        @pl.when(later(k) & (g > 0))
        def _():
            total_decay(k).wait_send()
    for k in range(1, n_row):
        @pl.when(r < k)
        def _():
            for cp in down_early(r, 0, k):
                cp.wait_send()
            down_values(r, 0, k).wait_send()

    @pl.when(c == 1)
    def _():
        copy_to(fbuf, precv, sent, s_recv, r, c).wait_recv()

    tiles = []
    zero_s = jnp.zeros((state, 128), BF16)
    @pl.when(c > 1)
    def _():
        whole(precv, sent, p_recv).wait_recv()

    for j in range(nj):
        ln = slice(j * 128, (j + 1) * 128)
        blocks = []
        for i in range(rows):
            s = precv[j * share + i // keep, i % keep]
            blocks += [jnp.where(first, s, zero_s), jnp.where(first, zero_s, s)]
        tiles.append((acc[:, ln] + mm(maps[j], jnp.concatenate(blocks, axis=0))) * gate[:, ln])

    loads[12].wait()
    mixed = jnp.concatenate(tiles, axis=1)
    gated = norm(mixed, og_ref[...]).astype(BF16)
    result = mm(gated, wo_ref[...]) + tok_ref[...].astype(F32).reshape(T, D)
    out_ref[...] = result.astype(BF16).reshape(rows, cols, D)

    skipped = jnp.where(g > 0, 0, jnp.where(c > 1, 2, 1))
    for n in range(3):
        @pl.when(skipped == n)
        def _():
            some = pbuf.at[pl.ds(0, G - 1 - n)]
            copy_to(some, some, sent, p_recv, r, c).wait_send()


def solution(mesh):
    n_row, n_col = mesh.shape["row"], mesh.shape["col"]

    def on_device(
        tokens, norm_gain, w_inner, w_select, w_step, step_bias, rate_across, rate_down,
        conv_weight, conv_bias, skip_gain, out_gain, w_out,
    ):
        rows, cols, D = tokens.shape
        heads = rate_across.shape[0]
        inner = w_out.shape[0]
        hs = w_select.shape[1] // 4
        state = hs // heads
        T = rows * cols
        nj = inner // 128
        share, keep, G = split(nj, rows, n_col)
        n_grp = n_col // G
        dims = (n_row, n_col, rows, cols, heads, state, float(cols * n_col), float(rows * n_row))
        vm = pltpu.VMEM
        dma = pltpu.SemaphoreType.DMA
        operands = (
            tokens, norm_gain[None], w_inner, w_select, w_step.T, step_bias[None], rate_across[None],
            rate_down[None], conv_weight, conv_bias[None], skip_gain[None], out_gain[None], w_out,
        )
        operands = tuple(pltpu.with_memory_space_constraint(o, pltpu.HBM) for o in operands)
        return pl.pallas_call(
            functools.partial(kernel, dims),
            out_shape=jax.ShapeDtypeStruct(tokens.shape, tokens.dtype),
            in_specs=[pl.BlockSpec(memory_space=pltpu.HBM)] * 13,
            out_specs=pl.BlockSpec(memory_space=pltpu.VMEM),
            scratch_shapes=[vm(o.shape, o.dtype) for o in operands] + [dma((6,))] + [
                vm((8, cols, D), BF16), vm((2, cols, D), BF16),
                vm((rows + 2, cols + 16, inner), F32),
                vm((nj + 1, T, 128), F32), vm((nj, T, 128), BF16), vm((T, hs), BF16),
                vm((2 * heads, T), F32), vm((nj, rows, 128), F32),
                vm((G, keep, state, 128), BF16), vm((G + 1, rows, 128), F32), vm((G, keep, state, 128), BF16),
                vm((keep, state, 128), BF16), vm((keep, 128), F32),
                vm((n_grp, keep, state, 128), BF16), vm((n_grp, keep, 128), F32), vm((keep, state, 128), F32),
                vm((G, keep, state, 128), BF16), vm((G, keep, state, 128), BF16),
                vm((n_row, nj, T, 128), BF16), vm((n_row, T, hs), BF16), vm((n_row, 2 * heads, T), F32),
                vm((heads // 2, T, 2 * T), BF16), vm((T, inner), F32), vm((T, inner), F32),
                vm((T, hs), BF16), vm((T, hs), BF16), vm((T, 2 * heads), F32), vm((2 * heads, T), F32),
                vm((hs, T), F32), vm((T, 2 * hs), F32), vm((nj, T, rows * 2 * state), BF16),
                vm((nj + 1, T, 128), F32), vm((2, rows + 16, inner), F32), vm((T, D), BF16),
                dma, dma((2,)), dma, dma, dma((2, max(n_grp - 1, 1))), dma, dma((3, n_row - 1)), dma, pltpu.SemaphoreType.REGULAR((2,)),
            ],
            compiler_params=pltpu.CompilerParams(
                collective_id=0, has_side_effects=True, vmem_limit_bytes=48 << 20
            ),
            name="block",
        )(*operands)

    placed = (P("row", "col", None),) + (P(),) * 12
    return jax.shard_map(
        on_device, mesh=mesh, in_specs=placed, out_specs=P("row", "col", None), check_vma=False
    )
```

```python
import functools
import jax
import jax.numpy as jnp
from jax import lax
from jax.experimental import pallas as pl
from jax.experimental.pallas import tpu as pltpu
from jax.sharding import PartitionSpec as P

MESH = pl.DeviceIdType.MESH
F32 = jnp.float32
BF16 = jnp.bfloat16
HI = lax.Precision.HIGHEST
epsilon = 1e-06


def iota(shape, dim):
    return lax.broadcasted_iota(jnp.int32, shape, dim)


def exact(a, b):
    return jnp.dot(a, b, precision=HI, preferred_element_type=F32)


def mm(a, b):
    return jnp.dot(a, b, preferred_element_type=F32)


def nt(a, b):
    return lax.dot_general(a, b, (((1,), (1,)), ((), ())), preferred_element_type=F32)


def norm(x, gain):
    return x * lax.rsqrt(jnp.mean(x * x, axis=-1, keepdims=True) + epsilon) * gain


def silu(v):
    return v * (1.0 / (1.0 + jnp.exp(-v)))


def softplus(x):
    return jnp.maximum(x, 0.0) + jnp.log1p(jnp.exp(-jnp.abs(x)))


def copy_to(src, dst, send, recv, row, col):
    return pltpu.make_async_remote_copy(
        src_ref=src, dst_ref=dst, send_sem=send, recv_sem=recv,
        device_id=(row, col), device_id_type=MESH,
    )


def split(nj, rows, n_col):
    return 2, rows // 2, 2 * nj


def kernel(
    dims,
    tok_ref, ng_ref, wi_ref, wsel_ref, wst_ref, sb_ref, ra_ref, rd_ref, cw_ref, cb_ref,
    sk_ref, og_ref, wo_ref,
    out_ref,
    tok_v, ng_v, wi_v, wsel_v, wst_v, sb_v, ra_v, rd_v, cw_v, cb_v, sk_v, og_v, wo_v, w_sem,
    hb, eb, xp, vals, vbf, bd_s, logs_s, dj, fbuf, drecv, frecv, tbuf, tdec, trecv, tdrecv, ibuf, pbuf, precv,
    vrecv, brecv, lrecv, sc, gate, acc, cexp, cds, cum_s, cum_ts, btail, sel_s, maps, pre, lh, norm_s,
    sent, h_recv, d_recv, f_recv, t_recv, p_recv, v_recv, s_recv, near,
):
    n_row, n_col, rows, cols, heads, state, full_w, height = dims
    T = rows * cols
    loads = [
        pltpu.make_async_copy(src, dst, w_sem.at[(0, 1, 2, 2, 1, 1, 1, 1, 3, 3, 3, 3, 3)[k]])
        for k, (src, dst) in enumerate((
            (tok_ref, tok_v), (ng_ref, ng_v), (wi_ref, wi_v), (wsel_ref, wsel_v), (wst_ref, wst_v),
            (sb_ref, sb_v), (ra_ref, ra_v), (rd_ref, rd_v), (cw_ref, cw_v), (cb_ref, cb_v),
            (sk_ref, sk_v), (og_ref, og_v), (wo_ref, wo_v),
        ))
    ]
    tok_ref, ng_ref, wi_ref, wsel_ref, wst_ref = tok_v, ng_v, wi_v, wsel_v, wst_v
    sb_ref, ra_ref, rd_ref, cw_ref, cb_ref = sb_v, ra_v, rd_v, cw_v, cb_v
    sk_ref, og_ref, wo_ref = sk_v, og_v, wo_v
    inner = wo_ref.shape[0]
    D = tok_ref.shape[2]
    nj = inner // 128
    share, keep, G = split(nj, rows, n_col)
    n_grp = n_col // G
    hs = heads * state
    nh = 2 * heads
    r = lax.axis_index("row")
    c = lax.axis_index("col")
    g, q = c // G, c % G
    mine_j, mine_h = q // share, q % share
    i0 = mine_h * keep
    if nj == 4:
        far = [3 - mine_j, (mine_j + 2) % 4, mine_j + 1 - 2 * (mine_j % 2), mine_j]
    else:
        far = [(mine_j + k) % nj for k in range(1, nj)] + [mine_j]
    peers = [(j, h, j * share + h) for j in far[:-1] for h in range(share)]
    peers += [(mine_j, h, mine_j * share + h) for h in [(mine_h + k) % share for k in range(1, share)]]
    if len(peers) == 7:
        peers = [peers[k] for k in (0, 2, 1, 3, 4, 5, 6)]
    base = g * G

    barrier = pltpu.get_barrier_semaphore()

    plan = (
        (4, 1, 1, eb.at[1]),
        (5, 1, -1, eb.at[0]),
        (6, -1, 1, eb.at[1]),
        (7, -1, -1, eb.at[0]),
        (0, 0, 1, eb.at[1]),
        (1, 0, -1, eb.at[0]),
        (2, 1, 0, tok_ref.at[rows - 1]),
        (3, -1, 0, tok_ref.at[0]),
    )

    def there(dr, dc):
        return (r + dr >= 0) & (r + dr < n_row) & (c + dc >= 0) & (c + dc < n_col)

    loads[0].start()
    hb[...] = jnp.zeros_like(hb)
    friends = [(dr, dc, there(dr, dc)) for _, dr, dc, _ in plan]
    friends += [(dr, 0, there(dr, 0)) for k in range(2, n_row) for dr in (k, -k)]
    ahead = [(0, dc, q + dc < G) for dc in range(2, G)] + [(0, G * k, g + k < n_grp) for k in range(1, n_grp)]
    for dr, dc, ok in friends + ahead:
        @pl.when(ok)
        def _():
            pl.semaphore_signal(barrier, inc=1, device_id=(r + dr, c + dc), device_id_type=MESH)
    for load in loads[1:]:
        load.start()
    eb[...] = jnp.zeros_like(eb)
    lh[...] = jnp.zeros_like(lh)
    for i in (0, rows + 1):
        xp[i] = jnp.zeros(xp.shape[1:], F32)
    for i in range(rows):
        xp[i + 1, 0:8, :] = jnp.zeros((8, inner), F32)
        xp[i + 1, 8 + cols:16 + cols, :] = jnp.zeros((8, inner), F32)

    loads[0].wait()
    eb[0, 0:rows, :] = tok_ref[:, 0, :]
    eb[1, 0:rows, :] = tok_ref[:, cols - 1, :]
    pl.semaphore_wait(barrier, sum(jnp.where(ok, 1, 0) for _, _, ok in friends) + jnp.maximum(q - 1, 0) + g)

    for slot, dr, dc, src in plan:
        @pl.when(there(dr, dc))
        def _():
            copy_to(src, hb.at[slot], sent, h_recv.at[min(slot, 2) // 2], r + dr, c + dc).start()

    for dc in range(2, G):
        @pl.when(q >= dc)
        def _():
            pl.semaphore_signal(near.at[0], inc=1, device_id=(r, c - dc), device_id_type=MESH)
    for k in range(1, n_grp):
        @pl.when(g >= k)
        def _():
            pl.semaphore_signal(near.at[1], inc=1, device_id=(r, c - G * k), device_id_type=MESH)

    for k in (1, 4, 5, 6, 7):
        loads[k].wait()
    x = tok_ref[...].astype(F32).reshape(T, D)
    normed = norm(x, ng_ref[...]).astype(BF16)
    norm_s[...] = normed
    for k in (2, 3):
        loads[k].wait()
    main_x = mm(normed, wi_ref[:, :inner]).astype(BF16).astype(F32)
    for i in range(rows):
        xp[i + 1, 8:8 + cols, :] = main_x[i * cols:(i + 1) * cols]

    def column(row):
        width = row.shape[1]
        square = jnp.broadcast_to(row, (width, width))
        return jnp.sum(
            jnp.where(iota((width, width), 0) == iota((width, width), 1), square, 0.0), axis=1, keepdims=True
        )

    t_i, u_i = iota((T, T), 0), iota((T, T), 1)
    row_same = (t_i // cols) == (u_i // cols)
    col_same = (t_i % cols) == (u_i % cols)
    step_t = nt(wst_ref[...], normed)
    rate = jnp.concatenate([column(ra_ref[...]) / full_w, column(rd_ref[...]) / height], axis=0)
    logs_t = -softplus(step_t + column(sb_ref[...])) * rate

    def thirds(v):
        hi = v.astype(BF16)
        rest = v - hi.astype(F32)
        mid = rest.astype(BF16)
        return hi, mid, (rest - mid.astype(F32)).astype(BF16)

    up = t_i <= u_i
    sums = jnp.concatenate(
        [jnp.where(m, 1.0, 0.0).astype(BF16) for m in (row_same & up, row_same, col_same & up, col_same)], axis=1
    )
    parts = mm(jnp.concatenate(thirds(logs_t), axis=0), sums)
    summed = parts[:nh] + parts[nh:2 * nh] + parts[2 * nh:]
    cum_t = jnp.concatenate([summed[:heads, 0:T], summed[heads:, 2 * T:3 * T]], axis=0)
    tot_t = jnp.concatenate([summed[:heads, T:2 * T], summed[heads:, 3 * T:]], axis=0)
    logs_s[0:heads] = tot_t[heads:] - cum_t[heads:]
    logs_s[heads:] = tot_t[heads:]
    cum_ts[...] = cum_t
    cum = jnp.concatenate([cum_t, jnp.zeros((T - nh, T), F32)], axis=0).T[:, :nh]
    cum_s[...] = cum

    row_tot = jnp.concatenate([cum[(i + 1) * cols - 1:(i + 1) * cols] for i in range(rows)], axis=0)
    spread = jnp.where(iota((nh, inner), 0) == iota((nh, inner), 1) // (inner // heads), 1.0, 0.0).astype(BF16)
    wide = sum(mm(part, spread) for part in thirds(row_tot))
    for j in range(nj):
        dj[j] = wide[:, j * 128:(j + 1) * 128]

    def per_state(v):
        return jnp.concatenate([jnp.broadcast_to(v[k:k + 1], (state, T)) for k in range(heads)], axis=0)

    sel = mm(normed, wsel_ref[...])
    sel_s[...] = sel[:, :2 * hs]
    btail[...] = sel[:, :hs].T * per_state(jnp.exp(tot_t - cum_t))
    bd_s[...] = sel[:, 2 * hs:3 * hs].astype(BF16)
    cds[...] = sel[:, 3 * hs:].astype(BF16)

    def down_early(to_row, slot, dest):
        return (
            copy_to(bd_s, brecv.at[slot], sent, v_recv.at[1, slot], to_row, c),
            copy_to(logs_s, lrecv.at[slot], sent, v_recv.at[2, slot], to_row, c),
        )

    def down_values(to_row, slot, dest):
        return copy_to(vbf, vrecv.at[slot], sent, v_recv.at[0, slot], to_row, c)

    for k in range(1, n_row):
        @pl.when(r < k)
        def _():
            for cp in down_early(k, r, k):
                cp.start()

    for k in (8, 9, 10, 11, 12):
        loads[k].wait()
    for j in range(nj):
        ln = slice(j * 128, (j + 1) * 128)
        w9 = [cw_ref[a, b:b + 1, ln] for a in range(3) for b in range(3)]
        bias = cb_ref[:, ln]
        for i in range(rows):
            total = jnp.zeros((cols, 128), F32) + bias
            for a in range(3):
                if 0 <= i + a - 1 < rows:
                    for b in range(3):
                        total = total + xp[i + a, 7 + b:7 + b + cols, ln] * w9[a * 3 + b]
            pre[j, i * cols:(i + 1) * cols] = total
            vals[j, i * cols:(i + 1) * cols] = silu(total)

    @pl.when(q < G - 2)
    def _():
        pl.semaphore_wait(near.at[0], G - 2 - q)

    for j, h, p in peers:
        copy_to(dj.at[j], drecv.at[q], sent, d_recv, r, base + p).start()

    sides, rest = (
        sum(jnp.where(there(dr, dc), 1, 0) for slot, dr, dc, _ in plan if (slot >= 2) == other)
        for other in (False, True)
    )

    def halos(n, kind):
        some = hb.at[pl.ds(0, n)]
        return copy_to(some, some, sent, h_recv.at[kind], r, c)

    def halo_x(lo, hi):
        edge = norm(hb[lo:hi].astype(F32).reshape((hi - lo) * cols, D), ng_ref[...]).astype(BF16)
        return mm(edge, wi_ref[:, :inner]).astype(BF16).astype(F32)

    for n in (1, 2):
        @pl.when(sides == n)
        def _():
            halos(n, 0).wait_recv()
    side_x = halo_x(0, 2)
    lh[0, 8:8 + rows, :] = side_x[0:rows]
    lh[1, 8:8 + rows, :] = side_x[cols:cols + rows]

    def take_rest():
        for n in (2, 3, 4, 6):
            @pl.when(rest == n)
            def _():
                halos(n, 1).wait_recv()
        corner = [hb[4, rows - 1:rows, :], hb[5, rows - 1:rows, :], hb[6, 0:1, :], hb[7, 0:1, :]]
        corner = [v.astype(F32) for v in corner] + [jnp.zeros((12, D), F32)]
        edge = jnp.concatenate([hb[2].astype(F32), hb[3].astype(F32)] + corner, axis=0)
        edge_x = mm(norm(edge, ng_ref[...]).astype(BF16), wi_ref[:, :inner]).astype(BF16).astype(F32)
        xp[0, 8:8 + cols, :] = edge_x[0:cols]
        xp[rows + 1, 8:8 + cols, :] = edge_x[cols:2 * cols]
        xp[0, 7:8, :] = edge_x[2 * cols + 0:2 * cols + 1]
        xp[0, 8 + cols:9 + cols, :] = edge_x[2 * cols + 1:2 * cols + 2]
        xp[rows + 1, 7:8, :] = edge_x[2 * cols + 2:2 * cols + 3]
        xp[rows + 1, 8 + cols:9 + cols, :] = edge_x[2 * cols + 3:2 * cols + 4]

    first = iota((1, 128), 1) < 64
    pair = 2 * state
    for j in range(nj):
        ln = slice(j * 128, (j + 1) * 128)
        for e, at, b in ((0, 0, 0), (1, cols - 1, 2)):
            some = pl.ds(at, rows, stride=cols)
            total = pre[j, some, :]
            for a in range(3):
                total = total + lh[e, 7 + a:7 + a + rows, ln] * cw_ref[a, b:b + 1, ln]
            pre[j, some, :] = total
            vals[j, some, :] = silu(total)

    def states(half):
        row, a, edge_row = ((0, 0, 0), (rows - 1, 2, rows + 1))[half]
        lo = half * keep * cols
        at = slice(row * cols, (row + 1) * cols)
        part = slice(lo, lo + keep * cols)
        own = (iota((keep * pair, keep * cols), 0) // pair) == (iota((keep * pair, keep * cols), 1) // cols)
        for j in range(nj):
            ln = slice(j * 128, (j + 1) * 128)
            total = pre[j, at]
            for b in range(3):
                total = total + xp[edge_row, 7 + b:7 + b + cols, ln] * cw_ref[a, b:b + 1, ln]
            vals[j, at] = silu(total)
            vbf[j, part] = vals[j, part].astype(BF16)
            piece = jnp.concatenate([btail[j * pair:(j + 1) * pair, part]] * keep, axis=0)
            piece = jnp.where(own, piece, 0.0).astype(BF16)
            res = mm(piece, vbf[j, part])
            for i in range(keep):
                top = res[i * pair:i * pair + state]
                bottom = res[i * pair + state:(i + 1) * pair]
                fbuf[j * share + half, i] = jnp.where(first, top, bottom).astype(BF16)

        def send(p):
            copy_to(fbuf.at[p], frecv.at[q], sent, f_recv, r, base + p).start()

        for j in far[:-1]:
            send(j * share + half)

        @pl.when(mine_h != half)
        def _():
            send(mine_j * share + half)

    @pl.when(r == 0)
    def _():
        states(0)
        take_rest()
        states(1)

    @pl.when((r > 0) & (r == n_row - 1))
    def _():
        states(1)
        take_rest()
        states(0)

    if n_row > 2:
        @pl.when((r > 0) & (r < n_row - 1))
        def _():
            take_rest()
            states(0)
            states(1)

    for k in range(1, n_row):
        @pl.when(r < k)
        def _():
            down_values(k, r, k).start()

    @pl.when(c == 0)
    def _():
        copy_to(fbuf, precv, sent, s_recv, r, c + 1).start()
        precv[...] = jnp.zeros_like(precv)

    frecv[q] = fbuf[q]
    drecv[q] = dj[mine_j]

    low = u_i <= t_i
    mask_a, mask_d = row_same & low, col_same & low
    lane_head = iota((T, hs), 1) // state
    zero_b = jnp.zeros((T, hs), BF16)
    b_a, c_a = sel_s[:, 0:hs], sel_s[:, hs:]
    cexp[...] = (c_a * per_state(jnp.exp(cum_ts[...])).T).astype(BF16)
    b_ab, c_ab, b_db, c_db = b_a.astype(BF16), c_a.astype(BF16), bd_s[...], cds[...]
    for k in range(heads):
        only = lane_head == k
        s_a = nt(c_ab, jnp.where(only, b_ab, zero_b))
        s_d = nt(c_db, jnp.where(only, b_db, zero_b))
        g_a = jnp.where(mask_a, cum_s[:, k:k + 1] - cum_ts[k:k + 1, :], -1e30)
        g_d = jnp.where(mask_d, cum_s[:, heads + k:heads + k + 1] - cum_ts[heads + k:heads + k + 1, :], -1e30)
        sc[k // 2, :, (k % 2) * T:(k % 2 + 1) * T] = (s_a * jnp.exp(g_a) + s_d * jnp.exp(g_d)).astype(BF16)

    def times_values(scores, v_tile):
        zero = jnp.zeros((T, 128), BF16)
        stacked = jnp.concatenate(
            [jnp.where(first, v_tile, zero), jnp.where(first, zero, v_tile)], axis=0
        )
        return mm(scores, stacked)

    others = pl.ds(0, G - 1)

    def whole(ref, send, recv):
        return copy_to(ref.at[others], ref.at[others], send, recv, r, c)

    whole(drecv, sent, d_recv).wait_recv()
    logs = [drecv[e, pl.ds(i0, keep), :] for e in range(G)]
    tdec[...] = sum(logs)
    decays = [jnp.exp(v)[:, None, :] for v in logs]

    def total_decay(k):
        return copy_to(tdec, tdrecv.at[g], sent, t_recv.at[0, g], r, c + G * k)

    def total_state(k):
        return copy_to(tbuf, trecv.at[g], sent, t_recv.at[1, g], r, c + G * k)

    def later(k):
        return g + k < n_grp

    whole(frecv, sent, f_recv).wait_recv()
    @pl.when(g < n_grp - 1)
    def _():
        pl.semaphore_wait(near.at[1], n_grp - 1 - g)

    carry = frecv[0].astype(F32)
    for e in range(1, G):
        carry = decays[e] * carry + frecv[e].astype(F32)
    tbuf[...] = carry.astype(BF16)
    for k in range(1, n_grp):
        @pl.when(later(k))
        def _():
            total_state(k).start()

        @pl.when(later(k) & (g > 0))
        def _():
            total_decay(k).start()

    gate[...] = silu(mm(norm_s[...], wi_ref[:, inner:]).astype(BF16).astype(F32))
    for j in range(nj):
        ln = slice(j * 128, (j + 1) * 128)
        acc[:, ln] = times_values(sc[j], vbf[j]) + sk_ref[:, ln] * vals[j]

    mine = (iota((T, rows * pair), 0) // cols) == (iota((T, rows * pair), 1) // pair)
    for j in range(nj):
        src = iota((hs, rows * pair), 0)
        dst = iota((hs, rows * pair), 1) % pair
        rep = (src == dst + j * pair).astype(BF16)
        maps[j] = jnp.where(mine, mm(cexp[...], rep), 0.0).astype(BF16)

    ibuf[...] = jnp.zeros_like(ibuf)
    for m in range(n_grp - 1):
        @pl.when(m < g)
        def _():
            if m:
                copy_to(tdec, tdrecv.at[m], sent, t_recv.at[0, m], r, c).wait_recv()
            copy_to(tbuf, trecv.at[m], sent, t_recv.at[1, m], r, c).wait_recv()
            if m:
                ibuf[...] = jnp.exp(tdrecv[m])[:, None, :] * ibuf[...] + trecv[m].astype(F32)
            else:
                ibuf[...] = trecv[m].astype(F32)
    carry = ibuf[...]
    for e in range(G):
        pbuf[e] = carry.astype(BF16)
        if e < G - 1:
            carry = decays[e] * carry + frecv[e].astype(F32)
    for j, h, p in peers:
        @pl.when(base + p > 1)
        def _():
            copy_to(pbuf.at[p], precv.at[q], sent, p_recv, r, base + p).start()

    @pl.when(c > 1)
    def _():
        precv[q] = pbuf[q]

    for back in range(1, n_row):
        @pl.when(r >= back)
        def _():
            slot = r - back
            for cp in down_early(r, slot, 1):
                cp.wait_recv()
            down_values(r, slot, 1).wait_recv()
            gap = lrecv[slot, 0:heads]
            for nearer in range(1, back):
                gap = gap + lrecv[r - nearer, heads:]
            same = (iota((T, T), 0) % cols) == (iota((T, T), 1) % cols)
            for j in range(nj):
                parts = []
                for k in (2 * j, 2 * j + 1):
                    only = (iota((T, hs), 1) // state) == k
                    s_d = nt(cds[...], jnp.where(only, brecv[slot], jnp.zeros((T, hs), BF16)))
                    g_d = jnp.where(same, cum_s[:, heads + k:heads + k + 1] + gap[k:k + 1, :], -1e30)
                    parts.append((s_d * jnp.exp(g_d)).astype(BF16))
                ln = slice(j * 128, (j + 1) * 128)
                acc[:, ln] += times_values(jnp.concatenate(parts, axis=1), vrecv[slot, j])

    for n in (3, 5, 8):
        @pl.when(sides + rest == n)
        def _():
            halos(n, 0).wait_send()
    whole(drecv, sent, d_recv).wait_send()
    whole(frecv, sent, f_recv).wait_send()
    @pl.when(c == 0)
    def _():
        copy_to(fbuf, precv, sent, s_recv, r, c).wait_send()
    for k in range(1, n_grp):
        @pl.when(later(k))
        def _():
            total_state(k).wait_send()

        @pl.when(later(k) & (g > 0))
        def _():
            total_decay(k).wait_send()
    for k in range(1, n_row):
        @pl.when(r < k)
        def _():
            for cp in down_early(r, 0, k):
                cp.wait_send()
            down_values(r, 0, k).wait_send()

    @pl.when(c == 1)
    def _():
        copy_to(fbuf, precv, sent, s_recv, r, c).wait_recv()

    tiles = []
    zero_s = jnp.zeros((state, 128), BF16)
    @pl.when(c > 1)
    def _():
        whole(precv, sent, p_recv).wait_recv()

    for j in range(nj):
        ln = slice(j * 128, (j + 1) * 128)
        blocks = []
        for i in range(rows):
            s = precv[j * share + i // keep, i % keep]
            blocks += [jnp.where(first, s, zero_s), jnp.where(first, zero_s, s)]
        tiles.append((acc[:, ln] + mm(maps[j], jnp.concatenate(blocks, axis=0))) * gate[:, ln])

    mixed = jnp.concatenate(tiles, axis=1)
    gated = norm(mixed, og_ref[...]).astype(BF16)
    result = mm(gated, wo_ref[...]) + tok_ref[...].astype(F32).reshape(T, D)
    out_ref[...] = result.astype(BF16).reshape(rows, cols, D)

    skipped = jnp.where(g > 0, 0, jnp.where(c > 1, 2, 1))
    for n in range(3):
        @pl.when(skipped == n)
        def _():
            some = pbuf.at[pl.ds(0, G - 1 - n)]
            copy_to(some, some, sent, p_recv, r, c).wait_send()


def solution(mesh):
    n_row, n_col = mesh.shape["row"], mesh.shape["col"]

    def on_device(
        tokens, norm_gain, w_inner, w_select, w_step, step_bias, rate_across, rate_down,
        conv_weight, conv_bias, skip_gain, out_gain, w_out,
    ):
        rows, cols, D = tokens.shape
        heads = rate_across.shape[0]
        inner = w_out.shape[0]
        hs = w_select.shape[1] // 4
        state = hs // heads
        T = rows * cols
        nj = inner // 128
        share, keep, G = split(nj, rows, n_col)
        n_grp = n_col // G
        dims = (n_row, n_col, rows, cols, heads, state, float(cols * n_col), float(rows * n_row))
        vm = pltpu.VMEM
        dma = pltpu.SemaphoreType.DMA
        operands = (
            tokens, norm_gain[None], w_inner, w_select, w_step.T, step_bias[None], rate_across[None],
            rate_down[None], conv_weight, conv_bias[None], skip_gain[None], out_gain[None], w_out,
        )
        operands = tuple(pltpu.with_memory_space_constraint(o, pltpu.HBM) for o in operands)
        return pl.pallas_call(
            functools.partial(kernel, dims),
            out_shape=jax.ShapeDtypeStruct(tokens.shape, tokens.dtype),
            in_specs=[pl.BlockSpec(memory_space=pltpu.HBM)] * 13,
            out_specs=pl.BlockSpec(memory_space=pltpu.VMEM),
            scratch_shapes=[vm(o.shape, o.dtype) for o in operands] + [dma((4,))] + [
                vm((8, cols, D), BF16), vm((2, cols, D), BF16),
                vm((rows + 2, cols + 16, inner), F32),
                vm((nj + 1, T, 128), F32), vm((nj, T, 128), BF16), vm((T, hs), BF16),
                vm((2 * heads, T), F32), vm((nj, rows, 128), F32),
                vm((G, keep, state, 128), BF16), vm((G + 1, rows, 128), F32), vm((G, keep, state, 128), BF16),
                vm((keep, state, 128), BF16), vm((keep, 128), F32),
                vm((n_grp, keep, state, 128), BF16), vm((n_grp, keep, 128), F32), vm((keep, state, 128), F32),
                vm((G, keep, state, 128), BF16), vm((G, keep, state, 128), BF16),
                vm((n_row, nj, T, 128), BF16), vm((n_row, T, hs), BF16), vm((n_row, 2 * heads, T), F32),
                vm((heads // 2, T, 2 * T), BF16), vm((T, inner), F32), vm((T, inner), F32),
                vm((T, hs), BF16), vm((T, hs), BF16), vm((T, 2 * heads), F32), vm((2 * heads, T), F32),
                vm((hs, T), F32), vm((T, 2 * hs), F32), vm((nj, T, rows * 2 * state), BF16),
                vm((nj + 1, T, 128), F32), vm((2, rows + 16, inner), F32), vm((T, D), BF16),
                dma, dma((2,)), dma, dma, dma((2, max(n_grp - 1, 1))), dma, dma((3, n_row - 1)), dma, pltpu.SemaphoreType.REGULAR((2,)),
            ],
            compiler_params=pltpu.CompilerParams(
                collective_id=0, has_side_effects=True, vmem_limit_bytes=48 << 20
            ),
            name="block",
        )(*operands)

    placed = (P("row", "col", None),) + (P(),) * 12
    return jax.shard_map(
        on_device, mesh=mesh, in_specs=placed, out_specs=P("row", "col", None), check_vma=False
    )
```
